256 devices in a mesh: dp: 16 (over y, x), expert: 16 (over z, core).
Axes of the slice: x: 4, y: 4, z: 8, core: 2. Of those that a mesh axis runs over, the one named last changes fastest.
Arguments:
- tokens: bfloat16 [256, 6144], P('dp'), may hold values from -6 to 6
- w_gate: bfloat16 [6144, 32768], P(None, ('expert', 'dp')), may hold values from -0.078125 to 0.078125
- w_up: bfloat16 [6144, 32768], P(None, ('expert', 'dp')), may hold values from -0.078125 to 0.078125
- basis: bfloat16 [2, 32768, 6144], P(None, ('expert', 'dp')), may hold values from -5 to 5
- routes: int32 [256, 2], replicated, may hold values from 0 to 3, all different within a row; in each aligned block of 16 rows (0 to 15, 16 to 31, ...) at most 9 rows name the same one
- gates: float32 [256, 2], replicated, may hold values from 0.1 to 0.9
- rho: float32 [256], P('dp'), may hold values from 0.3 to 3
- sigma: float32 [6144], replicated, may hold values from 0.3 to 3
Outputs:
- krylov_next: bfloat16 [32768, 6144], P(('expert', 'dp'))
- hessenberg: float32 [3, 1], replicated
The draws below stay inside these ranges and needn't reach their ends.
Inputs may be any that keep to these rules, and one draw needn't show every extreme that they name: `routes`: in each aligned block of 16 rows (the rows of one index of dp), no expert is named by more than 9 rows; the 2 entries of a row differ.
All inputs are finite; a program needn't handle non-finite values.
Results may differ from the reference program's by a relative error of at most 0.0062.
The reference program's roundings to bfloat16 on the way (of `picked`, `hidden` and `cotangent`) count: a program that leaves them out, or rounds other values in their place, can miss the bound.
Values may be sent and summed in bfloat16 or wider, within the bound.
A program may use at most 64 MiB of HBM per device.

```python
import math
import jax
import jax.numpy as jnp
import numpy as np
from jax import lax

D = 6144
FF = 8192
E = 4
TOP = 2
BASIS = 2
STEPS = 1
TOK_DEV = 16
CAP = 9
TOKENS = 256
N_DP = 16


def draw_basis(key, part):
    common_key = jax.random.fold_in(key, 11)
    own_key = jax.random.fold_in(key, 12)
    common = jax.random.normal(common_key, (1, E * FF, D), jnp.float32)
    own = jax.random.normal(own_key, (BASIS, E * FF, D), jnp.float32)
    return jnp.clip((0.8 * common + own) * 0.78, -5.0, 5.0).astype(jnp.bfloat16)


def block_levels(rng, shape, shards, smallest, largest):
    def one(dim, blocks):
        heights = jax.random.uniform(jax.random.fold_in(jax.random.fold_in(rng, 6), dim), (blocks,), jnp.float32, smallest / len(shards), largest / len(shards))
        return jnp.repeat(jnp.exp(heights), shape[dim] // blocks).reshape((-1,) + (1,) * (len(shape) - dim - 1))

    loudness = one(*shards[0])
    for cut in shards[1:]:
        loudness = loudness * one(*cut)
    return loudness


def shared_out(key, own, number, rows, amount, top, reach, slope):
    order = jax.random.permutation(key, amount)
    heavy_load, usual = load_shares(amount, rows * top, reach, slope, True), load_shares(amount, rows * top, reach, slope, False)
    places = jnp.arange(amount)

    def named(sizes, rotation):
        used = int((sizes > 0).sum())
        fixed = max(1, used // 4)
        moved = fixed + (places - fixed + rotation * (used - fixed)) % max(1, amount - fixed)
        return jnp.zeros((amount,), jnp.int32).at[order[jnp.where(places < fixed, places, moved)]].set(jnp.asarray(sizes, jnp.int32))

    sizes = jnp.where(number % 4 == 0, named(heavy_load, number // 4), named(usual, number - number // 4 - 1))
    mixed = jax.random.permutation(jax.random.fold_in(own, 3), amount)
    giver, sink = mixed[0:amount // 2 * 2:2], mixed[1:amount // 2 * 2:2]
    slack = jnp.minimum(sizes[giver] - 1, reach - sizes[sink]) // 2
    slack = jnp.where((giver == order[0]) | (sink == order[0]) | (sizes[sink] == 0), 0, jnp.maximum(slack, 0))
    moved = jax.random.randint(jax.random.fold_in(own, 4), (amount // 2,), 0, 1 << 20) % (slack + 1)
    sizes = sizes.at[giver].add(-moved).at[sink].add(moved)
    items = jnp.searchsorted(jnp.cumsum(sizes), jnp.arange(rows * top), side="right").astype(jnp.int32)
    grid = items.reshape(top, rows).T
    grid = grid[jax.random.permutation(jax.random.fold_in(own, 1), rows)]
    rotation = jax.random.randint(jax.random.fold_in(own, 2), (rows, 1), 0, top)
    return jnp.take_along_axis(grid, (jnp.arange(top)[None, :] + rotation) % top, axis=1)


def load_shares(count, total, bound, lean, full):
    loads = [(1 << 20) // math.isqrt(rank ** lean) + 1 for rank in range(1, count + 1)]
    largest = bound if full else min(bound, max(-(-total // count), total * loads[0] // sum(loads)))
    least = 1 if total - largest >= count - 1 else 0
    counts, surplus = [largest] + [least] * (count - 1), total - largest - least * (count - 1)
    while surplus > 0:
        candidates = [i for i in range(1, count) if counts[i] < largest] or [i for i in range(1, count) if counts[i] < bound]
        whole, budget = sum([loads[i] for i in candidates]), surplus
        for i in candidates:
            extra = min(bound - counts[i], max(1, budget * loads[i] // whole), surplus)
            counts[i] = counts[i] + extra
            surplus = surplus - extra
    return np.array(counts)


def gaussian(key, extent, deviation, reach, split=(), held_as=jnp.bfloat16):
    result = deviation * jax.random.normal(key, extent, jnp.float32)
    if split:
        result = result * block_levels(key, extent, split, -0.22, 0.18)
    return jnp.clip(result, -reach, reach).astype(held_as)


def setup_inputs(seed: int = 0) -> dict:
    arg_keys = jax.random.split(jax.random.key(seed), 9)
    tokens = gaussian(arg_keys[0], (TOKENS, D), 1.0, 6.0, ((0, 16),))
    w_gate = gaussian(arg_keys[1], (D, E * FF), D ** -0.5, 0.078125, ((1, 256),))
    w_up = gaussian(arg_keys[2], (D, E * FF), D ** -0.5, 0.078125, ((1, 256),))
    basis = draw_basis(jax.random.fold_in(arg_keys[8], 71), 0)
    routes_keys = jax.random.split(jax.random.fold_in(arg_keys[4], 1), TOKENS // TOK_DEV)
    routes_turns = jax.random.permutation(jax.random.fold_in(arg_keys[4], 3), TOKENS // TOK_DEV)
    routes = jax.vmap(lambda own, number: shared_out(jax.random.fold_in(arg_keys[4], 2), own, number, TOK_DEV, E, TOP, CAP, 1))(routes_keys, routes_turns).reshape((TOKENS, TOP))
    gates = jnp.clip(jax.random.uniform(arg_keys[5], (TOKENS, TOP), jnp.float32, 0.1, 0.9), 0.1, 0.9)
    rho = jnp.clip(jnp.exp(math.log(3.0) - 2.3025851 * jax.random.uniform(arg_keys[6], (TOKENS,), jnp.float32) ** block_levels(arg_keys[6], (TOKENS,), ((0, 16),), -0.2, 0.2)), 0.3, 3.0)
    sigma = jnp.clip(jnp.exp(jax.random.uniform(arg_keys[7], (D,), jnp.float32, math.log(0.3), math.log(3.0))), 0.3, 3.0)
    return dict(tokens=tokens, w_gate=w_gate, w_up=w_up, basis=basis, routes=routes, gates=gates, rho=rho, sigma=sigma)


def slot_tables(routes, gates, expert_id, sources, tok_dev, capacity):
    matches = (routes == expert_id).reshape(sources, tok_dev, routes.shape[1])
    member = lax.optimization_barrier(jnp.sum(matches.astype(jnp.int32), axis=2))
    gate_tok = lax.optimization_barrier(jnp.sum(jnp.where(matches, gates.reshape(sources, tok_dev, routes.shape[1]), 0.0), axis=2))
    slot_rank = jnp.cumsum(member, axis=1) - 1
    slot_index = lax.broadcasted_iota(jnp.int32, (sources, capacity, tok_dev), 1)
    placing = jnp.where((slot_rank[:, None, :] == slot_index) & (member[:, None, :] > 0), 1.0, 0.0).astype(jnp.float32)
    slot_gate = lax.optimization_barrier(jnp.sum(placing * gate_tok[:, None, :], axis=2))
    return (placing, slot_gate)

def reference(tokens, w_gate, w_up, basis, routes, gates, rho, sigma):
    scale_back = 1.0 / math.sqrt(FF)
    kappa = E * FF / TOKENS
    entries = float(E * FF * D)
    eye_block = jnp.eye(N_DP, dtype=jnp.float32)
    tables = []
    for expert in range(E):
        placing, slot_gate = slot_tables(routes, gates, expert, N_DP, TOK_DEV, CAP)
        full = (placing[:, :, None, :] * eye_block[:, None, :, None]).reshape(N_DP * CAP, TOKENS)
        picked = jnp.dot(full.astype(jnp.bfloat16), tokens, preferred_element_type=jnp.float32).astype(jnp.bfloat16)
        gate_part = jnp.dot(picked, w_gate[:, expert * FF:(expert + 1) * FF], preferred_element_type=jnp.float32)
        up_part = jnp.dot(picked, w_up[:, expert * FF:(expert + 1) * FF], preferred_element_type=jnp.float32)
        hidden = (jax.nn.silu(gate_part) * up_part * slot_gate.reshape(-1)[:, None]).astype(jnp.bfloat16)
        tables.append((full, hidden))

    def gn_product(direction):
        response = jnp.zeros((TOKENS, D), jnp.float32)
        for expert in range(E):
            full, hidden = tables[expert]
            part = jnp.dot(hidden, direction[expert * FF:(expert + 1) * FF], preferred_element_type=jnp.float32) * scale_back
            response = response + jnp.dot(full.T, part, precision=lax.Precision.HIGHEST)
        cotangent = (kappa * rho[:, None] * sigma[None, :] * response).astype(jnp.bfloat16)
        blocks = []
        for expert in range(E):
            full, hidden = tables[expert]
            chosen = jnp.dot(full.astype(jnp.bfloat16), cotangent, preferred_element_type=jnp.float32).astype(jnp.bfloat16)
            blocks.append(jnp.dot(hidden.T, chosen, preferred_element_type=jnp.float32) * scale_back)
        return jnp.concatenate(blocks, axis=0)
    vectors = [basis[index] for index in range(BASIS)]
    current = basis[BASIS - 1]
    columns = []
    for step in range(STEPS):
        image = gn_product(current)
        coeffs = jnp.stack([jnp.sum(vector.astype(jnp.float32) * image) for vector in vectors]) / entries
        resid = image
        for index in range(len(vectors)):
            resid = resid - coeffs[index] * vectors[index].astype(jnp.float32)
        beta = jnp.sqrt(jnp.sum(resid * resid) / entries)
        current = (resid / beta).astype(jnp.bfloat16)
        padding = jnp.zeros((STEPS - 1 - step,), jnp.float32)
        columns.append(jnp.concatenate([coeffs, padding, beta[None]]))
        vectors.append(current)
    return (current, jnp.stack(columns, axis=1))
```

```python
import functools
import math

import jax
import jax.numpy as jnp
from jax import lax
from jax.experimental import pallas as pl
from jax.experimental.pallas import tpu as pltpu
from jax.sharding import Mesh
from jax.sharding import PartitionSpec as P

D = 6144
FF = 8192
E = 4
HALF = 3072
GROUP = 768
SIDE = 128
MSG = HALF + SIDE + 512
ROWS = 144
CHUNK = 216
DP = ("dp_0", "dp_1")
EXPERT = ("expert_0", "expert_1")
EXPERT_DP = ("expert_0", "expert_1", "dp_0", "dp_1")
AXES = ("dp_0", "dp_1", "expert_0", "expert_1")
MESH = pl.DeviceIdType.MESH
F32 = jnp.float32
BF16 = jnp.bfloat16
SCALE = 1.0 / math.sqrt(FF)
KAPPA = E * FF / 256
ENTRIES = float(E * FF * D)
OFFSETS = (1, 3, 2)


def iota(shape, dim):
    return lax.broadcasted_iota(jnp.int32, shape, dim)


def parts(col):
    hi = col.astype(BF16)
    left = col - hi.astype(F32)
    mid = left.astype(BF16)
    low = (left - mid.astype(F32)).astype(BF16)
    return hi.astype(F32), mid.astype(F32), low.astype(F32)


def joined(side, first):
    return (side[:, first : first + 1] + side[:, first + 1 : first + 2]) + side[:, first + 2 : first + 3]


def slot_order(m):
    return jnp.concatenate([m[0:64], m[128:136], m[64:128], m[136:144]], axis=0)


def kernel(
    tok_hbm, wg_hbm, wu_hbm, basis_hbm, routes, gates, rho, sigma,
    out_hbm, hess,
    tokv, wbuf, v0, v1, v0x, v1x, gm, gd, exf, exs, side_main, pre_s, pre_r, hid, hid_t,
    tb, r1, town, p2s, r2, zs, rz0, zes, rz, amat, amat_h, rank_s, rho_s, c4, cx, cg, img,
    out_v, red_a, red_b, red_s,
    loc_sem, core_send, core_recv, ag_send, ag_recv, rs_send, rs_recv, z_send, z_recv,
    cg_send, cg_recv, cx_send, cx_recv, ra_send, ra_recv, rb_send, rb_recv,
):
    y, x, z, c = [lax.axis_index(name) for name in AXES]
    a1 = y * (1 - c) + x * c
    a2 = x * (1 - c) + y * c
    p = y * 4 + x
    q = z * 2 + c
    e = z // 2

    def plane(b1, b2):
        return (b1 * (1 - c) + b2 * c, b2 * (1 - c) + b1 * c, z, c)

    def send(src, dst, s_sem, r_sem, device):
        copy = pltpu.make_async_remote_copy(
            src_ref=src, dst_ref=dst, send_sem=s_sem, recv_sem=r_sem, device_id=device, device_id_type=MESH
        )
        copy.start()
        return copy

    def local(src, dst, sem):
        copy = pltpu.make_async_copy(src, dst, sem)
        copy.start()
        return copy

    barrier = pltpu.get_barrier_semaphore()
    for k in range(1, 16):
        o = (p + k) % 16
        pl.semaphore_signal(barrier, inc=1, device_id=(o // 4, o % 4, z, c), device_id_type=MESH)
        o = (q + k) % 16
        pl.semaphore_signal(barrier, inc=1, device_id=(y, x, o // 2, o % 2), device_id_type=MESH)

    mine = pl.ds(pl.multiple_of(c * HALF, HALF), HALF)
    other = pl.ds(pl.multiple_of((1 - c) * HALF, HALF), HALF)
    loads = [
        local(tok_hbm.at[:, mine], tokv, loc_sem.at[0]),
        local(wg_hbm.at[mine, :], wbuf.at[0, :, pl.ds(0, 128)], loc_sem.at[1]),
        local(wu_hbm.at[mine, :], wbuf.at[0, :, pl.ds(128, 128)], loc_sem.at[2]),
        local(basis_hbm.at[1, :, mine], v1.at[0], loc_sem.at[3]),
        local(basis_hbm.at[0, :, mine], v0.at[0], loc_sem.at[4]),
        local(basis_hbm.at[1, :, other], v1x, loc_sem.at[5]),
        local(basis_hbm.at[0, :, other], v0x, loc_sem.at[6]),
    ]

    own_routes = routes[pl.ds(pl.multiple_of(p * 16, 16), 16), :]
    own_gates = gates[pl.ds(pl.multiple_of(p * 16, 16), 16), :]
    hit0 = own_routes[:, 0:1] == e
    hit1 = own_routes[:, 1:2] == e
    member = hit0.astype(F32) + hit1.astype(F32)
    gate_tok = jnp.where(hit0, own_gates[:, 0:1], 0.0) + jnp.where(hit1, own_gates[:, 1:2], 0.0)
    tri = (iota((16, 16), 1) <= iota((16, 16), 0)).astype(F32).astype(BF16)
    member_b = jnp.broadcast_to(member, (16, 128))
    rank = jnp.dot(tri, member_b.astype(BF16), preferred_element_type=F32)
    lane = iota((16, 128), 1)
    place_t = jnp.where((rank - 1.0 == lane.astype(F32)) & (member_b > 0), 1.0, 0.0)
    place = jnp.transpose(place_t)[0:16, :].astype(BF16)
    r_hi, r_mid, r_low = parts(rho[...])
    g_hi, g_mid, g_low = parts(gate_tok)
    side_in = jnp.zeros((16, 128), F32)
    for index, col in enumerate((r_hi, r_mid, r_low, g_hi, g_mid, g_low)):
        side_in = jnp.where(lane == index, col, side_in)
    side = jnp.dot(place, side_in.astype(BF16), preferred_element_type=F32)
    m = a1 * 4 + a2
    gm[m, :, HALF : HALF + SIDE] = side[0:8].astype(BF16)
    gm[m, :, HALF + SIDE + 384 : MSG] = jnp.broadcast_to(side[8:9], (8, 128)).astype(BF16)
    loads[0].wait()
    picked = jnp.dot(place, tokv[...], preferred_element_type=F32)
    gm[m, :, 0:HALF] = picked[0:8].astype(BF16)
    for r in range(8):
        exs[r : r + 1, :] = picked[8:9, r * 384 : (r + 1) * 384]
    gm[m, :, HALF + SIDE : HALF + SIDE + 384] = exs[...].astype(BF16)

    pl.semaphore_wait(barrier, 30)

    first = [
        send(gm.at[m], gm.at[m], ag_send.at[d - 1], ag_recv.at[d - 1], plane(a1, (a2 + d) % 4)) for d in OFFSETS
    ]
    partner = (y, x, z, 1 - c)
    core = [
        send(wg_hbm.at[other, :], wbuf.at[1, :, pl.ds(0, 128)], core_send.at[0], core_recv.at[0], partner),
        send(wu_hbm.at[other, :], wbuf.at[1, :, pl.ds(128, 128)], core_send.at[1], core_recv.at[1], partner),
        send(basis_hbm.at[1, :, other], v1.at[1], core_send.at[2], core_recv.at[2], partner),
        send(basis_hbm.at[0, :, other], v0.at[1], core_send.at[3], core_recv.at[3], partner),
    ]

    sg = 2 * (z % 2) - 1
    t_lane = iota((256, 128), 1)
    shift = jnp.where(t_lane == 1, sg, 0) + jnp.where(t_lane == 2, -sg, 0) + jnp.where(t_lane == 3, 2, 0)
    names = jnp.where(t_lane < 4, (e + shift + 4) & 3, -1)
    member4 = ((routes[:, 0:1] == names) | (routes[:, 1:2] == names)).astype(F32)
    low = iota((256, 256), 0)
    col = iota((256, 256), 1)
    tri_b = ((col <= low) & ((col >> 4) == (low >> 4))).astype(F32).astype(BF16)
    rank4 = jnp.dot(tri_b, member4.astype(BF16), preferred_element_type=F32)
    token = iota((256, 128), 0)
    block = token >> 4
    slot = rank4.astype(jnp.int32) - 1
    where_to = (block >> 3) * 72 + jnp.where(slot < 8, (block & 7) * 8 + slot, 64 + (block & 7))
    where_to = jnp.where(member4 > 0, where_to, -1000)
    onehot = (where_to[:, 0:1] == col).astype(F32)
    rank_s[...] = jnp.transpose(onehot)
    h = a2 % 2
    half_rows = pl.ds(pl.multiple_of(h * 72, 8), 72)
    own_full = rank_s[0:ROWS, :].astype(BF16)
    own_half = rank_s[half_rows, :].astype(BF16)
    for k in range(3):
        theirs = (where_to[:, k + 1 : k + 2] == col).astype(F32).astype(BF16)
        amat[k] = jnp.dot(own_full, theirs, preferred_element_type=F32)[:, 0:ROWS].astype(BF16)
        theirs = (where_to[:, k + 1 : k + 2] - h * 72 == col).astype(F32).astype(BF16)
        amat_h[k] = jnp.dot(own_half, theirs, preferred_element_type=F32)[:, 0:72].astype(BF16)

    for copy in first:
        copy.wait_recv()
    mine4 = pl.ds(pl.multiple_of(a1 * 4, 4), 4)
    second = [
        send(gm.at[mine4], gm.at[mine4], ag_send.at[2 + d], ag_recv.at[2 + d], plane((a1 + d) % 4, a2))
        for d in OFFSETS
    ]

    for copy in loads[1:]:
        copy.wait()
    for copy in core[2:]:
        copy.wait_recv()

    def gram(k, sums):
        s00, s01, s11 = sums
        part = pl.ds(pl.multiple_of(k * 256, 256), 256)
        for u in range(2):
            b0 = v0[u, :, part].astype(F32)
            b1 = v1[u, :, part].astype(F32)
            fold = lambda a: jnp.sum(a.reshape(16, 8, 256), axis=0)
            s00 = s00 + fold(b0 * b0)
            s01 = s01 + fold(b0 * b1)
            s11 = s11 + fold(b1 * b1)
        return s00, s01, s11

    zero = jnp.zeros((8, 256), F32)
    s00, s01, s11 = lax.fori_loop(0, HALF // 256, gram, (zero, zero, zero))

    for copy in second:
        copy.wait_recv()
    for copy in core[:2]:
        copy.wait_recv()

    def source(o):
        return o * (1 - c) + ((o % 4) * 4 + o // 4) * c

    for k in range(8):
        pair = [gm[source(2 * k + u), :, 0:HALF].astype(F32) for u in range(2)]
        gd[16 * k : 16 * k + 16, :] = jnp.concatenate(pair, axis=0).astype(BF16)
    for o in range(16):
        block_o = gm[source(o)][:, HALF:MSG].astype(F32)
        side_main[8 * o : 8 * o + 8, :] = block_o[:, 0:SIDE]
        for t in range(4):
            exf[t, 8 * o : 8 * o + 8, :] = block_o[:, SIDE + t * 128 : SIDE + (t + 1) * 128]
    for r in range(8):
        for t in range(3):
            f = r * 384 + t * 128
            gd[128:144, f : f + 128] = exf[t, pl.ds(r, 16, stride=8), :].astype(BF16)
    side_main[128:144, :] = exf[3, pl.ds(0, 16, stride=8), :]

    for u in range(2):
        pre_s[u] = jnp.dot(gd[...], wbuf[u], preferred_element_type=F32)
    pre_copy = send(pre_s, pre_r, core_send.at[4], core_recv.at[4], partner)
    side_all = side_main[...]
    rho_slot = slot_order(jnp.broadcast_to(joined(side_all, 0), (ROWS, 128)))
    rho_s[...] = KAPPA * rho_slot
    gate_slot = slot_order(jnp.broadcast_to(joined(side_all, 3), (ROWS, 128)))
    pre_copy.wait_recv()
    hidden = []
    for u in range(2):
        both = slot_order(pre_s[u] + pre_r[1 - u])
        gate, up = both[:, 0:128], both[:, 128:256]
        hidden.append(gate / (1.0 + jnp.exp(-gate)) * up * gate_slot)
    hidden = jnp.concatenate(hidden, axis=1)
    hid[...] = hidden.astype(BF16)

    rs1 = []
    for d in OFFSETS + (0,):
        g = (a1 + d) % 4
        part = pl.ds(pl.multiple_of(g * GROUP, GROUP), GROUP)
        rows = v1[:, :, part].reshape(256, GROUP)
        tangent = jnp.dot(hid[...], rows, preferred_element_type=F32)
        for i in range(4):
            t = 4 + i // 2
            full = tangent[:, i * 128 : (i + 1) * 128]
            half = tangent[(i % 2) * 72 : (i % 2) * 72 + 72, t * 128 : (t + 1) * 128]
            if d:
                tb[d - 1, i, 0:ROWS] = full.astype(BF16)
                tb[d - 1, i, ROWS:CHUNK] = half.astype(BF16)
            else:
                town[i, 0:ROWS] = full
                town[i, ROWS:CHUNK] = half
        if d:
            rs1.append(send(tb.at[d - 1], r1.at[d - 1], rs_send.at[d - 1], rs_recv.at[d - 1], plane(g, a2)))
    hid_t[...] = jnp.transpose(jnp.concatenate([hidden, jnp.zeros((112, 256), F32)], axis=0)).astype(BF16)
    for copy in rs1:
        copy.wait_recv()

    def reduced(i):
        return ((town[i] + r1[0, i].astype(F32)) + r1[1, i].astype(F32)) + r1[2, i].astype(F32)

    rs2 = []
    for d in OFFSETS:
        i = (a2 + d) % 4
        p2s[d - 1] = reduced(i).astype(BF16)
        rs2.append(send(p2s.at[d - 1], r2.at[d - 1], rs_send.at[2 + d], rs_recv.at[2 + d], plane(a1, i)))
    mine_sum = reduced(a2)
    for copy in rs2:
        copy.wait_recv()
    mine_sum = ((mine_sum + r2[0].astype(F32)) + r2[1].astype(F32)) + r2[2].astype(F32)

    zs[...] = mine_sum.astype(BF16)
    zp = send(zs, rz0, z_send.at[0], z_recv.at[0], (y, x, z - sg, c))
    zp.wait_recv()
    total = mine_sum + rz0[...].astype(F32)
    zes[...] = total.astype(BF16)
    zc = [
        send(zes, rz.at[k], z_send.at[1 + k], z_recv.at[1 + k], (y, x, (z + sg * (k + 1) + 8) % 8, c))
        for k in range(3)
    ]
    resp_f, resp_h = total[0:ROWS], total[ROWS:CHUNK]
    for k in range(3):
        zc[k].wait_recv()
        resp_f = resp_f + jnp.dot(amat[k], rz[k, 0:ROWS, :], preferred_element_type=F32)
        resp_h = resp_h + jnp.dot(amat_h[k], rz[k, ROWS:CHUNK, :], preferred_element_type=F32)
    base = c * HALF + a1 * GROUP
    sig_f = sigma[:, pl.ds(pl.multiple_of(base + a2 * 128, 128), 128)]
    sig_h = sigma[:, pl.ds(pl.multiple_of(base + (4 + a2 // 2) * 128, 128), 128)]
    c4[m, 0:ROWS] = (rho_s[...] * sig_f * (resp_f * SCALE)).astype(BF16)
    c4[m, ROWS:CHUNK] = (rho_s[half_rows, :] * sig_h * (resp_h * SCALE)).astype(BF16)

    cg1 = [
        send(c4.at[m], c4.at[m], cg_send.at[d - 1], cg_recv.at[d - 1], plane(a1, (a2 + d) % 4)) for d in OFFSETS
    ]
    for copy in cg1:
        copy.wait_recv()
    cg2 = {
        d: send(c4.at[mine4], c4.at[mine4], cg_send.at[2 + d], cg_recv.at[2 + d], plane((a1 + d) % 4, a2))
        for d in OFFSETS
    }

    def assemble(ref, g):
        for i in range(4):
            cg[:, i * 128 : (i + 1) * 128] = ref[g * 4 + i, 0:ROWS, :]
        for i in range(2):
            both = [ref[g * 4 + 2 * i + u, ROWS:CHUNK, :].astype(F32) for u in range(2)]
            cg[:, (4 + i) * 128 : (5 + i) * 128] = jnp.concatenate(both, axis=0).astype(BF16)

    sums = (zero, zero, zero)
    cxs = []
    for d in (0,) + OFFSETS:
        if d:
            cg2[d].wait_recv()
        g = (a1 - d + 4) % 4
        block4 = pl.ds(pl.multiple_of(g * 4, 4), 4)
        cxs.append(send(c4.at[block4], cx.at[block4], cx_send.at[d], cx_recv.at[d], partner))
        assemble(c4, g)

        def image(k, sums):
            s0, s1, ss = sums
            part = pl.ds(pl.multiple_of(g * GROUP + k * 256, 256), 256)
            cols = cg[:, pl.ds(pl.multiple_of(k * 256, 256), 256)]
            fold = lambda a: jnp.sum(a.reshape(16, 8, 256), axis=0)
            for u in range(2):
                im = jnp.dot(hid_t[u * 128 : (u + 1) * 128, 0:ROWS], cols, preferred_element_type=F32) * SCALE
                if u == 0:
                    img[0, :, part] = im
                s0 = s0 + fold(im * v0[u, :, part].astype(F32))
                s1 = s1 + fold(im * v1[u, :, part].astype(F32))
                ss = ss + fold(im * im)
            return s0, s1, ss

        sums = lax.fori_loop(0, 3, image, sums)

    lines = [jnp.sum(s[:, 0:128] + s[:, 128:256], axis=0, keepdims=True) for s in sums + (s00, s01, s11)]
    lines.append(jnp.zeros((2, 128), F32))
    red_s[0] = jnp.concatenate(lines, axis=0)
    ras = []
    for k in range(1, 16):
        o = (p + k) % 16
        ras.append(send(red_s.at[0], red_a.at[k - 1], ra_send.at[k - 1], ra_recv.at[k - 1], (o // 4, o % 4, z, c)))

    for d in (0,) + OFFSETS:
        cxs_index = ((0,) + OFFSETS).index(d)
        cxs[cxs_index].wait_recv()
    for g in range(4):
        assemble(cx, g)

        def image_other(k, carry):
            part = pl.ds(pl.multiple_of(g * GROUP + k * 256, 256), 256)
            cols = cg[:, pl.ds(pl.multiple_of(k * 256, 256), 256)]
            img[1, :, part] = jnp.dot(hid_t[0:128, 0:ROWS], cols, preferred_element_type=F32) * SCALE
            return carry

        lax.fori_loop(0, 3, image_other, 0)

    acc = red_s[0]
    for k in range(15):
        ras[k].wait_recv()
        acc = acc + red_a[k]
    red_s[1] = acc
    rbs = []
    for k in range(1, 16):
        o = (q + k) % 16
        rbs.append(send(red_s.at[1], red_b.at[k - 1], rb_send.at[k - 1], rb_recv.at[k - 1], (y, x, o // 2, o % 2)))
    for k in range(15):
        rbs[k].wait_recv()
        acc = acc + red_b[k]
    scal = jnp.sum(acc, axis=1, keepdims=True) * (1.0 / ENTRIES)
    c0, c1, norm, g00, g01, g11 = [scal[k : k + 1, 0:1] for k in range(6)]
    norm = norm - 2.0 * (c0 * c0 + c1 * c1) + (c0 * c0 * g00 + 2.0 * (c0 * c1) * g01 + c1 * c1 * g11)
    beta = jnp.sqrt(norm)
    hess[0:1, :] = c0
    hess[1:2, :] = c1
    hess[2:3, :] = beta
    inv = 1.0 / beta
    stores = []
    for u, (w0, w1, lanes) in enumerate(((v0.at[0], v1.at[0], mine), (v0x, v1x, other))):

        def finish(k, carry):
            part = pl.ds(pl.multiple_of(k * 256, 256), 256)
            resid = (img[u, :, part] - c0 * w0[:, part].astype(F32)) - c1 * w1[:, part].astype(F32)
            out_v[u, :, part] = (resid * inv).astype(BF16)
            return carry

        lax.fori_loop(0, HALF // 256, finish, 0)
        stores.append(local(out_v.at[u], out_hbm.at[:, lanes], loc_sem.at[7 + u]))

    for copy in first + core + second + [pre_copy] + rs1 + rs2 + [zp] + zc + cg1 + list(cg2.values()) + cxs + ras + rbs:
        copy.wait_send()
    for copy in stores:
        copy.wait()


def body(tokens, w_gate, w_up, basis, routes, gates, rho, sigma):
    anywhere = pl.BlockSpec(memory_space=pl.ANY)
    vmem = pl.BlockSpec(memory_space=pltpu.VMEM)
    dma = pltpu.SemaphoreType.DMA
    scratch = [
        pltpu.VMEM((16, HALF), BF16),
        pltpu.VMEM((2, HALF, 256), BF16),
        pltpu.VMEM((2, 128, HALF), BF16),
        pltpu.VMEM((2, 128, HALF), BF16),
        pltpu.VMEM((128, HALF), BF16),
        pltpu.VMEM((128, HALF), BF16),
        pltpu.VMEM((16, 8, MSG), BF16),
        pltpu.VMEM((ROWS, HALF), BF16),
        pltpu.VMEM((4, 128, 128), F32),
        pltpu.VMEM((8, 384), F32),
        pltpu.VMEM((ROWS, 128), F32),
        pltpu.VMEM((2, ROWS, 256), F32),
        pltpu.VMEM((2, ROWS, 256), F32),
        pltpu.VMEM((ROWS, 256), BF16),
        pltpu.VMEM((256, 256), BF16),
        pltpu.VMEM((3, 4, CHUNK, 128), BF16),
        pltpu.VMEM((3, 4, CHUNK, 128), BF16),
        pltpu.VMEM((4, CHUNK, 128), F32),
        pltpu.VMEM((3, CHUNK, 128), BF16),
        pltpu.VMEM((3, CHUNK, 128), BF16),
        pltpu.VMEM((CHUNK, 128), BF16),
        pltpu.VMEM((CHUNK, 128), BF16),
        pltpu.VMEM((CHUNK, 128), BF16),
        pltpu.VMEM((3, CHUNK, 128), BF16),
        pltpu.VMEM((3, ROWS, ROWS), BF16),
        pltpu.VMEM((3, 72, 72), BF16),
        pltpu.VMEM((256, 256), F32),
        pltpu.VMEM((ROWS, 128), F32),
        pltpu.VMEM((16, CHUNK, 128), BF16),
        pltpu.VMEM((16, CHUNK, 128), BF16),
        pltpu.VMEM((ROWS, GROUP), BF16),
        pltpu.VMEM((2, 128, HALF), F32),
        pltpu.VMEM((2, 128, HALF), BF16),
        pltpu.VMEM((15, 8, 128), F32),
        pltpu.VMEM((15, 8, 128), F32),
        pltpu.VMEM((2, 8, 128), F32),
        dma((9,)),
        dma((5,)), dma((5,)),
        dma((6,)), dma((6,)),
        dma((6,)), dma((6,)),
        dma((4,)), dma((4,)),
        dma((6,)), dma((6,)),
        dma((4,)), dma((4,)),
        dma((15,)), dma((15,)),
        dma((15,)), dma((15,)),
    ]
    out, hess = pl.pallas_call(
        kernel,
        out_shape=(jax.ShapeDtypeStruct((128, D), BF16), jax.ShapeDtypeStruct((3, 1), F32)),
        in_specs=[anywhere] * 4 + [vmem] * 4,
        out_specs=(anywhere, vmem),
        scratch_shapes=scratch,
        compiler_params=pltpu.CompilerParams(
            collective_id=0, has_side_effects=True, vmem_limit_bytes=60000 * 1024
        ),
        name="arnoldi",
    )(tokens, w_gate, w_up, basis, routes, gates, rho.reshape(16, 1), sigma.reshape(1, D))
    return out, hess


def solution(mesh):
    finer = Mesh(mesh.devices.reshape(4, 4, 8, 2), AXES)
    in_specs = (
        P(DP, None),
        P(None, EXPERT_DP),
        P(None, EXPERT_DP),
        P(None, EXPERT_DP, None),
        P(),
        P(),
        P(DP),
        P(),
    )
    out_specs = (P(EXPERT_DP, None), P())
    return jax.shard_map(body, mesh=finer, in_specs=in_specs, out_specs=out_specs, check_vma=False)
```

```python
import functools
import math

import jax
import jax.numpy as jnp
from jax import lax
from jax.experimental import pallas as pl
from jax.experimental.pallas import tpu as pltpu
from jax.sharding import Mesh
from jax.sharding import PartitionSpec as P

D = 6144
FF = 8192
E = 4
HALF = 3072
GROUP = 768
SIDE = 128
MSG = HALF + SIDE + 512
ROWS = 144
CHUNK = 216
DP = ("dp_0", "dp_1")
EXPERT = ("expert_0", "expert_1")
EXPERT_DP = ("expert_0", "expert_1", "dp_0", "dp_1")
AXES = ("dp_0", "dp_1", "expert_0", "expert_1")
MESH = pl.DeviceIdType.MESH
F32 = jnp.float32
BF16 = jnp.bfloat16
SCALE = 1.0 / math.sqrt(FF)
KAPPA = E * FF / 256
ENTRIES = float(E * FF * D)
OFFSETS = (1, 3, 2)


def iota(shape, dim):
    return lax.broadcasted_iota(jnp.int32, shape, dim)


def parts(col):
    hi = col.astype(BF16)
    left = col - hi.astype(F32)
    mid = left.astype(BF16)
    low = (left - mid.astype(F32)).astype(BF16)
    return hi.astype(F32), mid.astype(F32), low.astype(F32)


def joined(side, first):
    return (side[:, first : first + 1] + side[:, first + 1 : first + 2]) + side[:, first + 2 : first + 3]


def slot_order(m):
    return jnp.concatenate([m[0:64], m[128:136], m[64:128], m[136:144]], axis=0)


def kernel(
    tok_hbm, wg_hbm, wu_hbm, basis_hbm, routes_hbm, gates_hbm, rho_hbm, sigma_hbm,
    out, hess,
    routes, gates, rho, sigma, cols, tokv, wbuf, v0, v1, v0x, v1x, gm, gd, exf, exs, side_main, pre_s, pre_r, hid, hid_t,
    tb, r1, town, p2s, r2, zs, rz0, zes, rz, amat, amat_h, rank_s, rho_s, c4, cx, cg, img,
    red_a, red_b, red_s,
    loc_sem, core_send, core_recv, ag_send, ag_recv, rs_send, rs_recv, z_send, z_recv,
    cg_send, cg_recv, cx_send, cx_recv, ra_send, ra_recv, rb_send, rb_recv,
):
    y, x, z, c = [lax.axis_index(name) for name in AXES]
    a1 = y * (1 - c) + x * c
    a2 = x * (1 - c) + y * c
    p = y * 4 + x
    q = z * 2 + c
    e = z // 2

    def plane(b1, b2):
        return (b1 * (1 - c) + b2 * c, b2 * (1 - c) + b1 * c, z, c)

    def send(src, dst, s_sem, r_sem, device):
        copy = pltpu.make_async_remote_copy(
            src_ref=src, dst_ref=dst, send_sem=s_sem, recv_sem=r_sem, device_id=device, device_id_type=MESH
        )
        copy.start()
        return copy

    def local(src, dst, sem):
        copy = pltpu.make_async_copy(src, dst, sem)
        copy.start()
        return copy

    mine = pl.ds(pl.multiple_of(c * HALF, HALF), HALF)
    other = pl.ds(pl.multiple_of((1 - c) * HALF, HALF), HALF)
    small = [
        local(routes_hbm, routes, loc_sem.at[7]),
        local(gates_hbm, gates, loc_sem.at[8]),
        local(rho_hbm, rho, loc_sem.at[9]),
    ]
    loads = [
        local(tok_hbm.at[:, mine], tokv, loc_sem.at[0]),
        local(wg_hbm.at[mine, :], wbuf.at[0, :, pl.ds(0, 128)], loc_sem.at[1]),
        local(wu_hbm.at[mine, :], wbuf.at[0, :, pl.ds(128, 128)], loc_sem.at[2]),
        local(basis_hbm.at[1, :, mine], v1.at[0], loc_sem.at[3]),
        local(basis_hbm.at[0, :, mine], v0.at[0], loc_sem.at[4]),
        local(basis_hbm.at[1, :, other], v1x, loc_sem.at[5]),
        local(basis_hbm.at[0, :, other], v0x, loc_sem.at[6]),
        local(sigma_hbm, sigma, loc_sem.at[10]),
    ]
    barrier = pltpu.get_barrier_semaphore()
    for k in range(1, 16):
        o = (p + k) % 16
        pl.semaphore_signal(barrier, inc=1, device_id=(o // 4, o % 4, z, c), device_id_type=MESH)
        o = (q + k) % 16
        pl.semaphore_signal(barrier, inc=1, device_id=(y, x, o // 2, o % 2), device_id_type=MESH)

    for copy in small:
        copy.wait()

    cols[...] = jnp.transpose(
        jnp.concatenate([routes[...].astype(F32), gates[...], jnp.zeros((4, 256), F32)], axis=0)
    )
    own = cols[pl.ds(pl.multiple_of(p * 16, 16), 16), :]
    ef = e.astype(F32)
    hit0 = own[:, 0:1] == ef
    hit1 = own[:, 1:2] == ef
    member = hit0.astype(F32) + hit1.astype(F32)
    gate_tok = jnp.where(hit0, own[:, 2:3], 0.0) + jnp.where(hit1, own[:, 3:4], 0.0)
    tri = (iota((16, 16), 1) <= iota((16, 16), 0)).astype(F32).astype(BF16)
    member_b = jnp.broadcast_to(member, (16, 128))
    rank = jnp.dot(tri, member_b.astype(BF16), preferred_element_type=F32)
    lane = iota((16, 128), 1)
    place_t = jnp.where((rank - 1.0 == lane.astype(F32)) & (member_b > 0), 1.0, 0.0)
    place = jnp.transpose(place_t)[0:16, :].astype(BF16)
    diagonal = iota((16, 16), 0) == iota((16, 16), 1)
    rho_tok = jnp.sum(jnp.where(diagonal, jnp.broadcast_to(rho[...], (16, 16)), 0.0), axis=1, keepdims=True)
    r_hi, r_mid, r_low = parts(rho_tok)
    g_hi, g_mid, g_low = parts(gate_tok)
    side_in = jnp.zeros((16, 128), F32)
    for index, col in enumerate((r_hi, r_mid, r_low, g_hi, g_mid, g_low)):
        side_in = jnp.where(lane == index, col, side_in)
    side = jnp.dot(place, side_in.astype(BF16), preferred_element_type=F32)
    m = a1 * 4 + a2
    gm[m, :, HALF : HALF + SIDE] = side[0:8].astype(BF16)
    gm[m, :, HALF + SIDE + 384 : MSG] = jnp.broadcast_to(side[8:9], (8, 128)).astype(BF16)
    loads[0].wait()
    picked = jnp.dot(place, tokv[...], preferred_element_type=F32)
    gm[m, :, 0:HALF] = picked[0:8].astype(BF16)
    for r in range(8):
        exs[r : r + 1, :] = picked[8:9, r * 384 : (r + 1) * 384]
    gm[m, :, HALF + SIDE : HALF + SIDE + 384] = exs[...].astype(BF16)

    pl.semaphore_wait(barrier, 30)

    def spread(ref, index, lap, s_sem, r_sem):
        return [
            send(ref.at[index], ref.at[index], s_sem.at[lap, d - 1], r_sem.at[lap, d - 1], plane((a1 + d) % 4, a2))
            for d in OFFSETS
        ]

    def along(ref, s_sem, r_sem):
        return [
            send(ref.at[m], ref.at[m], s_sem.at[4, d - 1], r_sem.at[4, d - 1], plane(a1, (a2 + d) % 4))
            for d in OFFSETS
        ]

    def behind(d):
        return a1 * 4 + (a2 + 4 - d) % 4

    first = along(gm, ag_send, ag_recv)
    second = spread(gm, m, 0, ag_send, ag_recv)
    partner = (y, x, z, 1 - c)
    core = [
        send(wg_hbm.at[other, :], wbuf.at[1, :, pl.ds(0, 128)], core_send.at[0], core_recv.at[0], partner),
        send(wu_hbm.at[other, :], wbuf.at[1, :, pl.ds(128, 128)], core_send.at[1], core_recv.at[1], partner),
        send(basis_hbm.at[1, :, other], v1.at[1], core_send.at[2], core_recv.at[2], partner),
        send(basis_hbm.at[0, :, other], v0.at[1], core_send.at[3], core_recv.at[3], partner),
    ]

    sg = 2 * (z % 2) - 1
    t_lane = iota((256, 128), 1)
    shift = jnp.where(t_lane == 1, sg, 0) + jnp.where(t_lane == 2, -sg, 0) + jnp.where(t_lane == 3, 2, 0)
    names = jnp.where(t_lane < 4, (e + shift + 4) & 3, -1)
    names = names.astype(F32)
    member4 = (cols[:, 0:1] == names).astype(F32) + (cols[:, 1:2] == names).astype(F32)
    low = iota((256, 256), 0)
    col = iota((256, 256), 1)
    tri_b = ((col <= low) & ((col >> 4) == (low >> 4))).astype(F32).astype(BF16)
    rank4 = jnp.dot(tri_b, member4.astype(BF16), preferred_element_type=F32)
    token = iota((256, 128), 0)
    block = token >> 4
    slot = rank4.astype(jnp.int32) - 1
    where_to = (block >> 3) * 72 + jnp.where(slot < 8, (block & 7) * 8 + slot, 64 + (block & 7))
    where_to = jnp.where(member4 > 0, where_to, -1000)
    onehot = (where_to[:, 0:1] == col).astype(F32)
    rank_s[...] = jnp.transpose(onehot)
    h = a2 % 2
    half_rows = pl.ds(pl.multiple_of(h * 72, 8), 72)
    own_full = rank_s[0:ROWS, :].astype(BF16)
    own_half = rank_s[half_rows, :].astype(BF16)
    for k in range(3):
        theirs = (where_to[:, k + 1 : k + 2] == col).astype(F32).astype(BF16)
        amat[k] = jnp.dot(own_full, theirs, preferred_element_type=F32)[:, 0:ROWS].astype(BF16)
        theirs = (where_to[:, k + 1 : k + 2] - h * 72 == col).astype(F32).astype(BF16)
        amat_h[k] = jnp.dot(own_half, theirs, preferred_element_type=F32)[:, 0:72].astype(BF16)

    for d, copy in zip(OFFSETS, first):
        copy.wait_recv()
        second += spread(gm, behind(d), d, ag_send, ag_recv)

    for copy in loads[1:]:
        copy.wait()
    for copy in core[2:]:
        copy.wait_recv()

    def gram(k, sums):
        s00, s01, s11 = sums
        part = pl.ds(pl.multiple_of(k * 256, 256), 256)
        for u in range(2):
            b0 = v0[u, :, part].astype(F32)
            b1 = v1[u, :, part].astype(F32)
            fold = lambda a: jnp.sum(a.reshape(16, 8, 256), axis=0)
            s00 = s00 + fold(b0 * b0)
            s01 = s01 + fold(b0 * b1)
            s11 = s11 + fold(b1 * b1)
        return s00, s01, s11

    zero = jnp.zeros((8, 256), F32)
    s00, s01, s11 = lax.fori_loop(0, HALF // 256, gram, (zero, zero, zero))

    for copy in second:
        copy.wait_recv()
    for copy in core[:2]:
        copy.wait_recv()

    def source(o):
        return o * (1 - c) + ((o % 4) * 4 + o // 4) * c

    for k in range(8):
        pair = [gm[source(2 * k + u), :, 0:HALF].astype(F32) for u in range(2)]
        gd[16 * k : 16 * k + 16, :] = jnp.concatenate(pair, axis=0).astype(BF16)
    for o in range(16):
        block_o = gm[source(o)][:, HALF:MSG].astype(F32)
        side_main[8 * o : 8 * o + 8, :] = block_o[:, 0:SIDE]
        for t in range(4):
            exf[t, 8 * o : 8 * o + 8, :] = block_o[:, SIDE + t * 128 : SIDE + (t + 1) * 128]
    for r in range(8):
        for t in range(3):
            f = r * 384 + t * 128
            gd[128:144, f : f + 128] = exf[t, pl.ds(r, 16, stride=8), :].astype(BF16)
    side_main[128:144, :] = exf[3, pl.ds(0, 16, stride=8), :]

    for u in range(2):
        pre_s[u] = jnp.dot(gd[...], wbuf[u], preferred_element_type=F32)
    pre_copy = send(pre_s, pre_r, core_send.at[4], core_recv.at[4], partner)
    side_all = side_main[...]
    rho_slot = slot_order(jnp.broadcast_to(joined(side_all, 0), (ROWS, 128)))
    rho_s[...] = KAPPA * rho_slot
    gate_slot = slot_order(jnp.broadcast_to(joined(side_all, 3), (ROWS, 128)))
    pre_copy.wait_recv()
    hidden = []
    for u in range(2):
        both = slot_order(pre_s[u] + pre_r[1 - u])
        gate, up = both[:, 0:128], both[:, 128:256]
        hidden.append(gate / (1.0 + jnp.exp(-gate)) * up * gate_slot)
    hidden = jnp.concatenate(hidden, axis=1)
    hid[...] = hidden.astype(BF16)

    rs1 = {}
    for d in OFFSETS + (0,):
        g = (a1 + d) % 4
        part = pl.ds(pl.multiple_of(g * GROUP, GROUP), GROUP)
        rows = v1[:, :, part].reshape(256, GROUP)
        tangent = jnp.dot(hid[...], rows, preferred_element_type=F32)
        for i in range(4):
            t = 4 + i // 2
            full = tangent[:, i * 128 : (i + 1) * 128]
            half = tangent[(i % 2) * 72 : (i % 2) * 72 + 72, t * 128 : (t + 1) * 128]
            if d:
                tb[d - 1, i, 0:ROWS] = full.astype(BF16)
                tb[d - 1, i, ROWS:CHUNK] = half.astype(BF16)
            else:
                town[i, 0:ROWS] = full
                town[i, ROWS:CHUNK] = half
        if d:
            for o in OFFSETS + (0,):
                i = (a2 + o) % 4
                rs1[o, d] = send(
                    tb.at[d - 1, i], r1.at[d - 1, i], rs_send.at[o, d - 1], rs_recv.at[o, d - 1], plane(g, a2)
                )
    hid_t[...] = jnp.transpose(jnp.concatenate([hidden, jnp.zeros((112, 256), F32)], axis=0)).astype(BF16)

    def reduced(i):
        return ((town[i] + r1[0, i].astype(F32)) + r1[1, i].astype(F32)) + r1[2, i].astype(F32)

    rs2 = []
    for o in OFFSETS + (0,):
        for d in OFFSETS:
            rs1[o, d].wait_recv()
        i = (a2 + o) % 4
        if o:
            p2s[o - 1] = reduced(i).astype(BF16)
            rs2.append(send(p2s.at[o - 1], r2.at[o - 1], rs_send.at[4, o - 1], rs_recv.at[4, o - 1], plane(a1, i)))
    mine_sum = reduced(a2)
    for copy in rs2:
        copy.wait_recv()
    mine_sum = ((mine_sum + r2[0].astype(F32)) + r2[1].astype(F32)) + r2[2].astype(F32)

    zs[...] = mine_sum.astype(BF16)
    zp = send(zs, rz0, z_send.at[0], z_recv.at[0], (y, x, z - sg, c))
    zp.wait_recv()
    total = mine_sum + rz0[...].astype(F32)
    zes[...] = total.astype(BF16)
    zc = [
        send(zes, rz.at[k], z_send.at[1 + k], z_recv.at[1 + k], (y, x, (z + sg * (k + 1) + 8) % 8, c))
        for k in range(3)
    ]
    resp_f, resp_h = total[0:ROWS], total[ROWS:CHUNK]
    for k in range(3):
        zc[k].wait_recv()
        resp_f = resp_f + jnp.dot(amat[k], rz[k, 0:ROWS, :], preferred_element_type=F32)
        resp_h = resp_h + jnp.dot(amat_h[k], rz[k, ROWS:CHUNK, :], preferred_element_type=F32)
    base = c * HALF + a1 * GROUP
    sig_f = sigma[:, pl.ds(pl.multiple_of(base + a2 * 128, 128), 128)]
    sig_h = sigma[:, pl.ds(pl.multiple_of(base + (4 + a2 // 2) * 128, 128), 128)]
    c4[m, 0:ROWS] = (rho_s[...] * sig_f * (resp_f * SCALE)).astype(BF16)
    c4[m, ROWS:CHUNK] = (rho_s[half_rows, :] * sig_h * (resp_h * SCALE)).astype(BF16)

    cg1 = along(c4, cg_send, cg_recv)
    cg2 = [spread(c4, m, 0, cg_send, cg_recv)]
    for d, copy in zip(OFFSETS, cg1):
        copy.wait_recv()
        cg2.append(spread(c4, behind(d), d, cg_send, cg_recv))

    def assemble(ref, g):
        for i in range(4):
            cg[:, i * 128 : (i + 1) * 128] = ref[g * 4 + i, 0:ROWS, :]
        for i in range(2):
            both = [ref[g * 4 + 2 * i + u, ROWS:CHUNK, :].astype(F32) for u in range(2)]
            cg[:, (4 + i) * 128 : (5 + i) * 128] = jnp.concatenate(both, axis=0).astype(BF16)

    sums = (zero, zero, zero)
    cxs = []
    for n, d in enumerate((0,) + OFFSETS):
        if d:
            for copies in cg2:
                copies[n - 1].wait_recv()
        g = (a1 - d + 4) % 4
        block4 = pl.ds(pl.multiple_of(g * 4, 4), 4)
        cxs.append(send(c4.at[block4], cx.at[block4], cx_send.at[d], cx_recv.at[d], partner))
        assemble(c4, g)

        def image(k, sums):
            s0, s1, ss = sums
            part = pl.ds(pl.multiple_of(g * GROUP + k * 256, 256), 256)
            cols = cg[:, pl.ds(pl.multiple_of(k * 256, 256), 256)]
            fold = lambda a: jnp.sum(a.reshape(16, 8, 256), axis=0)
            for u in range(2):
                im = jnp.dot(hid_t[u * 128 : (u + 1) * 128, 0:ROWS], cols, preferred_element_type=F32) * SCALE
                if u == 0:
                    img[0, :, part] = im
                s0 = s0 + fold(im * v0[u, :, part].astype(F32))
                s1 = s1 + fold(im * v1[u, :, part].astype(F32))
                ss = ss + fold(im * im)
            return s0, s1, ss

        sums = lax.fori_loop(0, 3, image, sums)

    lines = [jnp.sum(s[:, 0:128] + s[:, 128:256], axis=0, keepdims=True) for s in sums + (s00, s01, s11)]
    lines.append(jnp.zeros((2, 128), F32))
    red_s[0] = jnp.concatenate(lines, axis=0)
    ras = []
    for k in range(1, 16):
        o = (p + k) % 16
        ras.append(send(red_s.at[0], red_a.at[k - 1], ra_send.at[k - 1], ra_recv.at[k - 1], (o // 4, o % 4, z, c)))

    for copy in cxs:
        copy.wait_recv()
    for g in range(4):
        assemble(cx, g)

        def image_other(k, carry):
            part = pl.ds(pl.multiple_of(g * GROUP + k * 256, 256), 256)
            cols = cg[:, pl.ds(pl.multiple_of(k * 256, 256), 256)]
            img[1, :, part] = jnp.dot(hid_t[0:128, 0:ROWS], cols, preferred_element_type=F32) * SCALE
            return carry

        lax.fori_loop(0, 3, image_other, 0)

    acc = red_s[0]
    for k in range(15):
        ras[k].wait_recv()
        acc = acc + red_a[k]
    red_s[1] = acc
    rbs = []
    for k in range(1, 16):
        o = (q + k) % 16
        rbs.append(send(red_s.at[1], red_b.at[k - 1], rb_send.at[k - 1], rb_recv.at[k - 1], (y, x, o // 2, o % 2)))
    for k in range(15):
        rbs[k].wait_recv()
        acc = acc + red_b[k]
    scal = jnp.sum(acc, axis=1, keepdims=True) * (1.0 / ENTRIES)
    c0, c1, norm, g00, g01, g11 = [scal[k : k + 1, 0:1] for k in range(6)]
    norm = norm - 2.0 * (c0 * c0 + c1 * c1) + (c0 * c0 * g00 + 2.0 * (c0 * c1) * g01 + c1 * c1 * g11)
    beta = jnp.sqrt(norm)
    hess[...] = jnp.concatenate([c0, c1, beta], axis=1)
    inv = 1.0 / beta
    for u, (w0, w1, start) in enumerate(((v0.at[0], v1.at[0], c * HALF), (v0x, v1x, (1 - c) * HALF))):

        def finish(k, carry):
            part = pl.ds(pl.multiple_of(k * 256, 256), 256)
            resid = (img[u, :, part] - c0 * w0[:, part].astype(F32)) - c1 * w1[:, part].astype(F32)
            out[:, pl.ds(pl.multiple_of(start + k * 256, 256), 256)] = (resid * inv).astype(BF16)
            return carry

        lax.fori_loop(0, HALF // 256, finish, 0)

    for copy in first + core + second + [pre_copy] + list(rs1.values()) + rs2 + [zp] + zc + cg1 + sum(cg2, []) + cxs + ras + rbs:
        copy.wait_send()


def body(tokens, w_gate, w_up, basis, routes, gates, rho, sigma):
    anywhere = pl.BlockSpec(memory_space=pl.ANY)
    vmem = pl.BlockSpec(memory_space=pltpu.VMEM)
    dma = pltpu.SemaphoreType.DMA
    scratch = [
        pltpu.VMEM((2, 256), jnp.int32),
        pltpu.VMEM((2, 256), F32),
        pltpu.VMEM((1, 16), F32),
        pltpu.VMEM((1, D), F32),
        pltpu.VMEM((256, 8), F32),
        pltpu.VMEM((16, HALF), BF16),
        pltpu.VMEM((2, HALF, 256), BF16),
        pltpu.VMEM((2, 128, HALF), BF16),
        pltpu.VMEM((2, 128, HALF), BF16),
        pltpu.VMEM((128, HALF), BF16),
        pltpu.VMEM((128, HALF), BF16),
        pltpu.VMEM((16, 8, MSG), BF16),
        pltpu.VMEM((ROWS, HALF), BF16),
        pltpu.VMEM((4, 128, 128), F32),
        pltpu.VMEM((8, 384), F32),
        pltpu.VMEM((ROWS, 128), F32),
        pltpu.VMEM((2, ROWS, 256), F32),
        pltpu.VMEM((2, ROWS, 256), F32),
        pltpu.VMEM((ROWS, 256), BF16),
        pltpu.VMEM((256, 256), BF16),
        pltpu.VMEM((3, 4, CHUNK, 128), BF16),
        pltpu.VMEM((3, 4, CHUNK, 128), BF16),
        pltpu.VMEM((4, CHUNK, 128), F32),
        pltpu.VMEM((3, CHUNK, 128), BF16),
        pltpu.VMEM((3, CHUNK, 128), BF16),
        pltpu.VMEM((CHUNK, 128), BF16),
        pltpu.VMEM((CHUNK, 128), BF16),
        pltpu.VMEM((CHUNK, 128), BF16),
        pltpu.VMEM((3, CHUNK, 128), BF16),
        pltpu.VMEM((3, ROWS, ROWS), BF16),
        pltpu.VMEM((3, 72, 72), BF16),
        pltpu.VMEM((256, 256), F32),
        pltpu.VMEM((ROWS, 128), F32),
        pltpu.VMEM((16, CHUNK, 128), BF16),
        pltpu.VMEM((16, CHUNK, 128), BF16),
        pltpu.VMEM((ROWS, GROUP), BF16),
        pltpu.VMEM((2, 128, HALF), F32),
        pltpu.VMEM((15, 8, 128), F32),
        pltpu.VMEM((15, 8, 128), F32),
        pltpu.VMEM((2, 8, 128), F32),
        dma((11,)),
        dma((5,)), dma((5,)),
        dma((5, 3)), dma((5, 3)),
        dma((5, 3)), dma((5, 3)),
        dma((4,)), dma((4,)),
        dma((5, 3)), dma((5, 3)),
        dma((4,)), dma((4,)),
        dma((15,)), dma((15,)),
        dma((15,)), dma((15,)),
    ]
    operands = (tokens, w_gate, w_up, basis, routes.T, gates.T, rho.reshape(1, 16), sigma.reshape(1, D))
    operands = [pltpu.with_memory_space_constraint(a, pltpu.HBM) for a in operands]
    out, hess = pl.pallas_call(
        kernel,
        out_shape=(jax.ShapeDtypeStruct((128, D), BF16), jax.ShapeDtypeStruct((1, 3), F32)),
        in_specs=[anywhere] * 8,
        out_specs=(vmem, vmem),
        scratch_shapes=scratch,
        compiler_params=pltpu.CompilerParams(
            collective_id=0, has_side_effects=True, vmem_limit_bytes=26 * 1024 * 1024
        ),
        name="arnoldi",
    )(*operands)
    return out, hess.T


def solution(mesh):
    finer = Mesh(mesh.devices.reshape(4, 4, 8, 2), AXES)
    in_specs = (
        P(DP, None),
        P(None, EXPERT_DP),
        P(None, EXPERT_DP),
        P(None, EXPERT_DP, None),
        P(),
        P(),
        P(DP),
        P(),
    )
    out_specs = (P(EXPERT_DP, None), P())
    return jax.shard_map(body, mesh=finer, in_specs=in_specs, out_specs=out_specs, check_vma=False)
```

```python
import functools
import math

import jax
import jax.numpy as jnp
from jax import lax
from jax.experimental import pallas as pl
from jax.experimental.pallas import tpu as pltpu
from jax.sharding import Mesh
from jax.sharding import PartitionSpec as P

D = 6144
FF = 8192
E = 4
HALF = 3072
GROUP = 768
SIDE = 128
MSG = HALF + SIDE + 512
ROWS = 144
CHUNK = 216
DP = ("dp_0", "dp_1")
EXPERT = ("expert_0", "expert_1")
EXPERT_DP = ("expert_0", "expert_1", "dp_0", "dp_1")
AXES = ("dp_0", "dp_1", "expert_0", "expert_1")
MESH = pl.DeviceIdType.MESH
F32 = jnp.float32
BF16 = jnp.bfloat16
SCALE = 1.0 / math.sqrt(FF)
KAPPA = E * FF / 256
ENTRIES = float(E * FF * D)
OFFSETS = (1, 3, 2)


def iota(shape, dim):
    return lax.broadcasted_iota(jnp.int32, shape, dim)


def parts(col):
    hi = col.astype(BF16)
    left = col - hi.astype(F32)
    mid = left.astype(BF16)
    low = (left - mid.astype(F32)).astype(BF16)
    return hi.astype(F32), mid.astype(F32), low.astype(F32)


def joined(side, first):
    return (side[:, first : first + 1] + side[:, first + 1 : first + 2]) + side[:, first + 2 : first + 3]


def slot_order(m):
    return jnp.concatenate([m[0:64], m[128:136], m[64:128], m[136:144]], axis=0)


def kernel(
    tok_hbm, wg_hbm, wu_hbm, basis_hbm, routes_hbm, gates_hbm, rho_hbm, sigma_hbm,
    out, hess,
    routes, gates, rho, sigma, cols, tokv, wbuf, v0, v1, v0x, v1x, gm, gd, exf, exs, side_main, pre_s, pre_r, hid, hid_t,
    tb, r1, town, p2s, r2, tb0, r10, town0, p2s0, r20, held, sq_own, sq_out, sq_in, zs, rz0, zes, rz, amat, amat_h, rank_s, rho_s, c4, cx, cg, img,
    red_a, red_b, red_s,
    loc_sem, core_send, core_recv, ag_send, ag_recv, rs_send, rs_recv, rt_send, rt_recv, sq_send, sq_recv, z_send, z_recv,
    cg_send, cg_recv, cx_send, cx_recv, ra_send, ra_recv, rb_send, rb_recv,
):
    y, x, z, c = [lax.axis_index(name) for name in AXES]
    a1 = y * (1 - c) + x * c
    a2 = x * (1 - c) + y * c
    p = y * 4 + x
    q = z * 2 + c
    e = z // 2

    def plane(b1, b2):
        return (b1 * (1 - c) + b2 * c, b2 * (1 - c) + b1 * c, z, c)

    def send(src, dst, s_sem, r_sem, device):
        copy = pltpu.make_async_remote_copy(
            src_ref=src, dst_ref=dst, send_sem=s_sem, recv_sem=r_sem, device_id=device, device_id_type=MESH
        )
        copy.start()
        return copy

    def local(src, dst, sem):
        copy = pltpu.make_async_copy(src, dst, sem)
        copy.start()
        return copy

    mine = pl.ds(pl.multiple_of(c * HALF, HALF), HALF)
    other = pl.ds(pl.multiple_of((1 - c) * HALF, HALF), HALF)
    small = [
        local(routes_hbm, routes, loc_sem.at[7]),
        local(gates_hbm, gates, loc_sem.at[8]),
        local(rho_hbm, rho, loc_sem.at[9]),
    ]
    loads = [
        local(tok_hbm.at[:, mine], tokv, loc_sem.at[0]),
        local(wg_hbm.at[mine, :], wbuf.at[0, :, pl.ds(0, 128)], loc_sem.at[1]),
        local(wu_hbm.at[mine, :], wbuf.at[0, :, pl.ds(128, 128)], loc_sem.at[2]),
        local(basis_hbm.at[1, :, mine], v1.at[0], loc_sem.at[3]),
        local(basis_hbm.at[0, :, mine], v0.at[0], loc_sem.at[4]),
        local(basis_hbm.at[1, :, other], v1x, loc_sem.at[5]),
        local(basis_hbm.at[0, :, other], v0x, loc_sem.at[6]),
        local(sigma_hbm, sigma, loc_sem.at[10]),
    ]
    barrier = pltpu.get_barrier_semaphore()
    for k in range(1, 16):
        o = (p + k) % 16
        pl.semaphore_signal(barrier, inc=1, device_id=(o // 4, o % 4, z, c), device_id_type=MESH)
        o = (q + k) % 16
        pl.semaphore_signal(barrier, inc=1, device_id=(y, x, o // 2, o % 2), device_id_type=MESH)

    for copy in small:
        copy.wait()

    cols[...] = jnp.transpose(
        jnp.concatenate([routes[...].astype(F32), gates[...], jnp.zeros((4, 256), F32)], axis=0)
    )
    own = cols[pl.ds(pl.multiple_of(p * 16, 16), 16), :]
    ef = e.astype(F32)
    hit0 = own[:, 0:1] == ef
    hit1 = own[:, 1:2] == ef
    member = hit0.astype(F32) + hit1.astype(F32)
    gate_tok = jnp.where(hit0, own[:, 2:3], 0.0) + jnp.where(hit1, own[:, 3:4], 0.0)
    tri = (iota((16, 16), 1) <= iota((16, 16), 0)).astype(F32).astype(BF16)
    member_b = jnp.broadcast_to(member, (16, 128))
    rank = jnp.dot(tri, member_b.astype(BF16), preferred_element_type=F32)
    lane = iota((16, 128), 1)
    place_t = jnp.where((rank - 1.0 == lane.astype(F32)) & (member_b > 0), 1.0, 0.0)
    place = jnp.transpose(place_t)[0:16, :].astype(BF16)
    diagonal = iota((16, 16), 0) == iota((16, 16), 1)
    rho_tok = jnp.sum(jnp.where(diagonal, jnp.broadcast_to(rho[...], (16, 16)), 0.0), axis=1, keepdims=True)
    r_hi, r_mid, r_low = parts(rho_tok)
    g_hi, g_mid, g_low = parts(gate_tok)
    side_in = jnp.zeros((16, 128), F32)
    for index, col in enumerate((r_hi, r_mid, r_low, g_hi, g_mid, g_low)):
        side_in = jnp.where(lane == index, col, side_in)
    side = jnp.dot(place, side_in.astype(BF16), preferred_element_type=F32)
    m = a1 * 4 + a2
    gm[m, :, HALF : HALF + SIDE] = side[0:8].astype(BF16)
    gm[m, :, HALF + SIDE + 384 : MSG] = jnp.broadcast_to(side[8:9], (8, 128)).astype(BF16)
    loads[0].wait()
    picked = jnp.dot(place, tokv[...], preferred_element_type=F32)
    gm[m, :, 0:HALF] = picked[0:8].astype(BF16)
    for r in range(8):
        exs[r : r + 1, :] = picked[8:9, r * 384 : (r + 1) * 384]
    gm[m, :, HALF + SIDE : HALF + SIDE + 384] = exs[...].astype(BF16)

    pl.semaphore_wait(barrier, 30)

    def spread(ref, index, lap, s_sem, r_sem):
        return [
            send(ref.at[index], ref.at[index], s_sem.at[lap, d - 1], r_sem.at[lap, d - 1], plane((a1 + d) % 4, a2))
            for d in OFFSETS
        ]

    def along(ref, s_sem, r_sem):
        return [
            send(ref.at[m], ref.at[m], s_sem.at[4, d - 1], r_sem.at[4, d - 1], plane(a1, (a2 + d) % 4))
            for d in OFFSETS
        ]

    def behind(d):
        return a1 * 4 + (a2 + 4 - d) % 4

    first = along(gm, ag_send, ag_recv)
    second = spread(gm, m, 0, ag_send, ag_recv)
    partner = (y, x, z, 1 - c)
    core = [
        send(wg_hbm.at[other, :], wbuf.at[1, :, pl.ds(0, 128)], core_send.at[0], core_recv.at[0], partner),
        send(wu_hbm.at[other, :], wbuf.at[1, :, pl.ds(128, 128)], core_send.at[1], core_recv.at[1], partner),
        send(basis_hbm.at[1, :, other], v1.at[1], core_send.at[2], core_recv.at[2], partner),
        send(basis_hbm.at[0, :, other], v0.at[1], core_send.at[3], core_recv.at[3], partner),
    ]

    sg = 2 * (z % 2) - 1
    t_lane = iota((256, 128), 1)
    shift = jnp.where(t_lane == 1, sg, 0) + jnp.where(t_lane == 2, -sg, 0) + jnp.where(t_lane == 3, 2, 0)
    names = jnp.where(t_lane < 4, (e + shift + 4) & 3, -1)
    names = names.astype(F32)
    member4 = (cols[:, 0:1] == names).astype(F32) + (cols[:, 1:2] == names).astype(F32)
    low = iota((256, 256), 0)
    col = iota((256, 256), 1)
    tri_b = ((col <= low) & ((col >> 4) == (low >> 4))).astype(F32).astype(BF16)
    rank4 = jnp.dot(tri_b, member4.astype(BF16), preferred_element_type=F32)
    token = iota((256, 128), 0)
    block = token >> 4
    slot = rank4.astype(jnp.int32) - 1
    where_to = (block >> 3) * 72 + jnp.where(slot < 8, (block & 7) * 8 + slot, 64 + (block & 7))
    where_to = jnp.where(member4 > 0, where_to, -1000)
    onehot = (where_to[:, 0:1] == col).astype(F32)
    rank_s[...] = jnp.transpose(onehot)
    h = a2 % 2
    half_rows = pl.ds(pl.multiple_of(h * 72, 8), 72)
    own_full = rank_s[0:ROWS, :].astype(BF16)
    own_half = rank_s[half_rows, :].astype(BF16)
    for k in range(3):
        theirs = (where_to[:, k + 1 : k + 2] == col).astype(F32).astype(BF16)
        amat[k] = jnp.dot(own_full, theirs, preferred_element_type=F32)[:, 0:ROWS].astype(BF16)
        theirs = (where_to[:, k + 1 : k + 2] - h * 72 == col).astype(F32).astype(BF16)
        amat_h[k] = jnp.dot(own_half, theirs, preferred_element_type=F32)[:, 0:72].astype(BF16)

    for d, copy in zip(OFFSETS, first):
        copy.wait_recv()
        second += spread(gm, behind(d), d, ag_send, ag_recv)

    for copy in loads[1:]:
        copy.wait()
    for copy in core[2:]:
        copy.wait_recv()

    def gram(k, sums):
        s00, s01, s11 = sums
        part = pl.ds(pl.multiple_of(k * 256, 256), 256)
        for u in range(2):
            b0 = v0[u, :, part].astype(F32)
            b1 = v1[u, :, part].astype(F32)
            fold = lambda a: jnp.sum(a.reshape(16, 8, 256), axis=0)
            s00 = s00 + fold(b0 * b0)
            s01 = s01 + fold(b0 * b1)
            s11 = s11 + fold(b1 * b1)
        return s00, s01, s11

    zero = jnp.zeros((8, 256), F32)
    s00, s01, s11 = lax.fori_loop(0, HALF // 256, gram, (zero, zero, zero))

    for copy in second:
        copy.wait_recv()
    for copy in core[:2]:
        copy.wait_recv()

    def source(o):
        return o * (1 - c) + ((o % 4) * 4 + o // 4) * c

    for k in range(8):
        pair = [gm[source(2 * k + u), :, 0:HALF].astype(F32) for u in range(2)]
        gd[16 * k : 16 * k + 16, :] = jnp.concatenate(pair, axis=0).astype(BF16)
    for o in range(16):
        block_o = gm[source(o)][:, HALF:MSG].astype(F32)
        side_main[8 * o : 8 * o + 8, :] = block_o[:, 0:SIDE]
        for t in range(4):
            exf[t, 8 * o : 8 * o + 8, :] = block_o[:, SIDE + t * 128 : SIDE + (t + 1) * 128]
    for r in range(8):
        for t in range(3):
            f = r * 384 + t * 128
            gd[128:144, f : f + 128] = exf[t, pl.ds(r, 16, stride=8), :].astype(BF16)
    side_main[128:144, :] = exf[3, pl.ds(0, 16, stride=8), :]

    for u in range(2):
        pre_s[u] = jnp.dot(gd[...], wbuf[u], preferred_element_type=F32)
    pre_copy = send(pre_s, pre_r, core_send.at[4], core_recv.at[4], partner)
    side_all = side_main[...]
    rho_slot = slot_order(jnp.broadcast_to(joined(side_all, 0), (ROWS, 128)))
    rho_s[...] = KAPPA * rho_slot
    gate_slot = slot_order(jnp.broadcast_to(joined(side_all, 3), (ROWS, 128)))
    pre_copy.wait_recv()
    hidden = []
    for u in range(2):
        both = slot_order(pre_s[u] + pre_r[1 - u])
        gate, up = both[:, 0:128], both[:, 128:256]
        hidden.append(gate / (1.0 + jnp.exp(-gate)) * up * gate_slot)
    hidden = jnp.concatenate(hidden, axis=1)
    hid[...] = hidden.astype(BF16)

    def tangents(vector, parts_out, own_out, g, d):
        part = pl.ds(pl.multiple_of(g * GROUP, GROUP), GROUP)
        rows = vector[:, :, part].reshape(256, GROUP)
        tangent = jnp.dot(hid[...], rows, preferred_element_type=F32)
        for i in range(4):
            t = 4 + i // 2
            full = tangent[:, i * 128 : (i + 1) * 128]
            half = tangent[(i % 2) * 72 : (i % 2) * 72 + 72, t * 128 : (t + 1) * 128]
            if d:
                parts_out[d - 1, i, 0:ROWS] = full.astype(BF16)
                parts_out[d - 1, i, ROWS:CHUNK] = half.astype(BF16)
            else:
                own_out[i, 0:ROWS] = full
                own_out[i, ROWS:CHUNK] = half

    def reduce_first(parts_out, landing, d, s_sem, r_sem):
        return {
            (o, d): send(
                parts_out.at[d - 1, (a2 + o) % 4], landing.at[d - 1, (a2 + o) % 4],
                s_sem.at[o, d - 1], r_sem.at[o, d - 1], plane((a1 + d) % 4, a2),
            )
            for o in OFFSETS + (0,)
        }

    def reduce_second(copies, own_out, landing, parts_two, landing_two, s_sem, r_sem):
        def reduced(i):
            return ((own_out[i] + landing[0, i].astype(F32)) + landing[1, i].astype(F32)) + landing[2, i].astype(F32)

        later = []
        for o in OFFSETS + (0,):
            for d in OFFSETS:
                copies[o, d].wait_recv()
            i = (a2 + o) % 4
            if o:
                parts_two[o - 1] = reduced(i).astype(BF16)
                later.append(
                    send(
                        parts_two.at[o - 1], landing_two.at[o - 1],
                        s_sem.at[4, o - 1], r_sem.at[4, o - 1], plane(a1, i),
                    )
                )
        return later, reduced(a2)

    rs1 = {}
    for d in OFFSETS:
        tangents(v1, tb, town, (a1 + d) % 4, d)
        rs1.update(reduce_first(tb, r1, d, rs_send, rs_recv))
    tangents(v1, tb, town, a1, 0)
    square = lax.dot_general(hid[...], hid[...], (((1,), (1,)), ((), ())), preferred_element_type=F32)
    corner = jnp.concatenate([square[128:ROWS, 128:ROWS], jnp.zeros((16, 112), F32)], axis=1)
    sq_own[...] = jnp.concatenate([square[:, 0:128], corner], axis=0)
    sq_out[0] = sq_own[...].astype(BF16)
    hid_t[...] = jnp.transpose(jnp.concatenate([hidden, jnp.zeros((112, 256), F32)], axis=0)).astype(BF16)
    for d in OFFSETS + (0,):
        tangents(v0, tb0, town0, (a1 + d) % 4, d)

    rs2, mine_sum = reduce_second(rs1, town, r1, p2s, r2, rs_send, rs_recv)
    for copy in rs2:
        copy.wait_recv()
    mine_sum = ((mine_sum + r2[0].astype(F32)) + r2[1].astype(F32)) + r2[2].astype(F32)
    held[...] = mine_sum

    zs[...] = mine_sum.astype(BF16)
    zp = send(zs, rz0, z_send.at[0], z_recv.at[0], (y, x, z - sg, c))
    rs3 = {}
    for d in OFFSETS:
        rs3.update(reduce_first(tb0, r10, d, rt_send, rt_recv))
    squares = [
        send(sq_out.at[0], sq_in.at[0, d - 1], sq_send.at[0, d - 1], sq_recv.at[0, d - 1], plane((a1 + d) % 4, a2))
        for d in OFFSETS
    ]
    zp.wait_recv()
    total = mine_sum + rz0[...].astype(F32)
    zes[...] = total.astype(BF16)
    zc = {
        k: send(zes, rz.at[k], z_send.at[1 + k], z_recv.at[1 + k], (y, x, (z + sg * (k + 1) + 8) % 8, c))
        for k in (2, 1, 0)
    }
    rs4, mine_other = reduce_second(rs3, town0, r10, p2s0, r20, rt_send, rt_recv)
    for copy in squares:
        copy.wait_recv()
    sq_sum = ((sq_own[...] + sq_in[0, 0].astype(F32)) + sq_in[0, 1].astype(F32)) + sq_in[0, 2].astype(F32)
    sq_out[1] = sq_sum.astype(BF16)
    squares_two = [
        send(sq_out.at[1], sq_in.at[1, d - 1], sq_send.at[1, d - 1], sq_recv.at[1, d - 1], plane(a1, (a2 + d) % 4))
        for d in OFFSETS
    ]
    resp_f, resp_h = total[0:ROWS], total[ROWS:CHUNK]
    for k in range(3):
        zc[k].wait_recv()
        resp_f = resp_f + jnp.dot(amat[k], rz[k, 0:ROWS, :], preferred_element_type=F32)
        resp_h = resp_h + jnp.dot(amat_h[k], rz[k, ROWS:CHUNK, :], preferred_element_type=F32)
    base = c * HALF + a1 * GROUP
    sig_f = sigma[:, pl.ds(pl.multiple_of(base + a2 * 128, 128), 128)]
    sig_h = sigma[:, pl.ds(pl.multiple_of(base + (4 + a2 // 2) * 128, 128), 128)]
    c4[m, 0:ROWS] = (rho_s[...] * sig_f * (resp_f * SCALE)).astype(BF16)
    c4[m, ROWS:CHUNK] = (rho_s[half_rows, :] * sig_h * (resp_h * SCALE)).astype(BF16)

    cg1 = along(c4, cg_send, cg_recv)
    cg2 = [spread(c4, m, 0, cg_send, cg_recv)]
    for d, copy in zip(OFFSETS, cg1):
        copy.wait_recv()
        cg2.append(spread(c4, behind(d), d, cg_send, cg_recv))

    def assemble(ref, g):
        for i in range(4):
            cg[:, i * 128 : (i + 1) * 128] = ref[g * 4 + i, 0:ROWS, :]
        for i in range(2):
            both = [ref[g * 4 + 2 * i + u, ROWS:CHUNK, :].astype(F32) for u in range(2)]
            cg[:, (4 + i) * 128 : (5 + i) * 128] = jnp.concatenate(both, axis=0).astype(BF16)

    for copy in rs4 + squares_two:
        copy.wait_recv()
    mine_other = ((mine_other + r20[0].astype(F32)) + r20[1].astype(F32)) + r20[2].astype(F32)
    sq_sum = ((sq_sum + sq_in[1, 0].astype(F32)) + sq_in[1, 1].astype(F32)) + sq_in[1, 2].astype(F32)
    sq_b = sq_sum.astype(BF16)
    cot = c4[m].astype(F32)
    line = lambda a: jnp.sum(a, axis=0, keepdims=True)
    both = [c4[a1 * 4 + (a2 // 2) * 2 + u, ROWS:CHUNK, :].astype(F32) for u in range(2)]
    tiles = jnp.concatenate([cot[0:ROWS], jnp.concatenate(both, axis=0)], axis=1)
    tiles_b = tiles.astype(BF16)
    mixed = jnp.dot(sq_b[0:ROWS], tiles_b[0:128], preferred_element_type=F32)
    mixed_low = jnp.dot(sq_b[ROWS:160, 0:16], tiles_b[128:ROWS], preferred_element_type=F32)
    quad = line(tiles[0:128] * mixed[0:128]) + line(tiles[128:ROWS] * (2.0 * mixed[128:ROWS] + mixed_low))
    lines = [
        line(cot * mine_other) * SCALE,
        line(cot * held[...]) * SCALE,
        (quad[:, 0:128] + 0.5 * quad[:, 128:256]) * (SCALE * SCALE),
    ] + [line(s[:, 0:128] + s[:, 128:256]) for s in (s00, s01, s11)]
    lines.append(jnp.zeros((2, 128), F32))
    red_s[0] = jnp.concatenate(lines, axis=0)
    ras = []
    for k in range(1, 16):
        o = (p + k) % 16
        ras.append(send(red_s.at[0], red_a.at[k - 1], ra_send.at[k - 1], ra_recv.at[k - 1], (o // 4, o % 4, z, c)))

    def rows_image(ref, u, g):
        assemble(ref, g)

        def image(k, carry):
            part = pl.ds(pl.multiple_of(g * GROUP + k * 256, 256), 256)
            cols_k = cg[:, pl.ds(pl.multiple_of(k * 256, 256), 256)]
            img[u, :, part] = jnp.dot(hid_t[0:128, 0:ROWS], cols_k, preferred_element_type=F32) * SCALE
            return carry

        lax.fori_loop(0, 3, image, 0)

    cxs = []
    rbs = []
    for n, d in enumerate((0,) + OFFSETS):
        if d:
            for copies in cg2:
                copies[n - 1].wait_recv()
        g = (a1 - d + 4) % 4
        block4 = pl.ds(pl.multiple_of(g * 4, 4), 4)
        cxs.append(send(c4.at[block4], cx.at[block4], cx_send.at[d], cx_recv.at[d], partner))
        if n == 3:
            acc = red_s[0]
            for k in range(15):
                ras[k].wait_recv()
                acc = acc + red_a[k]
            red_s[1] = acc
            for k in range(1, 16):
                o = (q + k) % 16
                rbs.append(
                    send(red_s.at[1], red_b.at[k - 1], rb_send.at[k - 1], rb_recv.at[k - 1], (y, x, o // 2, o % 2))
                )
        rows_image(c4, 0, g)

    for copy in cxs:
        copy.wait_recv()
    for g in range(4):
        rows_image(cx, 1, g)
    for k in range(15):
        rbs[k].wait_recv()
        acc = acc + red_b[k]
    scal = jnp.sum(acc, axis=1, keepdims=True) * (1.0 / ENTRIES)
    c0, c1, norm, g00, g01, g11 = [scal[k : k + 1, 0:1] for k in range(6)]
    norm = norm - 2.0 * (c0 * c0 + c1 * c1) + (c0 * c0 * g00 + 2.0 * (c0 * c1) * g01 + c1 * c1 * g11)
    beta = jnp.sqrt(norm)
    hess[...] = jnp.concatenate([c0, c1, beta], axis=1)
    inv = 1.0 / beta
    for u, (w0, w1, start) in enumerate(((v0.at[0], v1.at[0], c * HALF), (v0x, v1x, (1 - c) * HALF))):

        def finish(k, carry):
            part = pl.ds(pl.multiple_of(k * 256, 256), 256)
            resid = (img[u, :, part] - c0 * w0[:, part].astype(F32)) - c1 * w1[:, part].astype(F32)
            out[:, pl.ds(pl.multiple_of(start + k * 256, 256), 256)] = (resid * inv).astype(BF16)
            return carry

        lax.fori_loop(0, HALF // 256, finish, 0)

    for copy in first + core + second + [pre_copy] + list(rs1.values()) + rs2 + [zp] + list(zc.values()) + list(rs3.values()) + rs4 + squares + squares_two + cg1 + sum(cg2, []) + cxs + ras + rbs:
        copy.wait_send()


def body(tokens, w_gate, w_up, basis, routes, gates, rho, sigma):
    anywhere = pl.BlockSpec(memory_space=pl.ANY)
    vmem = pl.BlockSpec(memory_space=pltpu.VMEM)
    dma = pltpu.SemaphoreType.DMA
    scratch = [
        pltpu.VMEM((2, 256), jnp.int32),
        pltpu.VMEM((2, 256), F32),
        pltpu.VMEM((1, 16), F32),
        pltpu.VMEM((1, D), F32),
        pltpu.VMEM((256, 8), F32),
        pltpu.VMEM((16, HALF), BF16),
        pltpu.VMEM((2, HALF, 256), BF16),
        pltpu.VMEM((2, 128, HALF), BF16),
        pltpu.VMEM((2, 128, HALF), BF16),
        pltpu.VMEM((128, HALF), BF16),
        pltpu.VMEM((128, HALF), BF16),
        pltpu.VMEM((16, 8, MSG), BF16),
        pltpu.VMEM((ROWS, HALF), BF16),
        pltpu.VMEM((4, 128, 128), F32),
        pltpu.VMEM((8, 384), F32),
        pltpu.VMEM((ROWS, 128), F32),
        pltpu.VMEM((2, ROWS, 256), F32),
        pltpu.VMEM((2, ROWS, 256), F32),
        pltpu.VMEM((ROWS, 256), BF16),
        pltpu.VMEM((256, 256), BF16),
        pltpu.VMEM((3, 4, CHUNK, 128), BF16),
        pltpu.VMEM((3, 4, CHUNK, 128), BF16),
        pltpu.VMEM((4, CHUNK, 128), F32),
        pltpu.VMEM((3, CHUNK, 128), BF16),
        pltpu.VMEM((3, CHUNK, 128), BF16),
        pltpu.VMEM((3, 4, CHUNK, 128), BF16),
        pltpu.VMEM((3, 4, CHUNK, 128), BF16),
        pltpu.VMEM((4, CHUNK, 128), F32),
        pltpu.VMEM((3, CHUNK, 128), BF16),
        pltpu.VMEM((3, CHUNK, 128), BF16),
        pltpu.VMEM((CHUNK, 128), F32),
        pltpu.VMEM((160, 128), F32),
        pltpu.VMEM((2, 160, 128), BF16),
        pltpu.VMEM((2, 3, 160, 128), BF16),
        pltpu.VMEM((CHUNK, 128), BF16),
        pltpu.VMEM((CHUNK, 128), BF16),
        pltpu.VMEM((CHUNK, 128), BF16),
        pltpu.VMEM((3, CHUNK, 128), BF16),
        pltpu.VMEM((3, ROWS, ROWS), BF16),
        pltpu.VMEM((3, 72, 72), BF16),
        pltpu.VMEM((256, 256), F32),
        pltpu.VMEM((ROWS, 128), F32),
        pltpu.VMEM((16, CHUNK, 128), BF16),
        pltpu.VMEM((16, CHUNK, 128), BF16),
        pltpu.VMEM((ROWS, GROUP), BF16),
        pltpu.VMEM((2, 128, HALF), F32),
        pltpu.VMEM((15, 8, 128), F32),
        pltpu.VMEM((15, 8, 128), F32),
        pltpu.VMEM((2, 8, 128), F32),
        dma((11,)),
        dma((5,)), dma((5,)),
        dma((5, 3)), dma((5, 3)),
        dma((5, 3)), dma((5, 3)),
        dma((5, 3)), dma((5, 3)),
        dma((2, 3)), dma((2, 3)),
        dma((4,)), dma((4,)),
        dma((5, 3)), dma((5, 3)),
        dma((4,)), dma((4,)),
        dma((15,)), dma((15,)),
        dma((15,)), dma((15,)),
    ]
    operands = (tokens, w_gate, w_up, basis, routes.T, gates.T, rho.reshape(1, 16), sigma.reshape(1, D))
    operands = [pltpu.with_memory_space_constraint(a, pltpu.HBM) for a in operands]
    out, hess = pl.pallas_call(
        kernel,
        out_shape=(jax.ShapeDtypeStruct((128, D), BF16), jax.ShapeDtypeStruct((1, 3), F32)),
        in_specs=[anywhere] * 8,
        out_specs=(vmem, vmem),
        scratch_shapes=scratch,
        compiler_params=pltpu.CompilerParams(
            collective_id=0, has_side_effects=True, vmem_limit_bytes=32 * 1024 * 1024
        ),
        name="arnoldi",
    )(*operands)
    return out, hess.T


def solution(mesh):
    finer = Mesh(mesh.devices.reshape(4, 4, 8, 2), AXES)
    in_specs = (
        P(DP, None),
        P(None, EXPERT_DP),
        P(None, EXPERT_DP),
        P(None, EXPERT_DP, None),
        P(),
        P(),
        P(DP),
        P(),
    )
    out_specs = (P(EXPERT_DP, None), P())
    return jax.shard_map(body, mesh=finer, in_specs=in_specs, out_specs=out_specs, check_vma=False)
```

```python
import functools
import math

import jax
import jax.numpy as jnp
from jax import lax
from jax.experimental import pallas as pl
from jax.experimental.pallas import tpu as pltpu
from jax.sharding import Mesh
from jax.sharding import PartitionSpec as P

D = 6144
FF = 8192
E = 4
HALF = 3072
GROUP = 768
SIDE = 128
MSG = HALF + SIDE + 512
ROWS = 144
CHUNK = 216
DP = ("dp_0", "dp_1")
EXPERT = ("expert_0", "expert_1")
EXPERT_DP = ("expert_0", "expert_1", "dp_0", "dp_1")
AXES = ("dp_0", "dp_1", "expert_0", "expert_1")
MESH = pl.DeviceIdType.MESH
F32 = jnp.float32
BF16 = jnp.bfloat16
SCALE = 1.0 / math.sqrt(FF)
KAPPA = E * FF / 256
ENTRIES = float(E * FF * D)
OFFSETS = (1, 3, 2)


def iota(shape, dim):
    return lax.broadcasted_iota(jnp.int32, shape, dim)


def parts(col):
    hi = col.astype(BF16)
    left = col - hi.astype(F32)
    mid = left.astype(BF16)
    low = (left - mid.astype(F32)).astype(BF16)
    return hi.astype(F32), mid.astype(F32), low.astype(F32)


def joined(side, first):
    return (side[:, first : first + 1] + side[:, first + 1 : first + 2]) + side[:, first + 2 : first + 3]


def slot_order(m):
    return jnp.concatenate([m[0:64], m[128:136], m[64:128], m[136:144]], axis=0)


def kernel(
    tok_hbm, wg_hbm, wu_hbm, basis_hbm, routes_hbm, gates_hbm, rho_hbm, sigma_hbm,
    out, hess,
    routes, gates, rho, sigma, cols, tokv, wbuf, v0, v1, v0x, v1x, gm, gd, exf, exs, side_main, pre_s, pre_r, hid, hid_t,
    tb, r1, town, p2s, r2, tb0, r10, town0, held, sq_own, sq_out, sq_in, zs, rz0, zes, rz, amat, amat_h, rank_s, rho_s, c4, cx, cg, img,
    red_a, red_b, red_s,
    loc_sem, core_send, core_recv, ag_send, ag_recv, rs_send, rs_recv, rt_send, rt_recv, sq_send, sq_recv, z_send, z_recv,
    cg_send, cg_recv, cx_send, cx_recv, ra_send, ra_recv, rb_send, rb_recv,
):
    y, x, z, c = [lax.axis_index(name) for name in AXES]
    a1 = y * (1 - c) + x * c
    a2 = x * (1 - c) + y * c
    p = y * 4 + x
    q = z * 2 + c
    e = z // 2
    sg = 2 * (z % 2) - 1
    h = a2 % 2
    half_rows = pl.ds(pl.multiple_of(h * 72, 8), 72)

    def plane(b1, b2):
        return (b1 * (1 - c) + b2 * c, b2 * (1 - c) + b1 * c, z, c)

    def send(src, dst, s_sem, r_sem, device):
        copy = pltpu.make_async_remote_copy(
            src_ref=src, dst_ref=dst, send_sem=s_sem, recv_sem=r_sem, device_id=device, device_id_type=MESH
        )
        copy.start()
        return copy

    def local(src, dst, sem):
        copy = pltpu.make_async_copy(src, dst, sem)
        copy.start()
        return copy

    barrier = pltpu.get_barrier_semaphore()
    for k in range(1, 16):
        o = (p + k) % 16
        pl.semaphore_signal(barrier, inc=1, device_id=(o // 4, o % 4, z, c), device_id_type=MESH)
        o = (q + k) % 16
        pl.semaphore_signal(barrier, inc=1, device_id=(y, x, o // 2, o % 2), device_id_type=MESH)

    mine = pl.ds(pl.multiple_of(c * HALF, HALF), HALF)
    other = pl.ds(pl.multiple_of((1 - c) * HALF, HALF), HALF)
    small = [
        local(routes_hbm, routes, loc_sem.at[7]),
        local(gates_hbm, gates, loc_sem.at[8]),
        local(rho_hbm, rho, loc_sem.at[9]),
    ]
    loads = [
        local(tok_hbm.at[:, mine], tokv, loc_sem.at[0]),
        local(wg_hbm.at[mine, :], wbuf.at[0, :, pl.ds(0, 128)], loc_sem.at[1]),
        local(wu_hbm.at[mine, :], wbuf.at[0, :, pl.ds(128, 128)], loc_sem.at[2]),
        local(basis_hbm.at[1, :, mine], v1.at[0], loc_sem.at[3]),
        local(basis_hbm.at[0, :, mine], v0.at[0], loc_sem.at[4]),
        local(basis_hbm.at[1, :, other], v1x, loc_sem.at[5]),
        local(basis_hbm.at[0, :, other], v0x, loc_sem.at[6]),
        local(sigma_hbm, sigma, loc_sem.at[10]),
    ]
    for copy in small:
        copy.wait()

    cols[...] = jnp.transpose(
        jnp.concatenate([routes[...].astype(F32), gates[...], jnp.zeros((4, 256), F32)], axis=0)
    )
    own = cols[pl.ds(pl.multiple_of(p * 16, 16), 16), :]
    ef = e.astype(F32)
    hit0 = own[:, 0:1] == ef
    hit1 = own[:, 1:2] == ef
    member = hit0.astype(F32) + hit1.astype(F32)
    gate_tok = jnp.where(hit0, own[:, 2:3], 0.0) + jnp.where(hit1, own[:, 3:4], 0.0)
    tri = (iota((16, 16), 1) <= iota((16, 16), 0)).astype(F32).astype(BF16)
    member_b = jnp.broadcast_to(member, (16, 128))
    rank = jnp.dot(tri, member_b.astype(BF16), preferred_element_type=F32)
    lane = iota((16, 128), 1)
    place_t = jnp.where((rank - 1.0 == lane.astype(F32)) & (member_b > 0), 1.0, 0.0)
    place = jnp.transpose(place_t)[0:16, :].astype(BF16)
    diagonal = iota((16, 16), 0) == iota((16, 16), 1)
    rho_tok = jnp.sum(jnp.where(diagonal, jnp.broadcast_to(rho[...], (16, 16)), 0.0), axis=1, keepdims=True)
    r_hi, r_mid, r_low = parts(rho_tok)
    g_hi, g_mid, g_low = parts(gate_tok)
    side_in = jnp.zeros((16, 128), F32)
    for index, col in enumerate((r_hi, r_mid, r_low, g_hi, g_mid, g_low)):
        side_in = jnp.where(lane == index, col, side_in)
    side = jnp.dot(place, side_in.astype(BF16), preferred_element_type=F32)
    m = a1 * 4 + a2
    gm[m, :, HALF : HALF + SIDE] = side[0:8].astype(BF16)
    gm[m, :, HALF + SIDE + 384 : MSG] = jnp.broadcast_to(side[8:9], (8, 128)).astype(BF16)
    loads[0].wait()
    picked = jnp.dot(place, tokv[...], preferred_element_type=F32)
    gm[m, :, 0:HALF] = picked[0:8].astype(BF16)
    for r in range(8):
        exs[r : r + 1, :] = picked[8:9, r * 384 : (r + 1) * 384]
    gm[m, :, HALF + SIDE : HALF + SIDE + 384] = exs[...].astype(BF16)

    pl.semaphore_wait(barrier, 30)

    def spread(ref, lap, s_sem, r_sem):
        index = a1 * 4 + (a2 + 4 - lap) % 4
        return {
            (lap, d): send(
                ref.at[index], ref.at[index], s_sem.at[lap, d - 1], r_sem.at[lap, d - 1], plane((a1 + d) % 4, a2)
            )
            for d in OFFSETS
        }

    def pass_on(copies, ref, lap, s_sem, r_sem):
        d = 1 if lap in (0, 3) else 3
        copies[lap, d].wait_recv()
        index = ((a1 + 4 - d) % 4) * 4 + (a2 + 4 - lap) % 4
        copies[lap, 2] = send(
            ref.at[index], ref.at[index], s_sem.at[lap, 1], r_sem.at[lap, 1], plane((a1 + d) % 4, a2)
        )

    def along(ref, s_sem, r_sem):
        return [
            send(ref.at[m], ref.at[m], s_sem.at[4, d - 1], r_sem.at[4, d - 1], plane(a1, (a2 + d) % 4))
            for d in OFFSETS
        ]

    def relay(first, copies, ref, s_sem, r_sem):
        for d, copy in zip(OFFSETS, first):
            copy.wait_recv()
            copies.update(spread(ref, d, s_sem, r_sem))

    def finish_laps(copies, ref, s_sem, r_sem):
        for lap in OFFSETS:
            pass_on(copies, ref, lap, s_sem, r_sem)

    def landed(copies, d):
        for lap in range(4):
            copies[lap, d].wait_recv()

    first = along(gm, ag_send, ag_recv)
    second = spread(gm, 0, ag_send, ag_recv)
    partner = (y, x, z, 1 - c)
    core = [
        send(wg_hbm.at[other, :], wbuf.at[1, :, pl.ds(0, 128)], core_send.at[0], core_recv.at[0], partner),
        send(wu_hbm.at[other, :], wbuf.at[1, :, pl.ds(128, 128)], core_send.at[1], core_recv.at[1], partner),
        send(basis_hbm.at[1, :, other], v1.at[1], core_send.at[2], core_recv.at[2], partner),
        send(basis_hbm.at[0, :, other], v0.at[1], core_send.at[3], core_recv.at[3], partner),
    ]

    relay(first, second, gm, ag_send, ag_recv)

    for d in OFFSETS:
        landed(second, d)
    for copy in loads[1:]:
        copy.wait()
    for copy in core:
        copy.wait_recv()

    def source(o):
        return o * (1 - c) + ((o % 4) * 4 + o // 4) * c

    for k in range(8):
        pair = [gm[source(2 * k + u), :, 0:HALF].astype(F32) for u in range(2)]
        gd[16 * k : 16 * k + 16, :] = jnp.concatenate(pair, axis=0).astype(BF16)
    for o in range(16):
        block_o = gm[source(o)][:, HALF:MSG].astype(F32)
        side_main[8 * o : 8 * o + 8, :] = block_o[:, 0:SIDE]
        for t in range(4):
            exf[t, 8 * o : 8 * o + 8, :] = block_o[:, SIDE + t * 128 : SIDE + (t + 1) * 128]
    for r in range(8):
        for t in range(3):
            f = r * 384 + t * 128
            gd[128:144, f : f + 128] = exf[t, pl.ds(r, 16, stride=8), :].astype(BF16)
    side_main[128:144, :] = exf[3, pl.ds(0, 16, stride=8), :]

    for u in range(2):
        pre_s[u] = jnp.dot(gd[...], wbuf[u], preferred_element_type=F32)
    pre_copy = send(pre_s, pre_r, core_send.at[4], core_recv.at[4], partner)
    side_all = side_main[...]
    rho_slot = slot_order(jnp.broadcast_to(joined(side_all, 0), (ROWS, 128)))
    rho_s[...] = KAPPA * rho_slot
    gate_slot = slot_order(jnp.broadcast_to(joined(side_all, 3), (ROWS, 128)))
    pre_copy.wait_recv()
    hidden = []
    for u in range(2):
        both = slot_order(pre_s[u] + pre_r[1 - u])
        gate, up = both[:, 0:128], both[:, 128:256]
        hidden.append(gate / (1.0 + jnp.exp(-gate)) * up * gate_slot)
    hidden = jnp.concatenate(hidden, axis=1)
    hid[...] = hidden.astype(BF16)

    def tangents(vector, parts_out, own_out, g, d):
        part = pl.ds(pl.multiple_of(g * GROUP, GROUP), GROUP)
        rows = vector[:, :, part].reshape(256, GROUP)
        tangent = jnp.dot(hid[...], rows, preferred_element_type=F32)
        for i in range(4):
            t = 4 + i // 2
            full = tangent[:, i * 128 : (i + 1) * 128]
            half = tangent[(i % 2) * 72 : (i % 2) * 72 + 72, t * 128 : (t + 1) * 128]
            if d:
                parts_out[d - 1, i, 0:ROWS] = full.astype(BF16)
                parts_out[d - 1, i, ROWS:CHUNK] = half.astype(BF16)
            else:
                own_out[i, 0:ROWS] = full
                own_out[i, ROWS:CHUNK] = half

    def reduce_first(parts_out, landing, d, s_sem, r_sem):
        return {
            (o, d): send(
                parts_out.at[d - 1, (a2 + o) % 4], landing.at[d - 1, (a2 + o) % 4],
                s_sem.at[o, d - 1], r_sem.at[o, d - 1], plane((a1 + d) % 4, a2),
            )
            for o in OFFSETS + (0,)
        }

    def reduce_second(copies, own_out, landing, parts_two, landing_two, s_sem, r_sem):
        def reduced(i):
            return ((own_out[i] + landing[0, i].astype(F32)) + landing[1, i].astype(F32)) + landing[2, i].astype(F32)

        later = []
        for o in OFFSETS + (0,):
            for d in OFFSETS:
                copies[o, d].wait_recv()
            i = (a2 + o) % 4
            if o:
                parts_two[o - 1] = reduced(i).astype(BF16)
                later.append(
                    send(
                        parts_two.at[o - 1], landing_two.at[o - 1],
                        s_sem.at[4, o - 1], r_sem.at[4, o - 1], plane(a1, i),
                    )
                )
        return later, reduced(a2)

    rs1 = {}
    for d in OFFSETS:
        tangents(v1, tb, town, (a1 + d) % 4, d)
        rs1.update(reduce_first(tb, r1, d, rs_send, rs_recv))
    tangents(v1, tb, town, a1, 0)
    square = lax.dot_general(hid[...], hid[...], (((1,), (1,)), ((), ())), preferred_element_type=F32)
    corner = jnp.concatenate([square[128:ROWS, 128:ROWS], jnp.zeros((16, 112), F32)], axis=1)
    sq_own[...] = jnp.concatenate([square[:, 0:128], corner], axis=0)
    sq_out[...] = sq_own[...].astype(BF16)
    hid_t[...] = jnp.transpose(jnp.concatenate([hidden, jnp.zeros((112, 256), F32)], axis=0)).astype(BF16)
    for d in (1, 3):
        tangents(v0, tb0, town0, (a1 + d) % 4, d)

    rs2, mine_sum = reduce_second(rs1, town, r1, p2s, r2, rs_send, rs_recv)
    for copy in rs2:
        copy.wait_recv()
    mine_sum = ((mine_sum + r2[0].astype(F32)) + r2[1].astype(F32)) + r2[2].astype(F32)
    held[...] = mine_sum

    zs[...] = mine_sum.astype(BF16)
    zp = send(zs, rz0, z_send.at[0], z_recv.at[0], (y, x, z - sg, c))
    rs3 = {}
    for d in OFFSETS:
        if d == 2:
            tangents(v0, tb0, town0, (a1 + d) % 4, d)
        rs3.update(reduce_first(tb0, r10, d, rt_send, rt_recv))
    squares = [
        send(sq_out, sq_in.at[d - 1], sq_send.at[d - 1], sq_recv.at[d - 1], plane((a1 + d) % 4, a2))
        for d in OFFSETS
    ]
    zp.wait_recv()
    total = mine_sum + rz0[...].astype(F32)
    zes[...] = total.astype(BF16)
    zc = {
        k: send(zes, rz.at[k], z_send.at[1 + k], z_recv.at[1 + k], (y, x, (z + sg * (k + 1) + 8) % 8, c))
        for k in (2, 1, 0)
    }

    t_lane = iota((256, 128), 1)
    shift = jnp.where(t_lane == 1, sg, 0) + jnp.where(t_lane == 2, -sg, 0) + jnp.where(t_lane == 3, 2, 0)
    names = jnp.where(t_lane < 4, (e + shift + 4) & 3, -1)
    names = names.astype(F32)
    member4 = (cols[:, 0:1] == names).astype(F32) + (cols[:, 1:2] == names).astype(F32)
    low = iota((256, 256), 0)
    col = iota((256, 256), 1)
    tri_b = ((col <= low) & ((col >> 4) == (low >> 4))).astype(F32).astype(BF16)
    rank4 = jnp.dot(tri_b, member4.astype(BF16), preferred_element_type=F32)
    token = iota((256, 128), 0)
    block = token >> 4
    slot = rank4.astype(jnp.int32) - 1
    where_to = (block >> 3) * 72 + jnp.where(slot < 8, (block & 7) * 8 + slot, 64 + (block & 7))
    where_to = jnp.where(member4 > 0, where_to, -1000)
    onehot = (where_to[:, 0:1] == col).astype(F32)
    rank_s[...] = jnp.transpose(onehot)
    own_full = rank_s[0:ROWS, :].astype(BF16)
    own_half = rank_s[half_rows, :].astype(BF16)
    for k in range(3):
        theirs = (where_to[:, k + 1 : k + 2] == col).astype(F32).astype(BF16)
        amat[k] = jnp.dot(own_full, theirs, preferred_element_type=F32)[:, 0:ROWS].astype(BF16)
        theirs = (where_to[:, k + 1 : k + 2] - h * 72 == col).astype(F32).astype(BF16)
        amat_h[k] = jnp.dot(own_half, theirs, preferred_element_type=F32)[:, 0:72].astype(BF16)

    tangents(v0, tb0, town0, a1, 0)
    def gram(k, sums):
        s00, s01, s11 = sums
        part = pl.ds(pl.multiple_of(k * 256, 256), 256)
        for u in range(2):
            b0 = v0[u, :, part].astype(F32)
            b1 = v1[u, :, part].astype(F32)
            fold = lambda a: jnp.sum(a.reshape(16, 8, 256), axis=0)
            s00 = s00 + fold(b0 * b0)
            s01 = s01 + fold(b0 * b1)
            s11 = s11 + fold(b1 * b1)
        return s00, s01, s11

    zero = jnp.zeros((8, 256), F32)
    s00, s01, s11 = lax.fori_loop(0, HALF // 256, gram, (zero, zero, zero))

    resp_f, resp_h = total[0:ROWS], total[ROWS:CHUNK]
    for k in range(3):
        zc[k].wait_recv()
        resp_f = resp_f + jnp.dot(amat[k], rz[k, 0:ROWS, :], preferred_element_type=F32)
        resp_h = resp_h + jnp.dot(amat_h[k], rz[k, ROWS:CHUNK, :], preferred_element_type=F32)
    base = c * HALF + a1 * GROUP
    sig_f = sigma[:, pl.ds(pl.multiple_of(base + a2 * 128, 128), 128)]
    sig_h = sigma[:, pl.ds(pl.multiple_of(base + (4 + a2 // 2) * 128, 128), 128)]
    c4[m, 0:ROWS] = (rho_s[...] * sig_f * (resp_f * SCALE)).astype(BF16)
    c4[m, ROWS:CHUNK] = (rho_s[half_rows, :] * sig_h * (resp_h * SCALE)).astype(BF16)

    cg1 = along(c4, cg_send, cg_recv)
    cg2 = spread(c4, 0, cg_send, cg_recv)
    relay(cg1, cg2, c4, cg_send, cg_recv)

    def assemble(ref, g):
        for i in range(4):
            cg[:, i * 128 : (i + 1) * 128] = ref[g * 4 + i, 0:ROWS, :]
        for i in range(2):
            both = [ref[g * 4 + 2 * i + u, ROWS:CHUNK, :].astype(F32) for u in range(2)]
            cg[:, (4 + i) * 128 : (5 + i) * 128] = jnp.concatenate(both, axis=0).astype(BF16)

    for copy in list(rs3.values()) + squares:
        copy.wait_recv()
    line = lambda a: jnp.sum(a, axis=0, keepdims=True)
    dot0 = jnp.zeros((1, 128), F32)
    for i in range(4):
        partial = ((town0[i] + r10[0, i].astype(F32)) + r10[1, i].astype(F32)) + r10[2, i].astype(F32)
        dot0 = dot0 + line(c4[a1 * 4 + i].astype(F32) * partial)
    square = ((sq_own[...] + sq_in[0].astype(F32)) + sq_in[1].astype(F32)) + sq_in[2].astype(F32)
    sq_b = square.astype(BF16)
    assemble(c4, a1)
    mixed = jnp.dot(sq_b[0:ROWS], cg[0:128, :], preferred_element_type=F32)
    mixed_low = jnp.dot(sq_b[ROWS:160, 0:16], cg[128:ROWS, :], preferred_element_type=F32)
    quad = line(cg[0:128, :].astype(F32) * mixed[0:128])
    quad = quad + line(cg[128:ROWS, :].astype(F32) * (2.0 * mixed[128:ROWS] + mixed_low))
    quad = sum(quad[:, i * 128 : (i + 1) * 128] for i in range(6))
    lines = [
        dot0 * SCALE,
        line(c4[m].astype(F32) * held[...]) * SCALE,
        quad * (SCALE * SCALE),
    ] + [line(s[:, 0:128] + s[:, 128:256]) for s in (s00, s01, s11)]
    lines.append(jnp.zeros((2, 128), F32))
    red_s[0] = jnp.concatenate(lines, axis=0)
    ras = []
    for k in range(1, 16):
        o = (q + k) % 16
        ras.append(send(red_s.at[0], red_a.at[k - 1], ra_send.at[k - 1], ra_recv.at[k - 1], (y, x, o // 2, o % 2)))

    def rows_image(ref, u, g):
        assemble(ref, g)

        part = pl.ds(pl.multiple_of(g * GROUP, GROUP), GROUP)
        img[u, :, part] = jnp.dot(hid_t[0:128, 0:ROWS], cg[...], preferred_element_type=F32) * SCALE

    cxs = []
    rbs = []
    for n, d in enumerate((0,) + OFFSETS):
        if d:
            landed(cg2, d)
        g = (a1 - d + 4) % 4
        block4 = pl.ds(pl.multiple_of(g * 4, 4), 4)
        cxs.append(send(c4.at[block4], cx.at[block4], cx_send.at[d], cx_recv.at[d], partner))
        if n == 3:
            acc = red_s[0]
            for k in range(15):
                ras[k].wait_recv()
                acc = acc + red_a[k]
            red_s[1] = acc
            for k in range(1, 16):
                o = (p + k) % 16
                rbs.append(
                    send(red_s.at[1], red_b.at[k - 1], rb_send.at[k - 1], rb_recv.at[k - 1], (o // 4, o % 4, z, c))
                )
        rows_image(c4, 0, g)
        if n:
            cxs[n - 1].wait_recv()
            rows_image(cx, 1, (a2 - ((0,) + OFFSETS)[n - 1] + 4) % 4)

    cxs[3].wait_recv()
    rows_image(cx, 1, (a2 - 2 + 4) % 4)
    for k in range(15):
        rbs[k].wait_recv()
        acc = acc + red_b[k]
    scal = jnp.sum(acc, axis=1, keepdims=True) * (1.0 / ENTRIES)
    c0, c1, norm, g00, g01, g11 = [scal[k : k + 1, 0:1] for k in range(6)]
    norm = norm - 2.0 * (c0 * c0 + c1 * c1) + (c0 * c0 * g00 + 2.0 * (c0 * c1) * g01 + c1 * c1 * g11)
    beta = jnp.sqrt(norm)
    hess[...] = jnp.concatenate([c0, c1, beta], axis=1)
    inv = 1.0 / beta
    for u, (w0, w1, start) in enumerate(((v0.at[0], v1.at[0], c * HALF), (v0x, v1x, (1 - c) * HALF))):

        def finish(k, carry):
            part = pl.ds(pl.multiple_of(k * 256, 256), 256)
            resid = (img[u, :, part] - c0 * w0[:, part].astype(F32)) - c1 * w1[:, part].astype(F32)
            out[:, pl.ds(pl.multiple_of(start + k * 256, 256), 256)] = (resid * inv).astype(BF16)
            return carry

        lax.fori_loop(0, HALF // 256, finish, 0)

    for copy in first + core + list(second.values()) + [pre_copy] + list(rs1.values()) + rs2 + [zp] + list(zc.values()) + list(rs3.values()) + squares + cg1 + list(cg2.values()) + cxs + ras + rbs:
        copy.wait_send()


def body(tokens, w_gate, w_up, basis, routes, gates, rho, sigma):
    anywhere = pl.BlockSpec(memory_space=pl.ANY)
    vmem = pl.BlockSpec(memory_space=pltpu.VMEM)
    dma = pltpu.SemaphoreType.DMA
    scratch = [
        pltpu.VMEM((2, 256), jnp.int32),
        pltpu.VMEM((2, 256), F32),
        pltpu.VMEM((1, 16), F32),
        pltpu.VMEM((1, D), F32),
        pltpu.VMEM((256, 8), F32),
        pltpu.VMEM((16, HALF), BF16),
        pltpu.VMEM((2, HALF, 256), BF16),
        pltpu.VMEM((2, 128, HALF), BF16),
        pltpu.VMEM((2, 128, HALF), BF16),
        pltpu.VMEM((128, HALF), BF16),
        pltpu.VMEM((128, HALF), BF16),
        pltpu.VMEM((16, 8, MSG), BF16),
        pltpu.VMEM((ROWS, HALF), BF16),
        pltpu.VMEM((4, 128, 128), F32),
        pltpu.VMEM((8, 384), F32),
        pltpu.VMEM((ROWS, 128), F32),
        pltpu.VMEM((2, ROWS, 256), F32),
        pltpu.VMEM((2, ROWS, 256), F32),
        pltpu.VMEM((ROWS, 256), BF16),
        pltpu.VMEM((256, 256), BF16),
        pltpu.VMEM((3, 4, CHUNK, 128), BF16),
        pltpu.VMEM((3, 4, CHUNK, 128), BF16),
        pltpu.VMEM((4, CHUNK, 128), F32),
        pltpu.VMEM((3, CHUNK, 128), BF16),
        pltpu.VMEM((3, CHUNK, 128), BF16),
        pltpu.VMEM((3, 4, CHUNK, 128), BF16),
        pltpu.VMEM((3, 4, CHUNK, 128), BF16),
        pltpu.VMEM((4, CHUNK, 128), F32),
        pltpu.VMEM((CHUNK, 128), F32),
        pltpu.VMEM((160, 128), F32),
        pltpu.VMEM((160, 128), BF16),
        pltpu.VMEM((3, 160, 128), BF16),
        pltpu.VMEM((CHUNK, 128), BF16),
        pltpu.VMEM((CHUNK, 128), BF16),
        pltpu.VMEM((CHUNK, 128), BF16),
        pltpu.VMEM((3, CHUNK, 128), BF16),
        pltpu.VMEM((3, ROWS, ROWS), BF16),
        pltpu.VMEM((3, 72, 72), BF16),
        pltpu.VMEM((256, 256), F32),
        pltpu.VMEM((ROWS, 128), F32),
        pltpu.VMEM((16, CHUNK, 128), BF16),
        pltpu.VMEM((16, CHUNK, 128), BF16),
        pltpu.VMEM((ROWS, GROUP), BF16),
        pltpu.VMEM((2, 128, HALF), F32),
        pltpu.VMEM((15, 8, 128), F32),
        pltpu.VMEM((15, 8, 128), F32),
        pltpu.VMEM((2, 8, 128), F32),
        dma((11,)),
        dma((5,)), dma((5,)),
        dma((5, 3)), dma((5, 3)),
        dma((5, 3)), dma((5, 3)),
        dma((4, 3)), dma((4, 3)),
        dma((3,)), dma((3,)),
        dma((4,)), dma((4,)),
        dma((5, 3)), dma((5, 3)),
        dma((4,)), dma((4,)),
        dma((15,)), dma((15,)),
        dma((15,)), dma((15,)),
    ]
    operands = (tokens, w_gate, w_up, basis, routes.T, gates.T, rho.reshape(1, 16), sigma.reshape(1, D))
    operands = [pltpu.with_memory_space_constraint(a, pltpu.HBM) for a in operands]
    out, hess = pl.pallas_call(
        kernel,
        out_shape=(jax.ShapeDtypeStruct((128, D), BF16), jax.ShapeDtypeStruct((1, 3), F32)),
        in_specs=[anywhere] * 8,
        out_specs=(vmem, vmem),
        scratch_shapes=scratch,
        compiler_params=pltpu.CompilerParams(
            collective_id=0, has_side_effects=True, vmem_limit_bytes=32 * 1024 * 1024
        ),
        name="arnoldi",
    )(*operands)
    return out, hess.T


def solution(mesh):
    finer = Mesh(mesh.devices.reshape(4, 4, 8, 2), AXES)
    in_specs = (
        P(DP, None),
        P(None, EXPERT_DP),
        P(None, EXPERT_DP),
        P(None, EXPERT_DP, None),
        P(),
        P(),
        P(DP),
        P(),
    )
    out_specs = (P(EXPERT_DP, None), P())
    return jax.shard_map(body, mesh=finer, in_specs=in_specs, out_specs=out_specs, check_vma=False)
```

```python
import functools
import math

import jax
import jax.numpy as jnp
from jax import lax
from jax.experimental import pallas as pl
from jax.experimental.pallas import tpu as pltpu
from jax.sharding import Mesh
from jax.sharding import PartitionSpec as P

D = 6144
FF = 8192
E = 4
HALF = 3072
GROUP = 768
SIDE = 128
MSG = HALF + SIDE + 512
ROWS = 144
CHUNK = 216
DP = ("dp_0", "dp_1")
EXPERT = ("expert_0", "expert_1")
EXPERT_DP = ("expert_0", "expert_1", "dp_0", "dp_1")
AXES = ("dp_0", "dp_1", "expert_0", "expert_1")
MESH = pl.DeviceIdType.MESH
F32 = jnp.float32
BF16 = jnp.bfloat16
SCALE = 1.0 / math.sqrt(FF)
KAPPA = E * FF / 256
ENTRIES = float(E * FF * D)
OFFSETS = (1, 3, 2)


def iota(shape, dim):
    return lax.broadcasted_iota(jnp.int32, shape, dim)


def parts(col):
    hi = col.astype(BF16)
    left = col - hi.astype(F32)
    mid = left.astype(BF16)
    low = (left - mid.astype(F32)).astype(BF16)
    return hi.astype(F32), mid.astype(F32), low.astype(F32)


def joined(side, first):
    return (side[:, first : first + 1] + side[:, first + 1 : first + 2]) + side[:, first + 2 : first + 3]


def slot_order(m):
    return jnp.concatenate([m[0:64], m[128:136], m[64:128], m[136:144]], axis=0)


def kernel(
    tok_hbm, wg_hbm, wu_hbm, basis_hbm, routes_hbm, gates_hbm, rho_hbm, sigma_hbm,
    out, hess,
    routes, gates, rho, sigma, cols, tokv, wbuf, v0, v1, v0x, v1x, gm, gd, exf, exs, side_main, pre_s, pre_r, hid, hid_t,
    tb, r1, town, p2s, r2, tb0, r10, town0, held, sq_own, sq_out, sq_in, zs, rz0, zes, rz, amat, amat_h, rank_s, rho_s, c4, cx, cg, img,
    red_a, red_b, red_s,
    loc_sem, core_send, core_recv, ag_send, ag_recv, rs_send, rs_recv, rt_send, rt_recv, sq_send, sq_recv, z_send, z_recv,
    cg_send, cg_recv, cx_send, cx_recv, ra_send, ra_recv, rb_send, rb_recv,
):
    y, x, z, c = [lax.axis_index(name) for name in AXES]
    a1 = y * (1 - c) + x * c
    a2 = x * (1 - c) + y * c
    p = y * 4 + x
    q = z * 2 + c
    e = z // 2
    sg = 2 * (z % 2) - 1
    h = a2 % 2
    half_rows = pl.ds(pl.multiple_of(h * 72, 8), 72)

    def plane(b1, b2):
        return (b1 * (1 - c) + b2 * c, b2 * (1 - c) + b1 * c, z, c)

    def send(src, dst, s_sem, r_sem, device):
        copy = pltpu.make_async_remote_copy(
            src_ref=src, dst_ref=dst, send_sem=s_sem, recv_sem=r_sem, device_id=device, device_id_type=MESH
        )
        copy.start()
        return copy

    def local(src, dst, sem):
        copy = pltpu.make_async_copy(src, dst, sem)
        copy.start()
        return copy

    barrier = pltpu.get_barrier_semaphore()
    greeted = [(y, x, z, 1 - c)]
    greeted += [((y + d) % 4, x, z, c) for d in OFFSETS] + [(y, (x + d) % 4, z, c) for d in OFFSETS]
    greeted += [(y, x, (z + sg * d + 8) % 8, c) for d in (-1, 1, -2, 3)]
    for device in greeted:
        pl.semaphore_signal(barrier, inc=1, device_id=device, device_id_type=MESH)

    mine = pl.ds(pl.multiple_of(c * HALF, HALF), HALF)
    other = pl.ds(pl.multiple_of((1 - c) * HALF, HALF), HALF)
    small = [
        local(routes_hbm, routes, loc_sem.at[7]),
        local(gates_hbm, gates, loc_sem.at[8]),
        local(rho_hbm, rho, loc_sem.at[9]),
    ]
    loads = [
        local(tok_hbm.at[:, mine], tokv, loc_sem.at[0]),
        local(wg_hbm.at[mine, :], wbuf.at[0, :, pl.ds(0, 128)], loc_sem.at[1]),
        local(wu_hbm.at[mine, :], wbuf.at[0, :, pl.ds(128, 128)], loc_sem.at[2]),
        local(basis_hbm.at[1, :, mine], v1.at[0], loc_sem.at[3]),
        local(basis_hbm.at[0, :, mine], v0.at[0], loc_sem.at[4]),
        local(basis_hbm.at[1, :, other], v1x, loc_sem.at[5]),
        local(basis_hbm.at[0, :, other], v0x, loc_sem.at[6]),
        local(sigma_hbm, sigma, loc_sem.at[10]),
    ]
    for copy in small:
        copy.wait()

    cols[...] = jnp.transpose(
        jnp.concatenate([routes[...].astype(F32), gates[...], jnp.zeros((4, 256), F32)], axis=0)
    )
    own = cols[pl.ds(pl.multiple_of(p * 16, 16), 16), :]
    ef = e.astype(F32)
    hit0 = own[:, 0:1] == ef
    hit1 = own[:, 1:2] == ef
    member = hit0.astype(F32) + hit1.astype(F32)
    gate_tok = jnp.where(hit0, own[:, 2:3], 0.0) + jnp.where(hit1, own[:, 3:4], 0.0)
    tri = (iota((16, 16), 1) <= iota((16, 16), 0)).astype(F32).astype(BF16)
    member_b = jnp.broadcast_to(member, (16, 128))
    rank = jnp.dot(tri, member_b.astype(BF16), preferred_element_type=F32)
    lane = iota((16, 128), 1)
    place_t = jnp.where((rank - 1.0 == lane.astype(F32)) & (member_b > 0), 1.0, 0.0)
    place = jnp.transpose(place_t)[0:16, :].astype(BF16)
    diagonal = iota((16, 16), 0) == iota((16, 16), 1)
    rho_tok = jnp.sum(jnp.where(diagonal, jnp.broadcast_to(rho[...], (16, 16)), 0.0), axis=1, keepdims=True)
    r_hi, r_mid, r_low = parts(rho_tok)
    g_hi, g_mid, g_low = parts(gate_tok)
    side_in = jnp.zeros((16, 128), F32)
    for index, col in enumerate((r_hi, r_mid, r_low, g_hi, g_mid, g_low)):
        side_in = jnp.where(lane == index, col, side_in)
    side = jnp.dot(place, side_in.astype(BF16), preferred_element_type=F32)
    m = a1 * 4 + a2
    gm[m, :, HALF : HALF + SIDE] = side[0:8].astype(BF16)
    gm[m, :, HALF + SIDE + 384 : MSG] = jnp.broadcast_to(side[8:9], (8, 128)).astype(BF16)
    loads[0].wait()
    picked = jnp.dot(place, tokv[...], preferred_element_type=F32)
    gm[m, :, 0:HALF] = picked[0:8].astype(BF16)
    for r in range(8):
        exs[r : r + 1, :] = picked[8:9, r * 384 : (r + 1) * 384]
    gm[m, :, HALF + SIDE : HALF + SIDE + 384] = exs[...].astype(BF16)

    pl.semaphore_wait(barrier, 11)

    def spread(ref, lap, s_sem, r_sem):
        index = a1 * 4 + (a2 + 4 - lap) % 4
        return {
            (lap, d): send(
                ref.at[index], ref.at[index], s_sem.at[lap, d - 1], r_sem.at[lap, d - 1], plane((a1 + d) % 4, a2)
            )
            for d in OFFSETS
        }

    def pass_on(copies, ref, lap, s_sem, r_sem):
        d = 1 if lap in (0, 3) else 3
        copies[lap, d].wait_recv()
        index = ((a1 + 4 - d) % 4) * 4 + (a2 + 4 - lap) % 4
        copies[lap, 2] = send(
            ref.at[index], ref.at[index], s_sem.at[lap, 1], r_sem.at[lap, 1], plane((a1 + d) % 4, a2)
        )

    def along(ref, s_sem, r_sem):
        return [
            send(ref.at[m], ref.at[m], s_sem.at[4, d - 1], r_sem.at[4, d - 1], plane(a1, (a2 + d) % 4))
            for d in OFFSETS
        ]

    def relay(first, copies, ref, s_sem, r_sem):
        for d, copy in zip(OFFSETS, first):
            copy.wait_recv()
            copies.update(spread(ref, d, s_sem, r_sem))

    def finish_laps(copies, ref, s_sem, r_sem):
        for lap in OFFSETS:
            pass_on(copies, ref, lap, s_sem, r_sem)

    def landed(copies, d):
        for lap in range(4):
            copies[lap, d].wait_recv()

    first = along(gm, ag_send, ag_recv)
    second = spread(gm, 0, ag_send, ag_recv)
    partner = (y, x, z, 1 - c)
    core = [
        send(wg_hbm.at[other, :], wbuf.at[1, :, pl.ds(0, 128)], core_send.at[0], core_recv.at[0], partner),
        send(wu_hbm.at[other, :], wbuf.at[1, :, pl.ds(128, 128)], core_send.at[1], core_recv.at[1], partner),
        send(basis_hbm.at[1, :, other], v1.at[1], core_send.at[2], core_recv.at[2], partner),
        send(basis_hbm.at[0, :, other], v0.at[1], core_send.at[3], core_recv.at[3], partner),
    ]

    relay(first, second, gm, ag_send, ag_recv)

    for d in OFFSETS:
        landed(second, d)
    for copy in loads[1:]:
        copy.wait()
    for copy in core:
        copy.wait_recv()

    def source(o):
        return o * (1 - c) + ((o % 4) * 4 + o // 4) * c

    for k in range(8):
        pair = [gm[source(2 * k + u), :, 0:HALF].astype(F32) for u in range(2)]
        gd[16 * k : 16 * k + 16, :] = jnp.concatenate(pair, axis=0).astype(BF16)
    for o in range(16):
        block_o = gm[source(o)][:, HALF:MSG].astype(F32)
        side_main[8 * o : 8 * o + 8, :] = block_o[:, 0:SIDE]
        for t in range(4):
            exf[t, 8 * o : 8 * o + 8, :] = block_o[:, SIDE + t * 128 : SIDE + (t + 1) * 128]
    for r in range(8):
        for t in range(3):
            f = r * 384 + t * 128
            gd[128:144, f : f + 128] = exf[t, pl.ds(r, 16, stride=8), :].astype(BF16)
    side_main[128:144, :] = exf[3, pl.ds(0, 16, stride=8), :]

    for u in range(2):
        pre_s[u] = jnp.dot(gd[...], wbuf[u], preferred_element_type=F32)
    pre_copy = send(pre_s, pre_r, core_send.at[4], core_recv.at[4], partner)
    side_all = side_main[...]
    rho_slot = slot_order(jnp.broadcast_to(joined(side_all, 0), (ROWS, 128)))
    rho_s[...] = KAPPA * rho_slot
    gate_slot = slot_order(jnp.broadcast_to(joined(side_all, 3), (ROWS, 128)))
    pre_copy.wait_recv()
    hidden = []
    for u in range(2):
        both = slot_order(pre_s[u] + pre_r[1 - u])
        gate, up = both[:, 0:128], both[:, 128:256]
        hidden.append(gate / (1.0 + jnp.exp(-gate)) * up * gate_slot)
    hidden = jnp.concatenate(hidden, axis=1)
    hid[...] = hidden.astype(BF16)

    def tangents(vector, parts_out, own_out, g, d):
        part = pl.ds(pl.multiple_of(g * GROUP, GROUP), GROUP)
        rows = vector[:, :, part].reshape(256, GROUP)
        tangent = jnp.dot(hid[...], rows, preferred_element_type=F32)
        for i in range(4):
            t = 4 + i // 2
            full = tangent[:, i * 128 : (i + 1) * 128]
            half = tangent[(i % 2) * 72 : (i % 2) * 72 + 72, t * 128 : (t + 1) * 128]
            if d:
                parts_out[d - 1, i, 0:ROWS] = full.astype(BF16)
                parts_out[d - 1, i, ROWS:CHUNK] = half.astype(BF16)
            else:
                own_out[i, 0:ROWS] = full
                own_out[i, ROWS:CHUNK] = half

    def reduce_first(parts_out, landing, d, s_sem, r_sem):
        return {
            (o, d): send(
                parts_out.at[d - 1, (a2 + o) % 4], landing.at[d - 1, (a2 + o) % 4],
                s_sem.at[o, d - 1], r_sem.at[o, d - 1], plane((a1 + d) % 4, a2),
            )
            for o in OFFSETS + (0,)
        }

    def reduce_second(copies, own_out, landing, parts_two, landing_two, s_sem, r_sem):
        def reduced(i):
            return ((own_out[i] + landing[0, i].astype(F32)) + landing[1, i].astype(F32)) + landing[2, i].astype(F32)

        later = []
        for o in OFFSETS + (0,):
            for d in OFFSETS:
                copies[o, d].wait_recv()
            i = (a2 + o) % 4
            if o:
                parts_two[o - 1] = reduced(i).astype(BF16)
                later.append(
                    send(
                        parts_two.at[o - 1], landing_two.at[o - 1],
                        s_sem.at[4, o - 1], r_sem.at[4, o - 1], plane(a1, i),
                    )
                )
        return later, reduced(a2)

    rs1 = {}
    for d in OFFSETS:
        tangents(v1, tb, town, (a1 + d) % 4, d)
        rs1.update(reduce_first(tb, r1, d, rs_send, rs_recv))
    tangents(v1, tb, town, a1, 0)
    square = lax.dot_general(hid[...], hid[...], (((1,), (1,)), ((), ())), preferred_element_type=F32)
    corner = jnp.concatenate([square[128:ROWS, 128:ROWS], jnp.zeros((16, 112), F32)], axis=1)
    sq_own[...] = jnp.concatenate([square[:, 0:128], corner], axis=0)
    sq_out[...] = sq_own[...].astype(BF16)
    hid_t[...] = jnp.transpose(jnp.concatenate([hidden, jnp.zeros((112, 256), F32)], axis=0)).astype(BF16)
    for d in (1, 3):
        tangents(v0, tb0, town0, (a1 + d) % 4, d)

    rs2, mine_sum = reduce_second(rs1, town, r1, p2s, r2, rs_send, rs_recv)
    for copy in rs2:
        copy.wait_recv()
    mine_sum = ((mine_sum + r2[0].astype(F32)) + r2[1].astype(F32)) + r2[2].astype(F32)
    held[...] = mine_sum

    zs[...] = mine_sum.astype(BF16)
    zp = send(zs, rz0, z_send.at[0], z_recv.at[0], (y, x, z - sg, c))
    rs3 = {}
    for d in OFFSETS:
        if d == 2:
            tangents(v0, tb0, town0, (a1 + d) % 4, d)
        rs3.update(reduce_first(tb0, r10, d, rt_send, rt_recv))
    squares = [
        send(sq_out, sq_in.at[d - 1], sq_send.at[d - 1], sq_recv.at[d - 1], plane((a1 + d) % 4, a2))
        for d in OFFSETS
    ]
    zp.wait_recv()
    total = mine_sum + rz0[...].astype(F32)
    zes[...] = total.astype(BF16)
    zc = {
        k: send(zes, rz.at[k], z_send.at[1 + k], z_recv.at[1 + k], (y, x, (z + sg * (k + 1) + 8) % 8, c))
        for k in (2, 1, 0)
    }

    t_lane = iota((256, 128), 1)
    shift = jnp.where(t_lane == 1, sg, 0) + jnp.where(t_lane == 2, -sg, 0) + jnp.where(t_lane == 3, 2, 0)
    names = jnp.where(t_lane < 4, (e + shift + 4) & 3, -1)
    names = names.astype(F32)
    member4 = (cols[:, 0:1] == names).astype(F32) + (cols[:, 1:2] == names).astype(F32)
    low = iota((256, 256), 0)
    col = iota((256, 256), 1)
    tri_b = ((col <= low) & ((col >> 4) == (low >> 4))).astype(F32).astype(BF16)
    rank4 = jnp.dot(tri_b, member4.astype(BF16), preferred_element_type=F32)
    token = iota((256, 128), 0)
    block = token >> 4
    slot = rank4.astype(jnp.int32) - 1
    where_to = (block >> 3) * 72 + jnp.where(slot < 8, (block & 7) * 8 + slot, 64 + (block & 7))
    where_to = jnp.where(member4 > 0, where_to, -1000)
    onehot = (where_to[:, 0:1] == col).astype(F32)
    rank_s[...] = jnp.transpose(onehot)
    own_full = rank_s[0:ROWS, :].astype(BF16)
    own_half = rank_s[half_rows, :].astype(BF16)
    for k in range(3):
        theirs = (where_to[:, k + 1 : k + 2] == col).astype(F32).astype(BF16)
        amat[k] = jnp.dot(own_full, theirs, preferred_element_type=F32)[:, 0:ROWS].astype(BF16)
        theirs = (where_to[:, k + 1 : k + 2] - h * 72 == col).astype(F32).astype(BF16)
        amat_h[k] = jnp.dot(own_half, theirs, preferred_element_type=F32)[:, 0:72].astype(BF16)

    tangents(v0, tb0, town0, a1, 0)
    def gram(k, sums):
        s00, s01, s11 = sums
        part = pl.ds(pl.multiple_of(k * 256, 256), 256)
        for u in range(2):
            b0 = v0[u, :, part].astype(F32)
            b1 = v1[u, :, part].astype(F32)
            fold = lambda a: jnp.sum(a.reshape(16, 8, 256), axis=0)
            s00 = s00 + fold(b0 * b0)
            s01 = s01 + fold(b0 * b1)
            s11 = s11 + fold(b1 * b1)
        return s00, s01, s11

    zero = jnp.zeros((8, 256), F32)
    s00, s01, s11 = lax.fori_loop(0, HALF // 256, gram, (zero, zero, zero))

    resp_f, resp_h = total[0:ROWS], total[ROWS:CHUNK]
    for k in range(3):
        zc[k].wait_recv()
        resp_f = resp_f + jnp.dot(amat[k], rz[k, 0:ROWS, :], preferred_element_type=F32)
        resp_h = resp_h + jnp.dot(amat_h[k], rz[k, ROWS:CHUNK, :], preferred_element_type=F32)
    base = c * HALF + a1 * GROUP
    sig_f = sigma[:, pl.ds(pl.multiple_of(base + a2 * 128, 128), 128)]
    sig_h = sigma[:, pl.ds(pl.multiple_of(base + (4 + a2 // 2) * 128, 128), 128)]
    c4[m, 0:ROWS] = (rho_s[...] * sig_f * (resp_f * SCALE)).astype(BF16)
    c4[m, ROWS:CHUNK] = (rho_s[half_rows, :] * sig_h * (resp_h * SCALE)).astype(BF16)

    cg1 = along(c4, cg_send, cg_recv)
    cg2 = spread(c4, 0, cg_send, cg_recv)
    relay(cg1, cg2, c4, cg_send, cg_recv)

    def assemble(ref, g):
        for i in range(4):
            cg[:, i * 128 : (i + 1) * 128] = ref[g * 4 + i, 0:ROWS, :]
        for i in range(2):
            both = [ref[g * 4 + 2 * i + u, ROWS:CHUNK, :].astype(F32) for u in range(2)]
            cg[:, (4 + i) * 128 : (5 + i) * 128] = jnp.concatenate(both, axis=0).astype(BF16)

    for copy in list(rs3.values()) + squares:
        copy.wait_recv()
    line = lambda a: jnp.sum(a, axis=0, keepdims=True)
    dot0 = jnp.zeros((1, 128), F32)
    for i in range(4):
        partial = ((town0[i] + r10[0, i].astype(F32)) + r10[1, i].astype(F32)) + r10[2, i].astype(F32)
        dot0 = dot0 + line(c4[a1 * 4 + i].astype(F32) * partial)
    square = ((sq_own[...] + sq_in[0].astype(F32)) + sq_in[1].astype(F32)) + sq_in[2].astype(F32)
    sq_b = square.astype(BF16)
    assemble(c4, a1)
    mixed = jnp.dot(sq_b[0:ROWS], cg[0:128, :], preferred_element_type=F32)
    mixed_low = jnp.dot(sq_b[ROWS:160, 0:16], cg[128:ROWS, :], preferred_element_type=F32)
    quad = line(cg[0:128, :].astype(F32) * mixed[0:128])
    quad = quad + line(cg[128:ROWS, :].astype(F32) * (2.0 * mixed[128:ROWS] + mixed_low))
    quad = sum(quad[:, i * 128 : (i + 1) * 128] for i in range(6))
    lines = [
        dot0 * SCALE,
        line(c4[m].astype(F32) * held[...]) * SCALE,
        quad * (SCALE * SCALE),
    ] + [line(s[:, 0:128] + s[:, 128:256]) for s in (s00, s01, s11)]
    lines.append(jnp.zeros((2, 128), F32))
    red_s[0] = jnp.concatenate(lines, axis=0)
    ras = []
    for k in range(1, 16):
        o = (q + k) % 16
        ras.append(send(red_s.at[0], red_a.at[k - 1], ra_send.at[k - 1], ra_recv.at[k - 1], (y, x, o // 2, o % 2)))

    def rows_image(ref, u, g):
        assemble(ref, g)

        part = pl.ds(pl.multiple_of(g * GROUP, GROUP), GROUP)
        img[u, :, part] = jnp.dot(hid_t[0:128, 0:ROWS], cg[...], preferred_element_type=F32) * SCALE

    cxs = []
    rbs = []
    for n, d in enumerate((0,) + OFFSETS):
        if n == 3:
            acc = red_s[0]
            for k in range(15):
                ras[k].wait_recv()
                acc = acc + red_a[k]
            red_s[1] = acc
            for k in range(1, 16):
                o = (p + k) % 16
                rbs.append(
                    send(red_s.at[1], red_b.at[k - 1], rb_send.at[k - 1], rb_recv.at[k - 1], (o // 4, o % 4, z, c))
                )
        if d:
            landed(cg2, d)
        g = (a1 - d + 4) % 4
        block4 = pl.ds(pl.multiple_of(g * 4, 4), 4)
        cxs.append(send(c4.at[block4], cx.at[block4], cx_send.at[d], cx_recv.at[d], partner))
        rows_image(c4, 0, g)
        if n:
            cxs[n - 1].wait_recv()
            rows_image(cx, 1, (a2 - ((0,) + OFFSETS)[n - 1] + 4) % 4)

    cxs[3].wait_recv()
    rows_image(cx, 1, (a2 - 2 + 4) % 4)
    for k in range(15):
        rbs[k].wait_recv()
        acc = acc + red_b[k]
    scal = jnp.sum(acc, axis=1, keepdims=True) * (1.0 / ENTRIES)
    c0, c1, norm, g00, g01, g11 = [scal[k : k + 1, 0:1] for k in range(6)]
    norm = norm - 2.0 * (c0 * c0 + c1 * c1) + (c0 * c0 * g00 + 2.0 * (c0 * c1) * g01 + c1 * c1 * g11)
    beta = jnp.sqrt(norm)
    hess[...] = jnp.concatenate([c0, c1, beta], axis=1)
    inv = 1.0 / beta
    for u, (w0, w1, start) in enumerate(((v0.at[0], v1.at[0], c * HALF), (v0x, v1x, (1 - c) * HALF))):

        def finish(k, carry):
            part = pl.ds(pl.multiple_of(k * 256, 256), 256)
            resid = (img[u, :, part] - c0 * w0[:, part].astype(F32)) - c1 * w1[:, part].astype(F32)
            out[:, pl.ds(pl.multiple_of(start + k * 256, 256), 256)] = (resid * inv).astype(BF16)
            return carry

        lax.fori_loop(0, HALF // 256, finish, 0)

    for copy in first + core + list(second.values()) + [pre_copy] + list(rs1.values()) + rs2 + [zp] + list(zc.values()) + list(rs3.values()) + squares + cg1 + list(cg2.values()) + cxs + ras + rbs:
        copy.wait_send()


def body(tokens, w_gate, w_up, basis, routes, gates, rho, sigma):
    anywhere = pl.BlockSpec(memory_space=pl.ANY)
    vmem = pl.BlockSpec(memory_space=pltpu.VMEM)
    dma = pltpu.SemaphoreType.DMA
    scratch = [
        pltpu.VMEM((2, 256), jnp.int32),
        pltpu.VMEM((2, 256), F32),
        pltpu.VMEM((1, 16), F32),
        pltpu.VMEM((1, D), F32),
        pltpu.VMEM((256, 8), F32),
        pltpu.VMEM((16, HALF), BF16),
        pltpu.VMEM((2, HALF, 256), BF16),
        pltpu.VMEM((2, 128, HALF), BF16),
        pltpu.VMEM((2, 128, HALF), BF16),
        pltpu.VMEM((128, HALF), BF16),
        pltpu.VMEM((128, HALF), BF16),
        pltpu.VMEM((16, 8, MSG), BF16),
        pltpu.VMEM((ROWS, HALF), BF16),
        pltpu.VMEM((4, 128, 128), F32),
        pltpu.VMEM((8, 384), F32),
        pltpu.VMEM((ROWS, 128), F32),
        pltpu.VMEM((2, ROWS, 256), F32),
        pltpu.VMEM((2, ROWS, 256), F32),
        pltpu.VMEM((ROWS, 256), BF16),
        pltpu.VMEM((256, 256), BF16),
        pltpu.VMEM((3, 4, CHUNK, 128), BF16),
        pltpu.VMEM((3, 4, CHUNK, 128), BF16),
        pltpu.VMEM((4, CHUNK, 128), F32),
        pltpu.VMEM((3, CHUNK, 128), BF16),
        pltpu.VMEM((3, CHUNK, 128), BF16),
        pltpu.VMEM((3, 4, CHUNK, 128), BF16),
        pltpu.VMEM((3, 4, CHUNK, 128), BF16),
        pltpu.VMEM((4, CHUNK, 128), F32),
        pltpu.VMEM((CHUNK, 128), F32),
        pltpu.VMEM((160, 128), F32),
        pltpu.VMEM((160, 128), BF16),
        pltpu.VMEM((3, 160, 128), BF16),
        pltpu.VMEM((CHUNK, 128), BF16),
        pltpu.VMEM((CHUNK, 128), BF16),
        pltpu.VMEM((CHUNK, 128), BF16),
        pltpu.VMEM((3, CHUNK, 128), BF16),
        pltpu.VMEM((3, ROWS, ROWS), BF16),
        pltpu.VMEM((3, 72, 72), BF16),
        pltpu.VMEM((256, 256), F32),
        pltpu.VMEM((ROWS, 128), F32),
        pltpu.VMEM((16, CHUNK, 128), BF16),
        pltpu.VMEM((16, CHUNK, 128), BF16),
        pltpu.VMEM((ROWS, GROUP), BF16),
        pltpu.VMEM((2, 128, HALF), F32),
        pltpu.VMEM((15, 8, 128), F32),
        pltpu.VMEM((15, 8, 128), F32),
        pltpu.VMEM((2, 8, 128), F32),
        dma((11,)),
        dma((5,)), dma((5,)),
        dma((5, 3)), dma((5, 3)),
        dma((5, 3)), dma((5, 3)),
        dma((4, 3)), dma((4, 3)),
        dma((3,)), dma((3,)),
        dma((4,)), dma((4,)),
        dma((5, 3)), dma((5, 3)),
        dma((4,)), dma((4,)),
        dma((15,)), dma((15,)),
        dma((15,)), dma((15,)),
    ]
    operands = (tokens, w_gate, w_up, basis, routes.T, gates.T, rho.reshape(1, 16), sigma.reshape(1, D))
    operands = [pltpu.with_memory_space_constraint(a, pltpu.HBM) for a in operands]
    out, hess = pl.pallas_call(
        kernel,
        out_shape=(jax.ShapeDtypeStruct((128, D), BF16), jax.ShapeDtypeStruct((1, 3), F32)),
        in_specs=[anywhere] * 8,
        out_specs=(vmem, vmem),
        scratch_shapes=scratch,
        compiler_params=pltpu.CompilerParams(
            collective_id=0, has_side_effects=True, vmem_limit_bytes=32 * 1024 * 1024
        ),
        name="arnoldi",
    )(*operands)
    return out, hess.T


def solution(mesh):
    finer = Mesh(mesh.devices.reshape(4, 4, 8, 2), AXES)
    in_specs = (
        P(DP, None),
        P(None, EXPERT_DP),
        P(None, EXPERT_DP),
        P(None, EXPERT_DP, None),
        P(),
        P(),
        P(DP),
        P(),
    )
    out_specs = (P(EXPERT_DP, None), P())
    return jax.shard_map(body, mesh=finer, in_specs=in_specs, out_specs=out_specs, check_vma=False)
```

```python
import functools
import math

import jax
import jax.numpy as jnp
from jax import lax
from jax.experimental import pallas as pl
from jax.experimental.pallas import tpu as pltpu
from jax.sharding import Mesh
from jax.sharding import PartitionSpec as P

D = 6144
FF = 8192
E = 4
HALF = 3072
GROUP = 768
SIDE = 128
MSG = HALF + SIDE + 512
ROWS = 144
CHUNK = 216
DP = ("dp_0", "dp_1")
EXPERT = ("expert_0", "expert_1")
EXPERT_DP = ("expert_0", "expert_1", "dp_0", "dp_1")
AXES = ("dp_0", "dp_1", "expert_0", "expert_1")
MESH = pl.DeviceIdType.MESH
F32 = jnp.float32
BF16 = jnp.bfloat16
SCALE = 1.0 / math.sqrt(FF)
KAPPA = E * FF / 256
ENTRIES = float(E * FF * D)
OFFSETS = (1, 3, 2)


def iota(shape, dim):
    return lax.broadcasted_iota(jnp.int32, shape, dim)


def parts(col):
    hi = col.astype(BF16)
    left = col - hi.astype(F32)
    mid = left.astype(BF16)
    low = (left - mid.astype(F32)).astype(BF16)
    return hi.astype(F32), mid.astype(F32), low.astype(F32)


def joined(side, first):
    return (side[:, first : first + 1] + side[:, first + 1 : first + 2]) + side[:, first + 2 : first + 3]


def slot_order(m):
    return jnp.concatenate([m[0:64], m[128:136], m[64:128], m[136:144]], axis=0)


def kernel(
    tok_hbm, wg_hbm, wu_hbm, basis_hbm, routes_hbm, gates_hbm, rho_hbm, sigma_hbm,
    out, hess,
    routes, gates, rho, sigma, cols, tokv, wbuf, v0, v1, v0x, v1x, gm, gd, exf, exs, side_main, pre_s, pre_r, hid, hid_t,
    tb, r1, town, p2s, r2, tb0, r10, town0, held, sq_own, sq_out, sq_in, zs, rz0, zes, rz, amat, amat_h, rank_s, rho_s, c4, cx, cg, img,
    red_a, red_b, red_s,
    loc_sem, core_send, core_recv, ag_send, ag_recv, rs_send, rs_recv, rt_send, rt_recv, sq_send, sq_recv, z_send, z_recv,
    cg_send, cg_recv, cx_send, cx_recv, ra_send, ra_recv, rb_send, rb_recv,
):
    y, x, z, c = [lax.axis_index(name) for name in AXES]
    a1 = y * (1 - c) + x * c
    a2 = x * (1 - c) + y * c
    p = y * 4 + x
    q = z * 2 + c
    e = z // 2
    sg = 2 * (z % 2) - 1
    h = a2 % 2
    half_rows = pl.ds(pl.multiple_of(h * 72, 8), 72)

    def plane(b1, b2):
        return (b1 * (1 - c) + b2 * c, b2 * (1 - c) + b1 * c, z, c)

    def send(src, dst, s_sem, r_sem, device):
        copy = pltpu.make_async_remote_copy(
            src_ref=src, dst_ref=dst, send_sem=s_sem, recv_sem=r_sem, device_id=device, device_id_type=MESH
        )
        copy.start()
        return copy

    def local(src, dst, sem):
        copy = pltpu.make_async_copy(src, dst, sem)
        copy.start()
        return copy

    barrier = pltpu.get_barrier_semaphore()
    greeted = [(y, x, z, 1 - c)]
    greeted += [((y + d) % 4, x, z, c) for d in OFFSETS] + [(y, (x + d) % 4, z, c) for d in OFFSETS]
    greeted += [(y, x, (z + sg * d + 8) % 8, c) for d in (-1, 1, -2, 3)]
    for device in greeted:
        pl.semaphore_signal(barrier, inc=1, device_id=device, device_id_type=MESH)

    mine = pl.ds(pl.multiple_of(c * HALF, HALF), HALF)
    other = pl.ds(pl.multiple_of((1 - c) * HALF, HALF), HALF)
    small = [
        local(routes_hbm, routes, loc_sem.at[7]),
        local(gates_hbm, gates, loc_sem.at[8]),
        local(rho_hbm, rho, loc_sem.at[9]),
    ]
    loads = [
        local(tok_hbm.at[:, mine], tokv, loc_sem.at[0]),
        local(wg_hbm.at[mine, :], wbuf.at[0, :, pl.ds(0, 128)], loc_sem.at[1]),
        local(wu_hbm.at[mine, :], wbuf.at[0, :, pl.ds(128, 128)], loc_sem.at[2]),
        local(basis_hbm.at[1, :, mine], v1.at[0], loc_sem.at[3]),
        local(basis_hbm.at[0, :, mine], v0.at[0], loc_sem.at[4]),
        local(basis_hbm.at[1, :, other], v1x, loc_sem.at[5]),
        local(basis_hbm.at[0, :, other], v0x, loc_sem.at[6]),
        local(sigma_hbm, sigma, loc_sem.at[10]),
    ]
    for copy in small:
        copy.wait()

    cols[...] = jnp.transpose(
        jnp.concatenate([routes[...].astype(F32), gates[...], jnp.zeros((4, 256), F32)], axis=0)
    )
    own = cols[pl.ds(pl.multiple_of(p * 16, 16), 16), :]
    ef = e.astype(F32)
    hit0 = own[:, 0:1] == ef
    hit1 = own[:, 1:2] == ef
    member = hit0.astype(F32) + hit1.astype(F32)
    gate_tok = jnp.where(hit0, own[:, 2:3], 0.0) + jnp.where(hit1, own[:, 3:4], 0.0)
    tri = (iota((16, 16), 1) <= iota((16, 16), 0)).astype(F32).astype(BF16)
    member_b = jnp.broadcast_to(member, (16, 128))
    rank = jnp.dot(tri, member_b.astype(BF16), preferred_element_type=F32)
    lane = iota((16, 128), 1)
    place_t = jnp.where((rank - 1.0 == lane.astype(F32)) & (member_b > 0), 1.0, 0.0)
    place = jnp.transpose(place_t)[0:16, :].astype(BF16)
    diagonal = iota((16, 16), 0) == iota((16, 16), 1)
    rho_tok = jnp.sum(jnp.where(diagonal, jnp.broadcast_to(rho[...], (16, 16)), 0.0), axis=1, keepdims=True)
    r_hi, r_mid, r_low = parts(rho_tok)
    g_hi, g_mid, g_low = parts(gate_tok)
    side_in = jnp.zeros((16, 128), F32)
    for index, col in enumerate((r_hi, r_mid, r_low, g_hi, g_mid, g_low)):
        side_in = jnp.where(lane == index, col, side_in)
    side = jnp.dot(place, side_in.astype(BF16), preferred_element_type=F32)
    m = a1 * 4 + a2
    gm[m, :, HALF : HALF + SIDE] = side[0:8].astype(BF16)
    gm[m, :, HALF + SIDE + 384 : MSG] = jnp.broadcast_to(side[8:9], (8, 128)).astype(BF16)
    loads[0].wait()
    picked = jnp.dot(place, tokv[...], preferred_element_type=F32)
    gm[m, :, 0:HALF] = picked[0:8].astype(BF16)
    for r in range(8):
        exs[r : r + 1, :] = picked[8:9, r * 384 : (r + 1) * 384]
    gm[m, :, HALF + SIDE : HALF + SIDE + 384] = exs[...].astype(BF16)

    pl.semaphore_wait(barrier, 11)

    def spread(ref, lap, s_sem, r_sem):
        index = a1 * 4 + (a2 + 4 - lap) % 4
        return {
            (lap, d): send(
                ref.at[index], ref.at[index], s_sem.at[lap, d - 1], r_sem.at[lap, d - 1], plane((a1 + d) % 4, a2)
            )
            for d in OFFSETS
        }

    def pass_on(copies, ref, lap, s_sem, r_sem):
        d = 1 if lap in (0, 3) else 3
        copies[lap, d].wait_recv()
        index = ((a1 + 4 - d) % 4) * 4 + (a2 + 4 - lap) % 4
        copies[lap, 2] = send(
            ref.at[index], ref.at[index], s_sem.at[lap, 1], r_sem.at[lap, 1], plane((a1 + d) % 4, a2)
        )

    def along(ref, s_sem, r_sem):
        return [
            send(ref.at[m], ref.at[m], s_sem.at[4, d - 1], r_sem.at[4, d - 1], plane(a1, (a2 + d) % 4))
            for d in OFFSETS
        ]

    def relay(first, copies, ref, s_sem, r_sem):
        for d, copy in zip(OFFSETS, first):
            copy.wait_recv()
            copies.update(spread(ref, d, s_sem, r_sem))

    def finish_laps(copies, ref, s_sem, r_sem):
        for lap in OFFSETS:
            pass_on(copies, ref, lap, s_sem, r_sem)

    def landed(copies, d):
        for lap in range(4):
            copies[lap, d].wait_recv()

    first = along(gm, ag_send, ag_recv)
    second = spread(gm, 0, ag_send, ag_recv)
    partner = (y, x, z, 1 - c)
    core = [
        send(wg_hbm.at[other, :], wbuf.at[1, :, pl.ds(0, 128)], core_send.at[0], core_recv.at[0], partner),
        send(wu_hbm.at[other, :], wbuf.at[1, :, pl.ds(128, 128)], core_send.at[1], core_recv.at[1], partner),
        send(basis_hbm.at[1, :, other], v1.at[1], core_send.at[2], core_recv.at[2], partner),
        send(basis_hbm.at[0, :, other], v0.at[1], core_send.at[3], core_recv.at[3], partner),
    ]

    relay(first, second, gm, ag_send, ag_recv)

    for d in OFFSETS:
        landed(second, d)
    for copy in loads[1:]:
        copy.wait()
    for copy in core:
        copy.wait_recv()

    def source(o):
        return o * (1 - c) + ((o % 4) * 4 + o // 4) * c

    for k in range(8):
        pair = [gm[source(2 * k + u), :, 0:HALF].astype(F32) for u in range(2)]
        gd[16 * k : 16 * k + 16, :] = jnp.concatenate(pair, axis=0).astype(BF16)
    for o in range(16):
        block_o = gm[source(o)][:, HALF:MSG].astype(F32)
        side_main[8 * o : 8 * o + 8, :] = block_o[:, 0:SIDE]
        for t in range(4):
            exf[t, 8 * o : 8 * o + 8, :] = block_o[:, SIDE + t * 128 : SIDE + (t + 1) * 128]
    for r in range(8):
        for t in range(3):
            f = r * 384 + t * 128
            gd[128:144, f : f + 128] = exf[t, pl.ds(r, 16, stride=8), :].astype(BF16)
    side_main[128:144, :] = exf[3, pl.ds(0, 16, stride=8), :]

    for u in range(2):
        pre_s[u] = jnp.dot(gd[...], wbuf[u], preferred_element_type=F32)
    pre_copy = send(pre_s, pre_r, core_send.at[4], core_recv.at[4], partner)
    side_all = side_main[...]
    rho_slot = slot_order(jnp.broadcast_to(joined(side_all, 0), (ROWS, 128)))
    rho_s[...] = KAPPA * rho_slot
    gate_slot = slot_order(jnp.broadcast_to(joined(side_all, 3), (ROWS, 128)))
    pre_copy.wait_recv()
    hidden = []
    for u in range(2):
        both = slot_order(pre_s[u] + pre_r[1 - u])
        gate, up = both[:, 0:128], both[:, 128:256]
        hidden.append(gate / (1.0 + jnp.exp(-gate)) * up * gate_slot)
    hidden = jnp.concatenate(hidden, axis=1)
    hid[...] = hidden.astype(BF16)

    def tangents(vector, parts_out, own_out, g, d):
        part = pl.ds(pl.multiple_of(g * GROUP, GROUP), GROUP)
        rows = vector[:, :, part].reshape(256, GROUP)
        tangent = jnp.dot(hid[...], rows, preferred_element_type=F32)
        for i in range(4):
            t = 4 + i // 2
            full = tangent[:, i * 128 : (i + 1) * 128]
            half = tangent[(i % 2) * 72 : (i % 2) * 72 + 72, t * 128 : (t + 1) * 128]
            if d:
                parts_out[d - 1, i, 0:ROWS] = full.astype(BF16)
                parts_out[d - 1, i, ROWS:CHUNK] = half.astype(BF16)
            else:
                own_out[i, 0:ROWS] = full
                own_out[i, ROWS:CHUNK] = half

    def reduce_first(parts_out, landing, d, s_sem, r_sem):
        return {
            (o, d): send(
                parts_out.at[d - 1, (a2 + o) % 4], landing.at[d - 1, (a2 + o) % 4],
                s_sem.at[o, d - 1], r_sem.at[o, d - 1], plane((a1 + d) % 4, a2),
            )
            for o in OFFSETS + (0,)
        }

    def reduce_second(copies, own_out, landing, parts_two, landing_two, s_sem, r_sem):
        def reduced(i):
            return ((own_out[i] + landing[0, i].astype(F32)) + landing[1, i].astype(F32)) + landing[2, i].astype(F32)

        later = []
        for o in OFFSETS + (0,):
            for d in OFFSETS:
                copies[o, d].wait_recv()
            i = (a2 + o) % 4
            if o:
                parts_two[o - 1] = reduced(i).astype(BF16)
                later.append(
                    send(
                        parts_two.at[o - 1], landing_two.at[o - 1],
                        s_sem.at[4, o - 1], r_sem.at[4, o - 1], plane(a1, i),
                    )
                )
        return later, reduced(a2)

    rs1 = {}
    for d in OFFSETS:
        tangents(v1, tb, town, (a1 + d) % 4, d)
        rs1.update(reduce_first(tb, r1, d, rs_send, rs_recv))
    tangents(v1, tb, town, a1, 0)
    square = lax.dot_general(hid[...], hid[...], (((1,), (1,)), ((), ())), preferred_element_type=F32)
    corner = jnp.concatenate([square[128:ROWS, 128:ROWS], jnp.zeros((16, 112), F32)], axis=1)
    sq_own[...] = jnp.concatenate([square[:, 0:128], corner], axis=0)
    sq_out[...] = sq_own[...].astype(BF16)
    hid_t[...] = jnp.transpose(jnp.concatenate([hidden, jnp.zeros((112, 256), F32)], axis=0)).astype(BF16)
    for d in (1, 3):
        tangents(v0, tb0, town0, (a1 + d) % 4, d)

    rs2, mine_sum = reduce_second(rs1, town, r1, p2s, r2, rs_send, rs_recv)
    for copy in rs2:
        copy.wait_recv()
    mine_sum = ((mine_sum + r2[0].astype(F32)) + r2[1].astype(F32)) + r2[2].astype(F32)
    held[...] = mine_sum

    zs[...] = mine_sum.astype(BF16)
    zp = send(zs, rz0, z_send.at[0], z_recv.at[0], (y, x, z - sg, c))
    rs3 = {}
    for d in OFFSETS:
        if d == 2:
            tangents(v0, tb0, town0, (a1 + d) % 4, d)
        rs3.update(reduce_first(tb0, r10, d, rt_send, rt_recv))
    squares = [
        send(sq_out, sq_in.at[d - 1], sq_send.at[d - 1], sq_recv.at[d - 1], plane((a1 + d) % 4, a2))
        for d in OFFSETS
    ]
    zp.wait_recv()
    total = mine_sum + rz0[...].astype(F32)
    zes[...] = total.astype(BF16)
    zc = {
        k: send(zes, rz.at[k], z_send.at[1 + k], z_recv.at[1 + k], (y, x, (z + sg * (k + 1) + 8) % 8, c))
        for k in (2, 1, 0)
    }

    t_lane = iota((256, 128), 1)
    shift = jnp.where(t_lane == 1, sg, 0) + jnp.where(t_lane == 2, -sg, 0) + jnp.where(t_lane == 3, 2, 0)
    names = jnp.where(t_lane < 4, (e + shift + 4) & 3, -1)
    names = names.astype(F32)
    member4 = (cols[:, 0:1] == names).astype(F32) + (cols[:, 1:2] == names).astype(F32)
    low = iota((256, 256), 0)
    col = iota((256, 256), 1)
    tri_b = ((col <= low) & ((col >> 4) == (low >> 4))).astype(F32).astype(BF16)
    rank4 = jnp.dot(tri_b, member4.astype(BF16), preferred_element_type=F32)
    token = iota((256, 128), 0)
    block = token >> 4
    slot = rank4.astype(jnp.int32) - 1
    where_to = (block >> 3) * 72 + jnp.where(slot < 8, (block & 7) * 8 + slot, 64 + (block & 7))
    where_to = jnp.where(member4 > 0, where_to, -1000)
    onehot = (where_to[:, 0:1] == col).astype(F32)
    rank_s[...] = jnp.transpose(onehot)
    own_full = rank_s[0:ROWS, :].astype(BF16)
    own_half = rank_s[half_rows, :].astype(BF16)
    for k in range(3):
        theirs = (where_to[:, k + 1 : k + 2] == col).astype(F32).astype(BF16)
        amat[k] = jnp.dot(own_full, theirs, preferred_element_type=F32)[:, 0:ROWS].astype(BF16)
        theirs = (where_to[:, k + 1 : k + 2] - h * 72 == col).astype(F32).astype(BF16)
        amat_h[k] = jnp.dot(own_half, theirs, preferred_element_type=F32)[:, 0:72].astype(BF16)

    tangents(v0, tb0, town0, a1, 0)
    def gram(k, sums):
        s00, s01, s11 = sums
        part = pl.ds(pl.multiple_of(k * 256, 256), 256)
        for u in range(2):
            b0 = v0[u, :, part].astype(F32)
            b1 = v1[u, :, part].astype(F32)
            fold = lambda a: jnp.sum(a.reshape(16, 8, 256), axis=0)
            s00 = s00 + fold(b0 * b0)
            s01 = s01 + fold(b0 * b1)
            s11 = s11 + fold(b1 * b1)
        return s00, s01, s11

    zero = jnp.zeros((8, 256), F32)
    s00, s01, s11 = lax.fori_loop(0, HALF // 256, gram, (zero, zero, zero))

    resp_f, resp_h = total[0:ROWS], total[ROWS:CHUNK]
    for k in range(3):
        zc[k].wait_recv()
        resp_f = resp_f + jnp.dot(amat[k], rz[k, 0:ROWS, :], preferred_element_type=F32)
        resp_h = resp_h + jnp.dot(amat_h[k], rz[k, ROWS:CHUNK, :], preferred_element_type=F32)
    base = c * HALF + a1 * GROUP
    sig_f = sigma[:, pl.ds(pl.multiple_of(base + a2 * 128, 128), 128)]
    sig_h = sigma[:, pl.ds(pl.multiple_of(base + (4 + a2 // 2) * 128, 128), 128)]
    c4[m, 0:ROWS] = (rho_s[...] * sig_f * (resp_f * SCALE)).astype(BF16)
    c4[m, ROWS:CHUNK] = (rho_s[half_rows, :] * sig_h * (resp_h * SCALE)).astype(BF16)

    cg1 = along(c4, cg_send, cg_recv)
    cg2 = spread(c4, 0, cg_send, cg_recv)
    relay(cg1, cg2, c4, cg_send, cg_recv)

    def assemble(ref, g):
        for i in range(4):
            cg[:, i * 128 : (i + 1) * 128] = ref[g * 4 + i, 0:ROWS, :]
        for i in range(2):
            both = [ref[g * 4 + 2 * i + u, ROWS:CHUNK, :].astype(F32) for u in range(2)]
            cg[:, (4 + i) * 128 : (5 + i) * 128] = jnp.concatenate(both, axis=0).astype(BF16)

    for copy in list(rs3.values()) + squares:
        copy.wait_recv()
    line = lambda a: jnp.sum(a, axis=0, keepdims=True)
    dot0 = jnp.zeros((1, 128), F32)
    for i in range(4):
        partial = ((town0[i] + r10[0, i].astype(F32)) + r10[1, i].astype(F32)) + r10[2, i].astype(F32)
        dot0 = dot0 + line(c4[a1 * 4 + i].astype(F32) * partial)
    square = ((sq_own[...] + sq_in[0].astype(F32)) + sq_in[1].astype(F32)) + sq_in[2].astype(F32)
    sq_b = square.astype(BF16)
    assemble(c4, a1)
    mixed = jnp.dot(sq_b[0:ROWS], cg[0:128, :], preferred_element_type=F32)
    mixed_low = jnp.dot(sq_b[ROWS:160, 0:16], cg[128:ROWS, :], preferred_element_type=F32)
    quad = line(cg[0:128, :].astype(F32) * mixed[0:128])
    quad = quad + line(cg[128:ROWS, :].astype(F32) * (2.0 * mixed[128:ROWS] + mixed_low))
    quad = sum(quad[:, i * 128 : (i + 1) * 128] for i in range(6))
    lines = [
        dot0 * SCALE,
        line(c4[m].astype(F32) * held[...]) * SCALE,
        quad * (SCALE * SCALE),
    ] + [line(s[:, 0:128] + s[:, 128:256]) for s in (s00, s01, s11)]
    lines.append(jnp.zeros((2, 128), F32))
    red_s[0] = jnp.concatenate(lines, axis=0)
    ras = []
    for k in range(1, 16):
        o = (q + k) % 16
        ras.append(send(red_s.at[0], red_a.at[k - 1], ra_send.at[k - 1], ra_recv.at[k - 1], (y, x, o // 2, o % 2)))

    def rows_image(ref, u, g):
        assemble(ref, g)

        part = pl.ds(pl.multiple_of(g * GROUP, GROUP), GROUP)
        img[u, :, part] = jnp.dot(hid_t[0:128, 0:ROWS], cg[...], preferred_element_type=F32) * SCALE

    cxs = []
    rbs = []
    for n, d in enumerate((0,) + OFFSETS):
        if n == 2:
            acc = red_s[0]
            for k in range(15):
                ras[k].wait_recv()
                acc = acc + red_a[k]
            red_s[1] = acc
            for k in range(1, 16):
                o = (p + k) % 16
                rbs.append(
                    send(red_s.at[1], red_b.at[k - 1], rb_send.at[k - 1], rb_recv.at[k - 1], (o // 4, o % 4, z, c))
                )
        if d:
            landed(cg2, d)
        g = (a1 - d + 4) % 4
        block4 = pl.ds(pl.multiple_of(g * 4, 4), 4)
        cxs.append(send(c4.at[block4], cx.at[block4], cx_send.at[d], cx_recv.at[d], partner))
        rows_image(c4, 0, g)
        if n:
            cxs[n - 1].wait_recv()
            rows_image(cx, 1, (a2 - ((0,) + OFFSETS)[n - 1] + 4) % 4)

    cxs[3].wait_recv()
    rows_image(cx, 1, (a2 - 2 + 4) % 4)
    for k in range(15):
        rbs[k].wait_recv()
        acc = acc + red_b[k]
    scal = jnp.sum(acc, axis=1, keepdims=True) * (1.0 / ENTRIES)
    c0, c1, norm, g00, g01, g11 = [scal[k : k + 1, 0:1] for k in range(6)]
    norm = norm - 2.0 * (c0 * c0 + c1 * c1) + (c0 * c0 * g00 + 2.0 * (c0 * c1) * g01 + c1 * c1 * g11)
    beta = jnp.sqrt(norm)
    hess[...] = jnp.concatenate([c0, c1, beta], axis=1)
    inv = 1.0 / beta
    for u, (w0, w1, start) in enumerate(((v0.at[0], v1.at[0], c * HALF), (v0x, v1x, (1 - c) * HALF))):

        def finish(k, carry):
            part = pl.ds(pl.multiple_of(k * 256, 256), 256)
            resid = (img[u, :, part] - c0 * w0[:, part].astype(F32)) - c1 * w1[:, part].astype(F32)
            out[:, pl.ds(pl.multiple_of(start + k * 256, 256), 256)] = (resid * inv).astype(BF16)
            return carry

        lax.fori_loop(0, HALF // 256, finish, 0)

    for copy in first + core + list(second.values()) + [pre_copy] + list(rs1.values()) + rs2 + [zp] + list(zc.values()) + list(rs3.values()) + squares + cg1 + list(cg2.values()) + cxs + ras + rbs:
        copy.wait_send()


def body(tokens, w_gate, w_up, basis, routes, gates, rho, sigma):
    anywhere = pl.BlockSpec(memory_space=pl.ANY)
    vmem = pl.BlockSpec(memory_space=pltpu.VMEM)
    dma = pltpu.SemaphoreType.DMA
    scratch = [
        pltpu.VMEM((2, 256), jnp.int32),
        pltpu.VMEM((2, 256), F32),
        pltpu.VMEM((1, 16), F32),
        pltpu.VMEM((1, D), F32),
        pltpu.VMEM((256, 8), F32),
        pltpu.VMEM((16, HALF), BF16),
        pltpu.VMEM((2, HALF, 256), BF16),
        pltpu.VMEM((2, 128, HALF), BF16),
        pltpu.VMEM((2, 128, HALF), BF16),
        pltpu.VMEM((128, HALF), BF16),
        pltpu.VMEM((128, HALF), BF16),
        pltpu.VMEM((16, 8, MSG), BF16),
        pltpu.VMEM((ROWS, HALF), BF16),
        pltpu.VMEM((4, 128, 128), F32),
        pltpu.VMEM((8, 384), F32),
        pltpu.VMEM((ROWS, 128), F32),
        pltpu.VMEM((2, ROWS, 256), F32),
        pltpu.VMEM((2, ROWS, 256), F32),
        pltpu.VMEM((ROWS, 256), BF16),
        pltpu.VMEM((256, 256), BF16),
        pltpu.VMEM((3, 4, CHUNK, 128), BF16),
        pltpu.VMEM((3, 4, CHUNK, 128), BF16),
        pltpu.VMEM((4, CHUNK, 128), F32),
        pltpu.VMEM((3, CHUNK, 128), BF16),
        pltpu.VMEM((3, CHUNK, 128), BF16),
        pltpu.VMEM((3, 4, CHUNK, 128), BF16),
        pltpu.VMEM((3, 4, CHUNK, 128), BF16),
        pltpu.VMEM((4, CHUNK, 128), F32),
        pltpu.VMEM((CHUNK, 128), F32),
        pltpu.VMEM((160, 128), F32),
        pltpu.VMEM((160, 128), BF16),
        pltpu.VMEM((3, 160, 128), BF16),
        pltpu.VMEM((CHUNK, 128), BF16),
        pltpu.VMEM((CHUNK, 128), BF16),
        pltpu.VMEM((CHUNK, 128), BF16),
        pltpu.VMEM((3, CHUNK, 128), BF16),
        pltpu.VMEM((3, ROWS, ROWS), BF16),
        pltpu.VMEM((3, 72, 72), BF16),
        pltpu.VMEM((256, 256), F32),
        pltpu.VMEM((ROWS, 128), F32),
        pltpu.VMEM((16, CHUNK, 128), BF16),
        pltpu.VMEM((16, CHUNK, 128), BF16),
        pltpu.VMEM((ROWS, GROUP), BF16),
        pltpu.VMEM((2, 128, HALF), F32),
        pltpu.VMEM((15, 8, 128), F32),
        pltpu.VMEM((15, 8, 128), F32),
        pltpu.VMEM((2, 8, 128), F32),
        dma((11,)),
        dma((5,)), dma((5,)),
        dma((5, 3)), dma((5, 3)),
        dma((5, 3)), dma((5, 3)),
        dma((4, 3)), dma((4, 3)),
        dma((3,)), dma((3,)),
        dma((4,)), dma((4,)),
        dma((5, 3)), dma((5, 3)),
        dma((4,)), dma((4,)),
        dma((15,)), dma((15,)),
        dma((15,)), dma((15,)),
    ]
    operands = (tokens, w_gate, w_up, basis, routes.T, gates.T, rho.reshape(1, 16), sigma.reshape(1, D))
    operands = [pltpu.with_memory_space_constraint(a, pltpu.HBM) for a in operands]
    out, hess = pl.pallas_call(
        kernel,
        out_shape=(jax.ShapeDtypeStruct((128, D), BF16), jax.ShapeDtypeStruct((1, 3), F32)),
        in_specs=[anywhere] * 8,
        out_specs=(vmem, vmem),
        scratch_shapes=scratch,
        compiler_params=pltpu.CompilerParams(
            collective_id=0, has_side_effects=True, vmem_limit_bytes=32 * 1024 * 1024
        ),
        name="arnoldi",
    )(*operands)
    return out, hess.T


def solution(mesh):
    finer = Mesh(mesh.devices.reshape(4, 4, 8, 2), AXES)
    in_specs = (
        P(DP, None),
        P(None, EXPERT_DP),
        P(None, EXPERT_DP),
        P(None, EXPERT_DP, None),
        P(),
        P(),
        P(DP),
        P(),
    )
    out_specs = (P(EXPERT_DP, None), P())
    return jax.shard_map(body, mesh=finer, in_specs=in_specs, out_specs=out_specs, check_vma=False)
```

```python
import functools
import math

import jax
import jax.numpy as jnp
from jax import lax
from jax.experimental import pallas as pl
from jax.experimental.pallas import tpu as pltpu
from jax.sharding import Mesh
from jax.sharding import PartitionSpec as P

D = 6144
FF = 8192
E = 4
HALF = 3072
GROUP = 768
SIDE = 128
MSG = HALF + SIDE + 512
ROWS = 144
CHUNK = 216
DP = ("dp_0", "dp_1")
EXPERT = ("expert_0", "expert_1")
EXPERT_DP = ("expert_0", "expert_1", "dp_0", "dp_1")
AXES = ("dp_0", "dp_1", "expert_0", "expert_1")
MESH = pl.DeviceIdType.MESH
F32 = jnp.float32
BF16 = jnp.bfloat16
SCALE = 1.0 / math.sqrt(FF)
KAPPA = E * FF / 256
ENTRIES = float(E * FF * D)
OFFSETS = (1, 3, 2)


def iota(shape, dim):
    return lax.broadcasted_iota(jnp.int32, shape, dim)


def parts(col):
    hi = col.astype(BF16)
    left = col - hi.astype(F32)
    mid = left.astype(BF16)
    low = (left - mid.astype(F32)).astype(BF16)
    return hi.astype(F32), mid.astype(F32), low.astype(F32)


def joined(side, first):
    return (side[:, first : first + 1] + side[:, first + 1 : first + 2]) + side[:, first + 2 : first + 3]


def slot_order(m):
    return jnp.concatenate([m[0:64], m[128:136], m[64:128], m[136:144]], axis=0)


def kernel(
    tok_hbm, wg_hbm, wu_hbm, basis_hbm, routes_hbm, gates_hbm, rho_hbm, sigma_hbm,
    out, hess,
    routes, gates, rho, sigma, cols, tokv, wbuf, v0, v1, v0x, v1x, gm, gd, exf, exs, side_main, pre_s, pre_r, hid, hid_t,
    tb, r1, town, p2s, r2, tb0, r10, town0, held, sq_own, sq_out, sq_in, zs, rz0, zes, rz, amat, amat_h, rank_s, rho_s, c4, cx, cg, img,
    red_a, red_b, red_s,
    far_sem, loc_sem, core_send, core_recv, ag_send, ag_recv, rs_send, rs_recv, rt_send, rt_recv, sq_send, sq_recv, z_send, z_recv,
    cg_send, cg_recv, cx_send, cx_recv, ra_send, ra_recv, rb_send, rb_recv,
):
    y, x, z, c = [lax.axis_index(name) for name in AXES]
    a1 = y * (1 - c) + x * c
    a2 = x * (1 - c) + y * c
    p = y * 4 + x
    q = z * 2 + c
    e = z // 2
    sg = 2 * (z % 2) - 1
    h = a2 % 2
    half_rows = pl.ds(pl.multiple_of(h * 72, 8), 72)

    def plane(b1, b2):
        return (b1 * (1 - c) + b2 * c, b2 * (1 - c) + b1 * c, z, c)

    def send(src, dst, s_sem, r_sem, device):
        copy = pltpu.make_async_remote_copy(
            src_ref=src, dst_ref=dst, send_sem=s_sem, recv_sem=r_sem, device_id=device, device_id_type=MESH
        )
        copy.start()
        return copy

    def local(src, dst, sem):
        copy = pltpu.make_async_copy(src, dst, sem)
        copy.start()
        return copy

    barrier = pltpu.get_barrier_semaphore()
    greeted = [(y, x, z, 1 - c)]
    greeted += [((y + d) % 4, x, z, c) for d in OFFSETS] + [(y, (x + d) % 4, z, c) for d in OFFSETS]
    beside = [(y, x, (z + d) % 8, c) for d in (1, 7)]
    greeted += beside
    for device in greeted:
        pl.semaphore_signal(barrier, inc=1, device_id=device, device_id_type=MESH)

    mine = pl.ds(pl.multiple_of(c * HALF, HALF), HALF)
    other = pl.ds(pl.multiple_of((1 - c) * HALF, HALF), HALF)
    small = [
        local(routes_hbm, routes, loc_sem.at[7]),
        local(gates_hbm, gates, loc_sem.at[8]),
        local(rho_hbm, rho, loc_sem.at[9]),
    ]
    loads = [
        local(tok_hbm.at[:, mine], tokv, loc_sem.at[0]),
        local(wg_hbm.at[mine, :], wbuf.at[0, :, pl.ds(0, 128)], loc_sem.at[1]),
        local(wu_hbm.at[mine, :], wbuf.at[0, :, pl.ds(128, 128)], loc_sem.at[2]),
        local(basis_hbm.at[1, :, mine], v1.at[0], loc_sem.at[3]),
        local(basis_hbm.at[0, :, mine], v0.at[0], loc_sem.at[4]),
        local(basis_hbm.at[1, :, other], v1x, loc_sem.at[5]),
        local(basis_hbm.at[0, :, other], v0x, loc_sem.at[6]),
        local(sigma_hbm, sigma, loc_sem.at[10]),
    ]
    for copy in small:
        copy.wait()

    cols[...] = jnp.transpose(
        jnp.concatenate([routes[...].astype(F32), gates[...], jnp.zeros((4, 256), F32)], axis=0)
    )
    own = cols[pl.ds(pl.multiple_of(p * 16, 16), 16), :]
    ef = e.astype(F32)
    hit0 = own[:, 0:1] == ef
    hit1 = own[:, 1:2] == ef
    member = hit0.astype(F32) + hit1.astype(F32)
    gate_tok = jnp.where(hit0, own[:, 2:3], 0.0) + jnp.where(hit1, own[:, 3:4], 0.0)
    tri = (iota((16, 16), 1) <= iota((16, 16), 0)).astype(F32).astype(BF16)
    member_b = jnp.broadcast_to(member, (16, 128))
    rank = jnp.dot(tri, member_b.astype(BF16), preferred_element_type=F32)
    lane = iota((16, 128), 1)
    place_t = jnp.where((rank - 1.0 == lane.astype(F32)) & (member_b > 0), 1.0, 0.0)
    place = jnp.transpose(place_t)[0:16, :].astype(BF16)
    diagonal = iota((16, 16), 0) == iota((16, 16), 1)
    rho_tok = jnp.sum(jnp.where(diagonal, jnp.broadcast_to(rho[...], (16, 16)), 0.0), axis=1, keepdims=True)
    r_hi, r_mid, r_low = parts(rho_tok)
    g_hi, g_mid, g_low = parts(gate_tok)
    side_in = jnp.zeros((16, 128), F32)
    for index, col in enumerate((r_hi, r_mid, r_low, g_hi, g_mid, g_low)):
        side_in = jnp.where(lane == index, col, side_in)
    side = jnp.dot(place, side_in.astype(BF16), preferred_element_type=F32)
    m = a1 * 4 + a2
    gm[m, :, HALF : HALF + SIDE] = side[0:8].astype(BF16)
    gm[m, :, HALF + SIDE + 384 : MSG] = jnp.broadcast_to(side[8:9], (8, 128)).astype(BF16)
    loads[0].wait()
    picked = jnp.dot(place, tokv[...], preferred_element_type=F32)
    gm[m, :, 0:HALF] = picked[0:8].astype(BF16)
    for r in range(8):
        exs[r : r + 1, :] = picked[8:9, r * 384 : (r + 1) * 384]
    gm[m, :, HALF + SIDE : HALF + SIDE + 384] = exs[...].astype(BF16)

    pl.semaphore_wait(barrier, 9)

    def hear(sem):
        for device in beside:
            pl.semaphore_signal(sem, inc=1, device_id=device, device_id_type=MESH)

    hear(far_sem.at[0])

    def spread(ref, lap, s_sem, r_sem):
        index = a1 * 4 + (a2 + 4 - lap) % 4
        return {
            (lap, d): send(
                ref.at[index], ref.at[index], s_sem.at[lap, d - 1], r_sem.at[lap, d - 1], plane((a1 + d) % 4, a2)
            )
            for d in OFFSETS
        }

    def pass_on(copies, ref, lap, s_sem, r_sem):
        d = 1 if lap in (0, 3) else 3
        copies[lap, d].wait_recv()
        index = ((a1 + 4 - d) % 4) * 4 + (a2 + 4 - lap) % 4
        copies[lap, 2] = send(
            ref.at[index], ref.at[index], s_sem.at[lap, 1], r_sem.at[lap, 1], plane((a1 + d) % 4, a2)
        )

    def along(ref, s_sem, r_sem):
        return [
            send(ref.at[m], ref.at[m], s_sem.at[4, d - 1], r_sem.at[4, d - 1], plane(a1, (a2 + d) % 4))
            for d in OFFSETS
        ]

    def relay(first, copies, ref, s_sem, r_sem):
        for d, copy in zip(OFFSETS, first):
            copy.wait_recv()
            copies.update(spread(ref, d, s_sem, r_sem))

    def finish_laps(copies, ref, s_sem, r_sem):
        for lap in OFFSETS:
            pass_on(copies, ref, lap, s_sem, r_sem)

    def landed(copies, d):
        for lap in range(4):
            copies[lap, d].wait_recv()

    first = along(gm, ag_send, ag_recv)
    second = spread(gm, 0, ag_send, ag_recv)
    partner = (y, x, z, 1 - c)
    core = [
        send(wg_hbm.at[other, :], wbuf.at[1, :, pl.ds(0, 128)], core_send.at[0], core_recv.at[0], partner),
        send(wu_hbm.at[other, :], wbuf.at[1, :, pl.ds(128, 128)], core_send.at[1], core_recv.at[1], partner),
        send(basis_hbm.at[1, :, other], v1.at[1], core_send.at[2], core_recv.at[2], partner),
        send(basis_hbm.at[0, :, other], v0.at[1], core_send.at[3], core_recv.at[3], partner),
    ]

    relay(first, second, gm, ag_send, ag_recv)
    pl.semaphore_wait(far_sem.at[0], 2)
    hear(far_sem.at[1])

    for d in OFFSETS:
        landed(second, d)
    for copy in loads[1:]:
        copy.wait()
    pl.semaphore_wait(far_sem.at[1], 2)
    for copy in core:
        copy.wait_recv()

    def source(o):
        return o * (1 - c) + ((o % 4) * 4 + o // 4) * c

    for k in range(8):
        pair = [gm[source(2 * k + u), :, 0:HALF].astype(F32) for u in range(2)]
        gd[16 * k : 16 * k + 16, :] = jnp.concatenate(pair, axis=0).astype(BF16)
    for o in range(16):
        block_o = gm[source(o)][:, HALF:MSG].astype(F32)
        side_main[8 * o : 8 * o + 8, :] = block_o[:, 0:SIDE]
        for t in range(4):
            exf[t, 8 * o : 8 * o + 8, :] = block_o[:, SIDE + t * 128 : SIDE + (t + 1) * 128]
    for r in range(8):
        for t in range(3):
            f = r * 384 + t * 128
            gd[128:144, f : f + 128] = exf[t, pl.ds(r, 16, stride=8), :].astype(BF16)
    side_main[128:144, :] = exf[3, pl.ds(0, 16, stride=8), :]

    for u in range(2):
        pre_s[u] = jnp.dot(gd[...], wbuf[u], preferred_element_type=F32)
    pre_copy = send(pre_s, pre_r, core_send.at[4], core_recv.at[4], partner)
    side_all = side_main[...]
    rho_slot = slot_order(jnp.broadcast_to(joined(side_all, 0), (ROWS, 128)))
    rho_s[...] = KAPPA * rho_slot
    gate_slot = slot_order(jnp.broadcast_to(joined(side_all, 3), (ROWS, 128)))
    pre_copy.wait_recv()
    hidden = []
    for u in range(2):
        both = slot_order(pre_s[u] + pre_r[1 - u])
        gate, up = both[:, 0:128], both[:, 128:256]
        hidden.append(gate / (1.0 + jnp.exp(-gate)) * up * gate_slot)
    hidden = jnp.concatenate(hidden, axis=1)
    hid[...] = hidden.astype(BF16)

    def tangents(vector, parts_out, own_out, g, d):
        part = pl.ds(pl.multiple_of(g * GROUP, GROUP), GROUP)
        rows = vector[:, :, part].reshape(256, GROUP)
        tangent = jnp.dot(hid[...], rows, preferred_element_type=F32)
        for i in range(4):
            t = 4 + i // 2
            full = tangent[:, i * 128 : (i + 1) * 128]
            half = tangent[(i % 2) * 72 : (i % 2) * 72 + 72, t * 128 : (t + 1) * 128]
            if d:
                parts_out[d - 1, i, 0:ROWS] = full.astype(BF16)
                parts_out[d - 1, i, ROWS:CHUNK] = half.astype(BF16)
            else:
                own_out[i, 0:ROWS] = full
                own_out[i, ROWS:CHUNK] = half

    def reduce_first(parts_out, landing, d, s_sem, r_sem):
        return {
            (o, d): send(
                parts_out.at[d - 1, (a2 + o) % 4], landing.at[d - 1, (a2 + o) % 4],
                s_sem.at[o, d - 1], r_sem.at[o, d - 1], plane((a1 + d) % 4, a2),
            )
            for o in OFFSETS + (0,)
        }

    def reduce_second(copies, own_out, landing, parts_two, landing_two, s_sem, r_sem):
        def reduced(i):
            return ((own_out[i] + landing[0, i].astype(F32)) + landing[1, i].astype(F32)) + landing[2, i].astype(F32)

        later = []
        for o in OFFSETS + (0,):
            for d in OFFSETS:
                copies[o, d].wait_recv()
            i = (a2 + o) % 4
            if o:
                parts_two[o - 1] = reduced(i).astype(BF16)
                later.append(
                    send(
                        parts_two.at[o - 1], landing_two.at[o - 1],
                        s_sem.at[4, o - 1], r_sem.at[4, o - 1], plane(a1, i),
                    )
                )
        return later, reduced(a2)

    rs1 = {}
    for d in OFFSETS:
        tangents(v1, tb, town, (a1 + d) % 4, d)
        rs1.update(reduce_first(tb, r1, d, rs_send, rs_recv))
    tangents(v1, tb, town, a1, 0)
    square = lax.dot_general(hid[...], hid[...], (((1,), (1,)), ((), ())), preferred_element_type=F32)
    corner = jnp.concatenate([square[128:ROWS, 128:ROWS], jnp.zeros((16, 112), F32)], axis=1)
    sq_own[...] = jnp.concatenate([square[:, 0:128], corner], axis=0)
    sq_out[...] = sq_own[...].astype(BF16)
    hid_t[...] = jnp.transpose(jnp.concatenate([hidden, jnp.zeros((112, 256), F32)], axis=0)).astype(BF16)
    for d in (1, 3):
        tangents(v0, tb0, town0, (a1 + d) % 4, d)

    rs2, mine_sum = reduce_second(rs1, town, r1, p2s, r2, rs_send, rs_recv)
    for copy in rs2:
        copy.wait_recv()
    mine_sum = ((mine_sum + r2[0].astype(F32)) + r2[1].astype(F32)) + r2[2].astype(F32)
    held[...] = mine_sum

    zs[...] = mine_sum.astype(BF16)
    zp = send(zs, rz0, z_send.at[0], z_recv.at[0], (y, x, z - sg, c))
    rs3 = {}
    for d in OFFSETS:
        if d == 2:
            tangents(v0, tb0, town0, (a1 + d) % 4, d)
        rs3.update(reduce_first(tb0, r10, d, rt_send, rt_recv))
    squares = [
        send(sq_out, sq_in.at[d - 1], sq_send.at[d - 1], sq_recv.at[d - 1], plane((a1 + d) % 4, a2))
        for d in OFFSETS
    ]
    zp.wait_recv()
    total = mine_sum + rz0[...].astype(F32)
    zes[...] = total.astype(BF16)
    zc = {
        k: send(zes, rz.at[k], z_send.at[1 + k], z_recv.at[1 + k], (y, x, (z + sg * (k + 1) + 8) % 8, c))
        for k in (2, 1, 0)
    }

    t_lane = iota((256, 128), 1)
    shift = jnp.where(t_lane == 1, sg, 0) + jnp.where(t_lane == 2, -sg, 0) + jnp.where(t_lane == 3, 2, 0)
    names = jnp.where(t_lane < 4, (e + shift + 4) & 3, -1)
    names = names.astype(F32)
    member4 = (cols[:, 0:1] == names).astype(F32) + (cols[:, 1:2] == names).astype(F32)
    low = iota((256, 256), 0)
    col = iota((256, 256), 1)
    tri_b = ((col <= low) & ((col >> 4) == (low >> 4))).astype(F32).astype(BF16)
    rank4 = jnp.dot(tri_b, member4.astype(BF16), preferred_element_type=F32)
    token = iota((256, 128), 0)
    block = token >> 4
    slot = rank4.astype(jnp.int32) - 1
    where_to = (block >> 3) * 72 + jnp.where(slot < 8, (block & 7) * 8 + slot, 64 + (block & 7))
    where_to = jnp.where(member4 > 0, where_to, -1000)
    onehot = (where_to[:, 0:1] == col).astype(F32)
    rank_s[...] = jnp.transpose(onehot)
    own_full = rank_s[0:ROWS, :].astype(BF16)
    own_half = rank_s[half_rows, :].astype(BF16)
    for k in range(3):
        theirs = (where_to[:, k + 1 : k + 2] == col).astype(F32).astype(BF16)
        amat[k] = jnp.dot(own_full, theirs, preferred_element_type=F32)[:, 0:ROWS].astype(BF16)
        theirs = (where_to[:, k + 1 : k + 2] - h * 72 == col).astype(F32).astype(BF16)
        amat_h[k] = jnp.dot(own_half, theirs, preferred_element_type=F32)[:, 0:72].astype(BF16)

    tangents(v0, tb0, town0, a1, 0)
    def gram(k, sums):
        s00, s01, s11 = sums
        part = pl.ds(pl.multiple_of(k * 256, 256), 256)
        for u in range(2):
            b0 = v0[u, :, part].astype(F32)
            b1 = v1[u, :, part].astype(F32)
            fold = lambda a: jnp.sum(a.reshape(16, 8, 256), axis=0)
            s00 = s00 + fold(b0 * b0)
            s01 = s01 + fold(b0 * b1)
            s11 = s11 + fold(b1 * b1)
        return s00, s01, s11

    zero = jnp.zeros((8, 256), F32)
    s00, s01, s11 = lax.fori_loop(0, HALF // 256, gram, (zero, zero, zero))

    resp_f, resp_h = total[0:ROWS], total[ROWS:CHUNK]
    for k in range(3):
        zc[k].wait_recv()
        resp_f = resp_f + jnp.dot(amat[k], rz[k, 0:ROWS, :], preferred_element_type=F32)
        resp_h = resp_h + jnp.dot(amat_h[k], rz[k, ROWS:CHUNK, :], preferred_element_type=F32)
    base = c * HALF + a1 * GROUP
    sig_f = sigma[:, pl.ds(pl.multiple_of(base + a2 * 128, 128), 128)]
    sig_h = sigma[:, pl.ds(pl.multiple_of(base + (4 + a2 // 2) * 128, 128), 128)]
    c4[m, 0:ROWS] = (rho_s[...] * sig_f * (resp_f * SCALE)).astype(BF16)
    c4[m, ROWS:CHUNK] = (rho_s[half_rows, :] * sig_h * (resp_h * SCALE)).astype(BF16)

    cg1 = along(c4, cg_send, cg_recv)
    cg2 = spread(c4, 0, cg_send, cg_recv)
    relay(cg1, cg2, c4, cg_send, cg_recv)

    def assemble(ref, g):
        for i in range(4):
            cg[:, i * 128 : (i + 1) * 128] = ref[g * 4 + i, 0:ROWS, :]
        for i in range(2):
            both = [ref[g * 4 + 2 * i + u, ROWS:CHUNK, :].astype(F32) for u in range(2)]
            cg[:, (4 + i) * 128 : (5 + i) * 128] = jnp.concatenate(both, axis=0).astype(BF16)

    for copy in list(rs3.values()) + squares:
        copy.wait_recv()
    line = lambda a: jnp.sum(a, axis=0, keepdims=True)
    dot0 = jnp.zeros((1, 128), F32)
    for i in range(4):
        partial = ((town0[i] + r10[0, i].astype(F32)) + r10[1, i].astype(F32)) + r10[2, i].astype(F32)
        dot0 = dot0 + line(c4[a1 * 4 + i].astype(F32) * partial)
    square = ((sq_own[...] + sq_in[0].astype(F32)) + sq_in[1].astype(F32)) + sq_in[2].astype(F32)
    sq_b = square.astype(BF16)
    assemble(c4, a1)
    mixed = jnp.dot(sq_b[0:ROWS], cg[0:128, :], preferred_element_type=F32)
    mixed_low = jnp.dot(sq_b[ROWS:160, 0:16], cg[128:ROWS, :], preferred_element_type=F32)
    quad = line(cg[0:128, :].astype(F32) * mixed[0:128])
    quad = quad + line(cg[128:ROWS, :].astype(F32) * (2.0 * mixed[128:ROWS] + mixed_low))
    quad = sum(quad[:, i * 128 : (i + 1) * 128] for i in range(6))
    lines = [
        dot0 * SCALE,
        line(c4[m].astype(F32) * held[...]) * SCALE,
        quad * (SCALE * SCALE),
    ] + [line(s[:, 0:128] + s[:, 128:256]) for s in (s00, s01, s11)]
    lines.append(jnp.zeros((2, 128), F32))
    red_s[0] = jnp.concatenate(lines, axis=0)
    ras = []
    for k in range(1, 16):
        o = (q + k) % 16
        ras.append(send(red_s.at[0], red_a.at[k - 1], ra_send.at[k - 1], ra_recv.at[k - 1], (y, x, o // 2, o % 2)))

    def rows_image(ref, u, g):
        assemble(ref, g)

        part = pl.ds(pl.multiple_of(g * GROUP, GROUP), GROUP)
        img[u, :, part] = jnp.dot(hid_t[0:128, 0:ROWS], cg[...], preferred_element_type=F32) * SCALE

    cxs = []
    rbs = []
    for n, d in enumerate((0,) + OFFSETS):
        if n == 2:
            acc = red_s[0]
            for k in range(15):
                ras[k].wait_recv()
                acc = acc + red_a[k]
            red_s[1] = acc
            for k in range(1, 16):
                o = (p + k) % 16
                rbs.append(
                    send(red_s.at[1], red_b.at[k - 1], rb_send.at[k - 1], rb_recv.at[k - 1], (o // 4, o % 4, z, c))
                )
        if d:
            landed(cg2, d)
        g = (a1 - d + 4) % 4
        block4 = pl.ds(pl.multiple_of(g * 4, 4), 4)
        cxs.append(send(c4.at[block4], cx.at[block4], cx_send.at[d], cx_recv.at[d], partner))
        rows_image(c4, 0, g)
        if n:
            cxs[n - 1].wait_recv()
            rows_image(cx, 1, (a2 - ((0,) + OFFSETS)[n - 1] + 4) % 4)

    cxs[3].wait_recv()
    rows_image(cx, 1, (a2 - 2 + 4) % 4)
    for k in range(15):
        rbs[k].wait_recv()
        acc = acc + red_b[k]
    scal = jnp.sum(acc, axis=1, keepdims=True) * (1.0 / ENTRIES)
    c0, c1, norm, g00, g01, g11 = [scal[k : k + 1, 0:1] for k in range(6)]
    norm = norm - 2.0 * (c0 * c0 + c1 * c1) + (c0 * c0 * g00 + 2.0 * (c0 * c1) * g01 + c1 * c1 * g11)
    beta = jnp.sqrt(norm)
    hess[...] = jnp.concatenate([c0, c1, beta], axis=1)
    inv = 1.0 / beta
    for u, (w0, w1, start) in enumerate(((v0.at[0], v1.at[0], c * HALF), (v0x, v1x, (1 - c) * HALF))):

        def finish(k, carry):
            part = pl.ds(pl.multiple_of(k * 256, 256), 256)
            resid = (img[u, :, part] - c0 * w0[:, part].astype(F32)) - c1 * w1[:, part].astype(F32)
            out[:, pl.ds(pl.multiple_of(start + k * 256, 256), 256)] = (resid * inv).astype(BF16)
            return carry

        lax.fori_loop(0, HALF // 256, finish, 0)

    for copy in first + core + list(second.values()) + [pre_copy] + list(rs1.values()) + rs2 + [zp] + list(zc.values()) + list(rs3.values()) + squares + cg1 + list(cg2.values()) + cxs + ras + rbs:
        copy.wait_send()


def body(tokens, w_gate, w_up, basis, routes, gates, rho, sigma):
    anywhere = pl.BlockSpec(memory_space=pl.ANY)
    vmem = pl.BlockSpec(memory_space=pltpu.VMEM)
    dma = pltpu.SemaphoreType.DMA
    scratch = [
        pltpu.VMEM((2, 256), jnp.int32),
        pltpu.VMEM((2, 256), F32),
        pltpu.VMEM((1, 16), F32),
        pltpu.VMEM((1, D), F32),
        pltpu.VMEM((256, 8), F32),
        pltpu.VMEM((16, HALF), BF16),
        pltpu.VMEM((2, HALF, 256), BF16),
        pltpu.VMEM((2, 128, HALF), BF16),
        pltpu.VMEM((2, 128, HALF), BF16),
        pltpu.VMEM((128, HALF), BF16),
        pltpu.VMEM((128, HALF), BF16),
        pltpu.VMEM((16, 8, MSG), BF16),
        pltpu.VMEM((ROWS, HALF), BF16),
        pltpu.VMEM((4, 128, 128), F32),
        pltpu.VMEM((8, 384), F32),
        pltpu.VMEM((ROWS, 128), F32),
        pltpu.VMEM((2, ROWS, 256), F32),
        pltpu.VMEM((2, ROWS, 256), F32),
        pltpu.VMEM((ROWS, 256), BF16),
        pltpu.VMEM((256, 256), BF16),
        pltpu.VMEM((3, 4, CHUNK, 128), BF16),
        pltpu.VMEM((3, 4, CHUNK, 128), BF16),
        pltpu.VMEM((4, CHUNK, 128), F32),
        pltpu.VMEM((3, CHUNK, 128), BF16),
        pltpu.VMEM((3, CHUNK, 128), BF16),
        pltpu.VMEM((3, 4, CHUNK, 128), BF16),
        pltpu.VMEM((3, 4, CHUNK, 128), BF16),
        pltpu.VMEM((4, CHUNK, 128), F32),
        pltpu.VMEM((CHUNK, 128), F32),
        pltpu.VMEM((160, 128), F32),
        pltpu.VMEM((160, 128), BF16),
        pltpu.VMEM((3, 160, 128), BF16),
        pltpu.VMEM((CHUNK, 128), BF16),
        pltpu.VMEM((CHUNK, 128), BF16),
        pltpu.VMEM((CHUNK, 128), BF16),
        pltpu.VMEM((3, CHUNK, 128), BF16),
        pltpu.VMEM((3, ROWS, ROWS), BF16),
        pltpu.VMEM((3, 72, 72), BF16),
        pltpu.VMEM((256, 256), F32),
        pltpu.VMEM((ROWS, 128), F32),
        pltpu.VMEM((16, CHUNK, 128), BF16),
        pltpu.VMEM((16, CHUNK, 128), BF16),
        pltpu.VMEM((ROWS, GROUP), BF16),
        pltpu.VMEM((2, 128, HALF), F32),
        pltpu.VMEM((15, 8, 128), F32),
        pltpu.VMEM((15, 8, 128), F32),
        pltpu.VMEM((2, 8, 128), F32),
        pltpu.SemaphoreType.REGULAR((2,)),
        dma((11,)),
        dma((5,)), dma((5,)),
        dma((5, 3)), dma((5, 3)),
        dma((5, 3)), dma((5, 3)),
        dma((4, 3)), dma((4, 3)),
        dma((3,)), dma((3,)),
        dma((4,)), dma((4,)),
        dma((5, 3)), dma((5, 3)),
        dma((4,)), dma((4,)),
        dma((15,)), dma((15,)),
        dma((15,)), dma((15,)),
    ]
    operands = (tokens, w_gate, w_up, basis, routes.T, gates.T, rho.reshape(1, 16), sigma.reshape(1, D))
    operands = [pltpu.with_memory_space_constraint(a, pltpu.HBM) for a in operands]
    out, hess = pl.pallas_call(
        kernel,
        out_shape=(jax.ShapeDtypeStruct((128, D), BF16), jax.ShapeDtypeStruct((1, 3), F32)),
        in_specs=[anywhere] * 8,
        out_specs=(vmem, vmem),
        scratch_shapes=scratch,
        compiler_params=pltpu.CompilerParams(
            collective_id=0, has_side_effects=True, vmem_limit_bytes=32 * 1024 * 1024
        ),
        name="arnoldi",
    )(*operands)
    return out, hess.T


def solution(mesh):
    finer = Mesh(mesh.devices.reshape(4, 4, 8, 2), AXES)
    in_specs = (
        P(DP, None),
        P(None, EXPERT_DP),
        P(None, EXPERT_DP),
        P(None, EXPERT_DP, None),
        P(),
        P(),
        P(DP),
        P(),
    )
    out_specs = (P(EXPERT_DP, None), P())
    return jax.shard_map(body, mesh=finer, in_specs=in_specs, out_specs=out_specs, check_vma=False)
```
